32 devices in a mesh: outer: 8 (over z, core), inner: 4 (over y, x).
Axes of the slice: x: 2, y: 2, z: 4, core: 2. Of those that a mesh axis runs over, the one named last changes fastest.
Arguments:
- queries: bfloat16 [2048, 4096], P(('outer', 'inner')), may hold values from -6 to 6
- keys: bfloat16 [2048, 4096], P(('outer', 'inner')), may hold values from -6 to 6
- values: bfloat16 [2048, 4096], P(('outer', 'inner')), may hold values from -6 to 6
- lengths: int32 [16], replicated, may hold values from 1 to 32, 128 in all
- norm_gain: float32 [4096], replicated, may hold values from 0.5 to 1.5
Outputs:
- attended: bfloat16 [2048, 4096], P(('outer', 'inner'))
The draws below stay inside these ranges and needn't reach their ends.
Inputs may be any that keep to these rules, and one draw needn't show every extreme that they name: The lengths sum to 128; one document is exactly 32 units long.
All inputs are finite; a program needn't handle non-finite values.
Results may differ from the reference program's by a relative error of at most 0.0049.
Values sent between devices are 32-bit elements; how exact they have to be, the bound alone decides.
No kernel may reach another device: no remote copies, remote signals or barrier semaphores. Data moves between devices by JAX's collectives and lax.ppermute only.
A program may use at most 64 MiB of HBM per device.

```python
import math
import jax
import jax.numpy as jnp
import numpy as np
from jax import lax

HEADS = 32
HEAD_DIM = 128
TOK_DEV = 64
BLOCK = 16
DOCS = 16
TOKENS = 2048
MOST = 32


def steps_of(key, extent, pieces, least, high):
    gain, own = 1.0, jax.random.fold_in(key, 6)
    for axis_at, blocks in pieces:
        heights = jnp.exp(jax.random.uniform(jax.random.fold_in(own, axis_at), (blocks,), jnp.float32, least / len(pieces), high / len(pieces)))
        gain = gain * jnp.repeat(heights, extent[axis_at] // blocks).reshape([-1 if axis == axis_at else 1 for axis in range(len(extent))])
    return gain


def length_profile(amount, total, bound, slope):
    weights = [(1 << 20) // math.isqrt(standing ** slope) + 1 for standing in range(2, amount + 1)]
    spare, given = total - bound - (amount - 1), [1] * (amount - 1)
    while spare > 0:
        movable = [i for i in range(amount - 1) if given[i] < bound]
        pool, left = sum([weights[i] for i in movable]), spare
        for i in movable:
            extra = min(bound - given[i], max(1, left * weights[i] // pool), spare)
            given[i] = given[i] + extra
            spare = spare - extra
    return np.array([bound] + given)


def uneven(stream_key, count, total, bound, skew):
    if count == 2:
        one = jax.random.randint(stream_key, (), max(1, total - bound), min(bound, total - 1) + 1)
        return jnp.stack([one, total - one])
    tallies = jnp.asarray(length_profile(count, total, bound, skew), jnp.int32)
    pairs = (count - 1) // 2
    source_of, taker = tallies[1:1 + 2 * pairs:2], tallies[2:2 + 2 * pairs:2]
    margin = jnp.minimum(source_of - 1, bound - taker)
    shifted = jax.random.randint(jax.random.fold_in(stream_key, 1), (pairs,), 0, 1 << 20) % (margin + 1)
    tallies = tallies.at[1:1 + 2 * pairs:2].set(source_of - shifted).at[2:2 + 2 * pairs:2].set(taker + shifted)
    return tallies[jax.random.permutation(jax.random.fold_in(stream_key, 2), count)]


def noise(stream_key, extent, scale, reach, pieces=(), kind=jnp.bfloat16):
    array = scale * jax.random.normal(stream_key, extent, jnp.float32)
    if pieces:
        array = array * steps_of(stream_key, extent, pieces, -0.22, 0.18)
    return jnp.clip(array, -reach, reach).astype(kind)


def setup_inputs(seed: int = 0) -> dict:
    streams_of = jax.random.split(jax.random.key(seed), 6)
    queries = noise(streams_of[0], (TOKENS, HEADS * HEAD_DIM), 1.0, 6.0, ((0, 32),))
    keys = noise(streams_of[1], (TOKENS, HEADS * HEAD_DIM), 1.0, 6.0, ((0, 32),))
    values = noise(streams_of[2], (TOKENS, HEADS * HEAD_DIM), 1.0, 6.0, ((0, 32),))
    lengths = uneven(streams_of[3], DOCS, TOKENS // BLOCK, MOST, 1).astype(jnp.int32)
    norm_gain = jnp.clip(1.0 + 0.1 * jax.random.normal(streams_of[4], (HEADS * HEAD_DIM,), jnp.float32), 0.5, 1.5)
    return {"queries": queries, "keys": keys, "values": values, "lengths": lengths, "norm_gain": norm_gain}


EPSILON = 1e-05

def doc_ids(tok_rows, doc_starts):
    return (lax.optimization_barrier(jnp.sum((tok_rows[:, None] >= doc_starts[None, :]).astype(jnp.int32), axis=1)) - 1).astype(jnp.int32)

def reference(queries, keys, values, lengths, norm_gain):
    block_count = TOKENS // TOK_DEV
    shape = (block_count, TOK_DEV, HEADS, HEAD_DIM)
    query_blocks = queries.reshape(shape)
    key_blocks = keys.reshape(shape)
    value_blocks = values.reshape(shape)
    doc_starts = (BLOCK * (jnp.cumsum(lengths) - lengths)).astype(jnp.int32)
    gain_heads = norm_gain.reshape(HEADS, HEAD_DIM)
    offsets = jnp.arange(TOK_DEV, dtype=jnp.int32)

    def advance(carried, inputs):
        state, prior_doc = carried
        query_blk, key_blk, value_blk, index = inputs
        tok_rows = (index * TOK_DEV + offsets).astype(jnp.int32)
        docs = doc_ids(tok_rows, doc_starts)
        first_doc = docs[0]
        final_doc = docs[-1]
        carry_in = jnp.where(first_doc == prior_doc, state, jnp.zeros_like(state))
        query_f = query_blk.astype(jnp.float32)
        key_f = key_blk.astype(jnp.float32)
        value_f = value_blk.astype(jnp.float32)
        scores = jnp.einsum('thd,shd->hts', query_f, key_f)
        allowed = (tok_rows[:, None] >= tok_rows[None, :]) & (docs[:, None] == docs[None, :])
        weights = jnp.where(allowed[None], scores, 0.0).astype(jnp.bfloat16)
        weights = lax.optimization_barrier(weights).astype(jnp.float32)
        intra = jnp.einsum('hts,she->the', weights, value_f)
        held = lax.optimization_barrier(carry_in.astype(jnp.bfloat16)).astype(jnp.float32)
        inter = jnp.einsum('thd,hde->the', query_f, held)
        inter = jnp.where((docs == first_doc)[:, None, None], inter, 0.0)
        mixed = intra + inter
        scale = lax.rsqrt(lax.optimization_barrier(jnp.mean(mixed * mixed, axis=-1, keepdims=True)) + EPSILON)
        attended = (mixed * scale * gain_heads[None]).astype(jnp.bfloat16)
        final_keys = jnp.where((docs == final_doc)[:, None, None], key_f, 0.0)
        local_state = jnp.einsum('thd,the->hde', final_keys, value_f)
        new_state = local_state + jnp.where(first_doc == final_doc, carry_in, jnp.zeros_like(carry_in))
        return ((new_state, final_doc), attended)
    start_state = jnp.zeros((HEADS, HEAD_DIM, HEAD_DIM), jnp.float32)
    indices = jnp.arange(block_count, dtype=jnp.int32)
    carried, outputs = lax.scan(advance, (start_state, jnp.int32(-1)), (query_blocks, key_blocks, value_blocks, indices))
    return outputs.reshape(TOKENS, HEADS * HEAD_DIM)
```

```python
import functools

import jax
import jax.numpy as jnp
from jax import lax
from jax.experimental import pallas as pl
from jax.experimental.pallas import tpu as pltpu
from jax.sharding import PartitionSpec as P

HEAD_DIM = 128
BLOCK = 16
CORES = 2
SHARE = 4
EPSILON = 1e-05


def spread(members, width, place, *refs):
    count = len(refs) - members
    sources, outs = refs[:count], refs[count:]
    me = place[0]
    for d in range(members):
        column = pl.multiple_of((me ^ d) * width, width)
        for i, source in enumerate(sources):
            part = source[:, pl.ds(column, width)].astype(jnp.float32)
            if count == 1:
                outs[d][...] = part
            else:
                outs[d][i] = part


def doc_table(lengths, starts, docs):
    total = jnp.int32(0)
    for i in range(docs):
        starts[i] = total
        total = total + lengths[i] * BLOCK


def start_of(starts, docs, token):
    found = jnp.int32(0)
    for i in range(docs):
        found = jnp.where(starts[i] <= token, starts[i], found)
    return found


def gather_states(members, heads, docs, rows, place, lengths, *refs):
    parts = refs[:members]
    key_out, value_out, carry_out, total_out, starts, first_of = refs[members:]
    me, base = place[0], place[1]
    doc_table(lengths, starts, docs)
    for j in range(members + 1):
        first_of[j] = start_of(starts, docs, base + j * rows)
    for d in range(members):
        j = me ^ d
        key_out[j] = parts[d][0].astype(jnp.bfloat16)
        value_out[j] = parts[d][1].astype(jnp.bfloat16)
    row = lax.broadcasted_iota(jnp.int32, (rows, heads * HEAD_DIM), 0)
    state = [jnp.zeros((HEAD_DIM, HEAD_DIM), jnp.float32) for _ in range(heads)]
    for j in range(members):
        begin = base + j * rows
        since = first_of[j + 1]
        keys = key_out[j].astype(jnp.float32)
        keys = jnp.where(row + begin >= since, keys, 0.0).astype(jnp.bfloat16)
        values = value_out[j]
        keep = jnp.where(since <= begin, 1.0, 0.0).astype(jnp.float32)
        for h in range(heads):
            span = slice(h * HEAD_DIM, (h + 1) * HEAD_DIM)
            carry_out[j, h] = state[h]
            own = lax.dot_general(
                keys[:, span], values[:, span], (((0,), (0,)), ((), ())), preferred_element_type=jnp.float32
            )
            state[h] = keep * state[h] + own
    for h in range(heads):
        total_out[h] = state[h]


def attend(members, heads, docs, rows, place, lengths, *refs):
    query_parts = refs[:members]
    keys, values, carry, earlier, gain = refs[members : members + 5]
    outs = refs[members + 5 : 2 * members + 5]
    starts = refs[2 * members + 5]
    me, base = place[0], place[1]
    doc_table(lengths, starts, docs)
    row = lax.broadcasted_iota(jnp.int32, (rows, HEAD_DIM), 0)
    lane = lax.broadcasted_iota(jnp.int32, (rows, rows), 1)
    for d in range(members):
        j = me ^ d
        begin = base + j * rows
        token = row + begin
        since = jnp.zeros((rows, HEAD_DIM), jnp.int32)
        for i in range(docs):
            since = jnp.where(starts[i] <= token, starts[i], since)
        local = since - begin
        continued = local <= 0
        allowed = (lane <= row[:, :rows]) & (lane >= local[:, :rows])
        from_earlier = jnp.where(start_of(starts, docs, begin) < base, 1.0, 0.0).astype(jnp.float32)
        for h in range(heads):
            span = slice(h * HEAD_DIM, (h + 1) * HEAD_DIM)
            query = query_parts[d][:, span].astype(jnp.bfloat16)
            scores = lax.dot_general(
                query, keys[j, :, span], (((1,), (1,)), ((), ())), preferred_element_type=jnp.float32
            )
            weights = jnp.where(allowed, scores, 0.0).astype(jnp.bfloat16)
            mixed = jnp.dot(weights, values[j, :, span], preferred_element_type=jnp.float32)
            held = (carry[j, h] + from_earlier * earlier[h]).astype(jnp.bfloat16)
            inter = jnp.dot(query, held, preferred_element_type=jnp.float32)
            mixed = mixed + jnp.where(continued, inter, 0.0)
            scale = lax.rsqrt(jnp.mean(mixed * mixed, axis=-1, keepdims=True) + EPSILON)
            outs[d][:, span] = mixed * scale * gain[:, pl.ds(pl.multiple_of(me * heads * HEAD_DIM, HEAD_DIM) + h * HEAD_DIM, HEAD_DIM)]


def place_rows(members, width, place, *refs):
    out = refs[members]
    me = place[0]
    for d in range(members):
        column = pl.multiple_of((me ^ d) * width, width)
        out[:, pl.ds(column, width)] = refs[d][...].astype(jnp.bfloat16)


def body(queries, keys, values, lengths, norm_gain):
    rows, columns = queries.shape
    head_count = columns // HEAD_DIM
    docs = lengths.shape[0]
    inner_count = lax.axis_size("inner")
    devices = lax.axis_size("outer") * inner_count
    members = CORES * inner_count
    planes = devices // members
    heads = head_count // members
    width = heads * HEAD_DIM
    reach = -(-(devices // SHARE) // members)
    everyone = ("outer", "inner")
    index = lax.axis_index("outer") * inner_count + lax.axis_index("inner")
    me = index % members
    base = (index - me) * rows
    place = jnp.stack([me, base]).astype(jnp.int32)
    smem = pl.BlockSpec(memory_space=pltpu.SMEM)
    vmem = pl.BlockSpec(memory_space=pltpu.VMEM)
    params = pltpu.CompilerParams(vmem_limit_bytes=48 * 1024 * 1024)
    f32 = jnp.float32

    def exchange(parts):
        got = [parts[0]]
        for d in range(1, members):
            pairs = [(g, g - g % members + (g % members ^ d)) for g in range(devices)]
            got.append(lax.ppermute(parts[d], everyone, pairs))
        return got

    pair_parts = pl.pallas_call(
        functools.partial(spread, members, width),
        out_shape=[jax.ShapeDtypeStruct((2, rows, width), f32)] * members,
        in_specs=[smem, vmem, vmem],
        out_specs=[vmem] * members,
        compiler_params=params,
        name="spread_kv",
    )(place, keys, values)
    pair_got = exchange(pair_parts)
    query_parts = pl.pallas_call(
        functools.partial(spread, members, width),
        out_shape=[jax.ShapeDtypeStruct((rows, width), f32)] * members,
        in_specs=[smem, vmem],
        out_specs=[vmem] * members,
        compiler_params=params,
        name="spread_q",
    )(place, queries)
    query_got = exchange(query_parts)
    key_blocks, value_blocks, carry, total = pl.pallas_call(
        functools.partial(gather_states, members, heads, docs, rows),
        out_shape=[
            jax.ShapeDtypeStruct((members, rows, width), jnp.bfloat16),
            jax.ShapeDtypeStruct((members, rows, width), jnp.bfloat16),
            jax.ShapeDtypeStruct((members, heads, HEAD_DIM, HEAD_DIM), f32),
            jax.ShapeDtypeStruct((heads, HEAD_DIM, HEAD_DIM), f32),
        ],
        in_specs=[smem, smem] + [vmem] * members,
        out_specs=[vmem] * 4,
        scratch_shapes=[pltpu.SMEM((docs,), jnp.int32), pltpu.SMEM((members + 1,), jnp.int32)],
        compiler_params=params,
        name="gather_states",
    )(place, lengths, *pair_got)
    up = [(g, g + members) for g in range(devices - members)]
    moving = lax.ppermute(total, everyone, up)
    earlier = moving
    if reach > 1:
        starts = BLOCK * (jnp.cumsum(lengths) - lengths)
        opens = jnp.max(jnp.where(starts <= base, starts, 0))
        for k in range(2, min(reach, planes - 1) + 1):
            moving = lax.ppermute(moving, everyone, up)
            earlier = earlier + jnp.where(opens < base - (k - 1) * members * rows, moving, 0.0)
    mixed_parts = pl.pallas_call(
        functools.partial(attend, members, heads, docs, rows),
        out_shape=[jax.ShapeDtypeStruct((rows, width), f32)] * members,
        in_specs=[smem, smem] + [vmem] * (members + 5),
        out_specs=[vmem] * members,
        scratch_shapes=[pltpu.SMEM((docs,), jnp.int32)],
        compiler_params=params,
        name="attend",
    )(place, lengths, *query_got, key_blocks, value_blocks, carry, earlier, norm_gain.reshape(1, columns))
    mixed_got = exchange(mixed_parts)
    return pl.pallas_call(
        functools.partial(place_rows, members, width),
        out_shape=jax.ShapeDtypeStruct((rows, columns), jnp.bfloat16),
        in_specs=[smem] + [vmem] * members,
        out_specs=vmem,
        compiler_params=params,
        name="place_rows",
    )(place, *mixed_got)


def solution(mesh):
    placed = (
        P(("outer", "inner"), None),
        P(("outer", "inner"), None),
        P(("outer", "inner"), None),
        P(),
        P(),
    )
    return jax.shard_map(
        body, mesh=mesh, in_specs=placed, out_specs=P(("outer", "inner"), None), check_vma=False
    )
```

```python
import functools

import jax
import jax.numpy as jnp
from jax import lax
from jax.experimental import pallas as pl
from jax.experimental.pallas import tpu as pltpu
from jax.sharding import PartitionSpec as P

HEAD_DIM = 128
BLOCK = 16
CORES = 2
SHARE = 4
EPSILON = 1e-05
SMEM = pl.BlockSpec(memory_space=pltpu.SMEM)
VMEM = pl.BlockSpec(memory_space=pltpu.VMEM)
ANY = pl.BlockSpec(memory_space=pl.ANY)


def columns_of(member, width):
    return pl.ds(pl.multiple_of(member * width, width), width)


def heads_of(heads):
    return [slice(h * HEAD_DIM, (h + 1) * HEAD_DIM) for h in range(heads)]


def start_of(lengths, docs, token):
    begin = jnp.int32(0)
    found = jnp.int32(0)
    after = jnp.int32(jnp.iinfo(jnp.int32).max)
    for i in range(docs):
        found = jnp.where(begin <= token, begin, found)
        after = jnp.where(begin > token, jnp.minimum(begin, after), after)
        begin = begin + lengths[i] * BLOCK
    return found, after


def spread_pairs(members, width, place, keys, values, *refs):
    outs = refs[:members]
    key_buffer, value_buffer, sems = refs[members:]
    me = place[0]

    def copies(d):
        span = columns_of(me ^ d, width)
        return [
            pltpu.make_async_copy(keys.at[:, span], key_buffer.at[d], sems.at[0, d]),
            pltpu.make_async_copy(values.at[:, span], value_buffer.at[d], sems.at[1, d]),
        ]

    order = list(reversed(range(members)))
    for d in order:
        for copy in copies(d):
            copy.start()
    for d in order:
        for copy in copies(d):
            copy.wait()
        outs[d][0] = key_buffer[d].astype(jnp.float32)
        outs[d][1] = value_buffer[d].astype(jnp.float32)


def pick_other(members, width, place, queries, out):
    half = members // CORES
    side = 1 - place[0] // half
    out[...] = queries[:, columns_of(side, half * width)].astype(jnp.float32)


def spread_queries(members, width, gates, place, queries, swapped, *refs):
    half = members // CORES
    outs = refs[gates:]
    me = place[0]
    for e in range(half):
        outs[e][0] = queries[:, columns_of(me ^ e, width)].astype(jnp.float32)
        outs[e][1] = swapped[:, columns_of((me ^ e) % half, width)]


def gather_states(members, heads, docs, rows, place, lengths, *refs):
    parts = refs[:members]
    carry_out, total_out, key_blocks, value_blocks = refs[members + 1 :]
    me, base = place[0], place[1]
    row = lax.broadcasted_iota(jnp.int32, (rows, heads * HEAD_DIM), 0)
    for d in range(members):
        j = me ^ d
        since, _ = start_of(lengths, docs, base + (j + 1) * rows)
        key_blocks[j] = jnp.where(row >= since - base - j * rows, parts[d][0], 0.0).astype(jnp.bfloat16)
        value_blocks[j] = parts[d][1].astype(jnp.bfloat16)
    state = [jnp.zeros((HEAD_DIM, HEAD_DIM), jnp.float32) for _ in range(heads)]
    for j in range(members):
        since, _ = start_of(lengths, docs, base + (j + 1) * rows)
        keep = jnp.where(since <= base + j * rows, 1.0, 0.0).astype(jnp.float32)
        for h, span in enumerate(heads_of(heads)):
            carry_out[j, h] = state[h]
            own = lax.dot_general(
                key_blocks[j, :, span],
                value_blocks[j, :, span],
                (((0,), (0,)), ((), ())),
                preferred_element_type=jnp.float32,
            )
            state[h] = keep * state[h] + own
    for h in range(heads):
        total_out[h] = state[h]


def inside(head_count, docs, rows, place, lengths, queries, keys, values, out):
    begin = place[2]
    row = lax.broadcasted_iota(jnp.int32, (rows, rows), 0)
    lane = lax.broadcasted_iota(jnp.int32, (rows, rows), 1)
    since = jnp.zeros((rows, rows), jnp.int32)
    start = -begin
    for i in range(docs):
        since = jnp.where(start <= row, start, since)
        start = start + lengths[i] * BLOCK
    allowed = (lane <= row) & (lane >= since)
    for span in heads_of(head_count):
        scores = lax.dot_general(
            queries[:, span], keys[:, span], (((1,), (1,)), ((), ())), preferred_element_type=jnp.float32
        )
        weights = jnp.where(allowed, scores, 0.0).astype(jnp.bfloat16)
        out[:, span] = jnp.dot(weights, values[:, span], preferred_element_type=jnp.float32)


def reach_back(members, heads, docs, rows, place, lengths, *refs):
    half = members // CORES
    query_parts = refs[:half]
    carry, earlier = refs[half : half + 2]
    outs = refs[half + 2 :]
    me, base = place[0], place[1]
    for e in range(half):
        for side in range(CORES):
            d = e ^ (side * half)
            j = me ^ d
            first, _ = start_of(lengths, docs, base + j * rows)
            before = jnp.where(first < base, 1.0, 0.0).astype(jnp.float32)
            for h, span in enumerate(heads_of(heads)):
                held = (carry[j, h] + before * earlier[h]).astype(jnp.bfloat16)
                query = query_parts[e][side, :, span].astype(jnp.bfloat16)
                outs[d][:, span] = jnp.dot(query, held, preferred_element_type=jnp.float32)


def finish(chosen, heads, docs, rows, place, lengths, own, gain, *refs):
    count = len(chosen)
    parts, out = refs[:count], refs[-3]
    buffer, sems = refs[-2:]
    width = heads * HEAD_DIM
    me, begin = place[0], place[2]
    row = lax.broadcasted_iota(jnp.int32, (rows, HEAD_DIM), 0)
    _, after = start_of(lengths, docs, begin)
    continued = row < after - begin
    copies = []
    for i, d in enumerate(chosen):
        columns = columns_of(me ^ d, width)
        inner = own[:, columns]
        scales = gain[:, columns]
        for span in heads_of(heads):
            mixed = inner[:, span] + jnp.where(continued, parts[i][:, span], 0.0)
            scale = lax.rsqrt(jnp.mean(mixed * mixed, axis=-1, keepdims=True) + EPSILON)
            buffer[i, :, span] = (mixed * scale * scales[:, span]).astype(jnp.bfloat16)
        copy = pltpu.make_async_copy(buffer.at[i], out.at[:, columns], sems.at[i])
        copy.start()
        copies.append(copy)
    for copy in copies:
        copy.wait()


def body(queries, keys, values, lengths, norm_gain):
    rows, columns = queries.shape
    head_count = columns // HEAD_DIM
    docs = lengths.shape[0]
    inner_count = lax.axis_size("inner")
    devices = lax.axis_size("outer") * inner_count
    members = CORES * inner_count
    half = inner_count
    planes = devices // members
    heads = head_count // members
    width = heads * HEAD_DIM
    reach = -(-(devices // SHARE) // members)
    everyone = ("outer", "inner")
    index = lax.axis_index("outer") * inner_count + lax.axis_index("inner")
    me = index % members
    base = (index - me) * rows
    place = jnp.stack([me, base, index * rows]).astype(jnp.int32)
    f32, bf16 = jnp.float32, jnp.bfloat16
    params = pltpu.CompilerParams(vmem_limit_bytes=48 * 1024 * 1024)

    def call(kernel, name, out_shape, in_specs, out_specs, scratch=(), flops=0, moved=0, aliases=None):
        return pl.pallas_call(
            kernel,
            out_shape=out_shape,
            in_specs=in_specs,
            out_specs=out_specs,
            scratch_shapes=scratch,
            compiler_params=params,
            cost_estimate=pl.CostEstimate(flops=flops, bytes_accessed=moved, transcendentals=0),
            input_output_aliases=aliases or {},
            name=name,
        )

    def shape(*sizes, dtype=f32):
        return jax.ShapeDtypeStruct(sizes, dtype)

    def swap(part, d):
        pairs = [(g, g - g % members + (g % members ^ d)) for g in range(devices)]
        return lax.ppermute(part, everyone, pairs)

    block_bytes = rows * columns * 4
    pair_parts = call(
        functools.partial(spread_pairs, members, width),
        "spread_pairs",
        [shape(2, rows, width)] * members,
        [SMEM, ANY, ANY],
        [VMEM] * members,
        [
            pltpu.VMEM((members, rows, width), bf16),
            pltpu.VMEM((members, rows, width), bf16),
            pltpu.SemaphoreType.DMA((2, members)),
        ],
        moved=3 * block_bytes,
    )(place, keys, values)
    pair_got = [pair_parts[0]] + [swap(pair_parts[d], d) for d in range(1, members)]

    other = call(
        functools.partial(pick_other, members, width),
        "pick_other",
        shape(rows, half * width),
        [SMEM, VMEM],
        VMEM,
        moved=block_bytes,
    )(place, queries)
    swapped = swap(other, half)
    gates = pair_got[half:]
    query_parts = call(
        functools.partial(spread_queries, members, width, len(gates)),
        "spread_queries",
        [shape(CORES, rows, width)] * half,
        [SMEM, VMEM, VMEM] + [ANY] * len(gates),
        [VMEM] * half,
        moved=2 * block_bytes,
    )(place, queries, swapped, *gates)
    query_got = [query_parts[0]] + [swap(query_parts[e], e) for e in range(1, half)]

    own = call(
        functools.partial(inside, head_count, docs, rows),
        "inside",
        shape(rows, columns),
        [SMEM, SMEM, VMEM, VMEM, VMEM],
        VMEM,
        flops=4 * rows * rows * columns,
        moved=3 * block_bytes,
    )(place, lengths, queries, keys, values)

    carry, total = call(
        functools.partial(gather_states, members, heads, docs, rows),
        "gather_states",
        [shape(members, heads, HEAD_DIM, HEAD_DIM), shape(heads, HEAD_DIM, HEAD_DIM)],
        [SMEM, SMEM] + [VMEM] * members + [ANY],
        [VMEM] * 2,
        [pltpu.VMEM((members, rows, width), bf16)] * 2,
        flops=2 * rows * HEAD_DIM * columns,
        moved=4 * block_bytes,
    )(place, lengths, *pair_got, query_parts[0])
    up = [(g, g + members) for g in range(devices - members)]
    moving = lax.ppermute(total, everyone, up)
    earlier = moving
    if reach > 1:
        starts = BLOCK * (jnp.cumsum(lengths) - lengths)
        opens = jnp.max(jnp.where(starts <= base, starts, 0))
        for k in range(2, min(reach, planes - 1) + 1):
            moving = lax.ppermute(moving, everyone, up)
            earlier = earlier + jnp.where(opens < base - (k - 1) * members * rows, moving, 0.0)
    crossed = call(
        functools.partial(reach_back, members, heads, docs, rows),
        "reach_back",
        [shape(rows, width)] * members,
        [SMEM, SMEM] + [VMEM] * (half + 2),
        [VMEM] * members,
        flops=2 * rows * HEAD_DIM * columns,
        moved=4 * block_bytes,
    )(place, lengths, *query_got, carry, earlier)
    crossed_got = [crossed[0]] + [swap(crossed[d], d) for d in range(1, members)]

    gain = norm_gain.reshape(1, columns)
    first = [0] + list(range(half, members))
    last = list(range(1, half))
    out = None
    for chosen in (first, last):
        more = [] if out is None else [out]
        out = call(
            functools.partial(finish, chosen, heads, docs, rows),
            "finish",
            shape(rows, columns, dtype=bf16),
            [SMEM, SMEM, VMEM, VMEM] + [VMEM] * len(chosen) + [ANY] * len(more),
            ANY,
            [pltpu.VMEM((len(chosen), rows, width), bf16), pltpu.SemaphoreType.DMA((len(chosen),))],
            moved=2 * block_bytes,
            aliases={4 + len(chosen): 0} if more else None,
        )(place, lengths, own, gain, *[crossed_got[d] for d in chosen], *more)
    return out


def solution(mesh):
    placed = (
        P(("outer", "inner"), None),
        P(("outer", "inner"), None),
        P(("outer", "inner"), None),
        P(),
        P(),
    )
    return jax.shard_map(
        body, mesh=mesh, in_specs=placed, out_specs=P(("outer", "inner"), None), check_vma=False
    )
```

```python
import functools

import jax
import jax.numpy as jnp
from jax import lax
from jax.experimental import pallas as pl
from jax.experimental.pallas import tpu as pltpu
from jax.sharding import PartitionSpec as P

HEAD_DIM = 128
BLOCK = 16
CORES = 2
SHARE = 4
EPSILON = 1e-05
SMEM = pl.BlockSpec(memory_space=pltpu.SMEM)
VMEM = pl.BlockSpec(memory_space=pltpu.VMEM)
ANY = pl.BlockSpec(memory_space=pl.ANY)
HBM = pl.BlockSpec(memory_space=pltpu.HBM)


def columns_of(member, width):
    return pl.ds(pl.multiple_of(member * width, width), width)


def heads_of(heads):
    return [slice(h * HEAD_DIM, (h + 1) * HEAD_DIM) for h in range(heads)]


def start_of(lengths, docs, token):
    begin = jnp.int32(0)
    found = jnp.int32(0)
    after = jnp.int32(jnp.iinfo(jnp.int32).max)
    for i in range(docs):
        found = jnp.where(begin <= token, begin, found)
        after = jnp.where(begin > token, jnp.minimum(begin, after), after)
        begin = begin + lengths[i] * BLOCK
    return found, after


def spread(members, width, place, queries, keys, values, *refs):
    half = members // CORES
    near, cross = refs[:half], refs[half]
    buffers, sems = refs[half + 1 : half + 4], refs[half + 4]
    me = place[0]

    def copies(d):
        span = columns_of(me ^ d, width)
        sources = (keys, values) if d < half else (keys, values, queries)
        return [
            pltpu.make_async_copy(source.at[:, span], buffers[i].at[d], sems.at[i, d])
            for i, source in enumerate(sources)
        ]

    for d in range(members):
        for copy in copies(d):
            copy.start()
    for d in range(members):
        for i, copy in enumerate(copies(d)):
            copy.wait()
            part = buffers[i][d].astype(jnp.float32)
            if d < half:
                near[d][i] = part
            else:
                cross[d - half, i] = part


def forward(half, swapped, *outs):
    for e in range(1, half):
        outs[e - 1][...] = swapped[e, 0:2]


def join_queries(half, width, gates, place, queries, swapped, *refs):
    outs = refs[gates:]
    me = place[0]
    for e in range(half):
        outs[e][0] = queries[:, columns_of(me ^ e, width)].astype(jnp.float32)
        outs[e][1] = swapped[e, 2]


def gather_states(members, heads, docs, rows, place, lengths, *refs):
    half = members // CORES
    parts = refs[:members]
    carry_out, total_out, key_blocks, value_blocks = refs[members + 1 :]
    me, base = place[0], place[1]
    row = lax.broadcasted_iota(jnp.int32, (rows, heads * HEAD_DIM), 0)
    for d in range(members):
        j = me ^ d
        since, _ = start_of(lengths, docs, base + (j + 1) * rows)
        key, value = (parts[d][0, 0], parts[d][0, 1]) if d == half else (parts[d][0], parts[d][1])
        key_blocks[j] = jnp.where(row >= since - base - j * rows, key, 0.0).astype(jnp.bfloat16)
        value_blocks[j] = value.astype(jnp.bfloat16)
    state = [jnp.zeros((HEAD_DIM, HEAD_DIM), jnp.float32) for _ in range(heads)]
    for j in range(members):
        since, _ = start_of(lengths, docs, base + (j + 1) * rows)
        keep = jnp.where(since <= base + j * rows, 1.0, 0.0).astype(jnp.float32)
        for h, span in enumerate(heads_of(heads)):
            carry_out[j, h] = state[h]
            own = lax.dot_general(
                key_blocks[j, :, span],
                value_blocks[j, :, span],
                (((0,), (0,)), ((), ())),
                preferred_element_type=jnp.float32,
            )
            state[h] = keep * state[h] + own
    for h in range(heads):
        total_out[h] = state[h]


def inside(head_count, docs, rows, place, lengths, queries, keys, values, out):
    begin = place[2]
    row = lax.broadcasted_iota(jnp.int32, (rows, rows), 0)
    lane = lax.broadcasted_iota(jnp.int32, (rows, rows), 1)
    since = jnp.zeros((rows, rows), jnp.int32)
    start = -begin
    for i in range(docs):
        since = jnp.where(start <= row, start, since)
        start = start + lengths[i] * BLOCK
    allowed = (lane <= row) & (lane >= since)
    for span in heads_of(head_count):
        scores = lax.dot_general(
            queries[:, span], keys[:, span], (((1,), (1,)), ((), ())), preferred_element_type=jnp.float32
        )
        weights = jnp.where(allowed, scores, 0.0).astype(jnp.bfloat16)
        out[:, span] = jnp.dot(weights, values[:, span], preferred_element_type=jnp.float32)


def reach_back(members, heads, docs, rows, place, lengths, *refs):
    half = members // CORES
    query_parts = refs[:half]
    carry, earlier = refs[half : half + 2]
    outs = refs[half + 3 :]
    me, base = place[0], place[1]
    for e in range(half):
        for side in range(CORES):
            d = e ^ (side * half)
            j = me ^ d
            first, _ = start_of(lengths, docs, base + j * rows)
            before = jnp.where(first < base, 1.0, 0.0).astype(jnp.float32)
            for h, span in enumerate(heads_of(heads)):
                held = (carry[j, h] + before * earlier[h]).astype(jnp.bfloat16)
                query = query_parts[e][side, :, span].astype(jnp.bfloat16)
                outs[d][:, span] = jnp.dot(query, held, preferred_element_type=jnp.float32)


def finish(chosen, heads, docs, rows, place, lengths, own, gain, *refs):
    count = len(chosen)
    parts, out = refs[:count], refs[-3]
    buffer, sems = refs[-2:]
    width = heads * HEAD_DIM
    me, begin = place[0], place[2]
    row = lax.broadcasted_iota(jnp.int32, (rows, HEAD_DIM), 0)
    _, after = start_of(lengths, docs, begin)
    continued = row < after - begin
    copies = []
    for i, d in enumerate(chosen):
        columns = columns_of(me ^ d, width)
        inner = own[:, columns]
        scales = gain[:, columns]
        for span in heads_of(heads):
            mixed = inner[:, span] + jnp.where(continued, parts[i][:, span], 0.0)
            scale = lax.rsqrt(jnp.mean(mixed * mixed, axis=-1, keepdims=True) + EPSILON)
            buffer[i, :, span] = (mixed * scale * scales[:, span]).astype(jnp.bfloat16)
        copy = pltpu.make_async_copy(buffer.at[i], out.at[:, columns], sems.at[i])
        copy.start()
        copies.append(copy)
    for copy in copies:
        copy.wait()


def body(queries, keys, values, lengths, norm_gain):
    rows, columns = queries.shape
    head_count = columns // HEAD_DIM
    docs = lengths.shape[0]
    inner_count = lax.axis_size("inner")
    devices = lax.axis_size("outer") * inner_count
    members = CORES * inner_count
    half = inner_count
    planes = devices // members
    heads = head_count // members
    width = heads * HEAD_DIM
    reach = -(-(devices // SHARE) // members)
    everyone = ("outer", "inner")
    index = lax.axis_index("outer") * inner_count + lax.axis_index("inner")
    me = index % members
    base = (index - me) * rows
    place = jnp.stack([me, base, index * rows]).astype(jnp.int32)
    f32, bf16 = jnp.float32, jnp.bfloat16
    params = pltpu.CompilerParams(vmem_limit_bytes=48 * 1024 * 1024)

    def call(kernel, name, out_shape, in_specs, out_specs, scratch=(), flops=0, moved=0, aliases=None):
        return pl.pallas_call(
            kernel,
            out_shape=out_shape,
            in_specs=in_specs,
            out_specs=out_specs,
            scratch_shapes=scratch,
            compiler_params=params,
            cost_estimate=pl.CostEstimate(flops=flops, bytes_accessed=moved, transcendentals=0),
            input_output_aliases=aliases or {},
            name=name,
        )

    def shape(*sizes, dtype=f32):
        return jax.ShapeDtypeStruct(sizes, dtype)

    def swap(part, d):
        pairs = [(g, g - g % members + (g % members ^ d)) for g in range(devices)]
        return lax.ppermute(part, everyone, pairs)

    block_bytes = rows * columns * 4
    parts = call(
        functools.partial(spread, members, width),
        "spread",
        [shape(2, rows, width)] * half + [shape(half, 3, rows, width)],
        [SMEM, HBM, HBM, HBM],
        [VMEM] * (half + 1),
        [pltpu.VMEM((members, rows, width), bf16)] * 3 + [pltpu.SemaphoreType.DMA((3, members))],
        moved=4 * block_bytes,
    )(place, queries, keys, values)
    near_got = [parts[0]] + [swap(parts[e], e) for e in range(1, half)]
    swapped = swap(parts[half], half)
    far_parts = call(
        functools.partial(forward, half),
        "forward",
        [shape(2, rows, width)] * (half - 1),
        [VMEM],
        [VMEM] * (half - 1),
        moved=2 * block_bytes,
    )(swapped)
    far_got = [swapped] + [swap(part, e + 1) for e, part in enumerate(far_parts)]
    gates = near_got[1:]
    query_parts = call(
        functools.partial(join_queries, half, width, len(gates)),
        "join_queries",
        [shape(CORES, rows, width)] * half,
        [SMEM, VMEM, VMEM] + [ANY] * len(gates),
        [VMEM] * half,
        moved=2 * block_bytes,
    )(place, queries, swapped, *gates)
    query_got = [query_parts[0]] + [swap(query_parts[e], e) for e in range(1, half)]

    own = call(
        functools.partial(inside, head_count, docs, rows),
        "inside",
        shape(rows, columns),
        [SMEM, SMEM, VMEM, VMEM, VMEM],
        VMEM,
        flops=4 * rows * rows * columns,
        moved=3 * block_bytes,
    )(place, lengths, queries, keys, values)

    carry, total = call(
        functools.partial(gather_states, members, heads, docs, rows),
        "gather_states",
        [shape(members, heads, HEAD_DIM, HEAD_DIM), shape(heads, HEAD_DIM, HEAD_DIM)],
        [SMEM, SMEM] + [VMEM] * members + [ANY],
        [VMEM] * 2,
        [pltpu.VMEM((members, rows, width), bf16)] * 2,
        flops=2 * rows * HEAD_DIM * columns,
        moved=4 * block_bytes,
    )(place, lengths, *near_got, *far_got, query_parts[0])
    up = [(g, g + members) for g in range(devices - members)]
    moving = lax.ppermute(total, everyone, up)
    earlier = moving
    if reach > 1:
        starts = BLOCK * (jnp.cumsum(lengths) - lengths)
        opens = jnp.max(jnp.where(starts <= base, starts, 0))
        for k in range(2, min(reach, planes - 1) + 1):
            moving = lax.ppermute(moving, everyone, up)
            earlier = earlier + jnp.where(opens < base - (k - 1) * members * rows, moving, 0.0)
    crossed = call(
        functools.partial(reach_back, members, heads, docs, rows),
        "reach_back",
        [shape(rows, width)] * members,
        [SMEM, SMEM] + [VMEM] * (half + 2) + [ANY],
        [VMEM] * members,
        flops=2 * rows * HEAD_DIM * columns,
        moved=4 * block_bytes,
    )(place, lengths, *query_got, carry, earlier, own)
    crossed_got = [crossed[0]] + [swap(crossed[d], d) for d in range(1, members)]

    gain = norm_gain.reshape(1, columns)
    first = [0] + list(range(half, members))
    last = list(range(1, half))
    out = None
    for chosen in (first, last):
        more = [] if out is None else [out]
        out = call(
            functools.partial(finish, chosen, heads, docs, rows),
            "finish",
            shape(rows, columns, dtype=bf16),
            [SMEM, SMEM, VMEM, VMEM] + [VMEM] * len(chosen) + [ANY] * len(more),
            ANY,
            [pltpu.VMEM((len(chosen), rows, width), bf16), pltpu.SemaphoreType.DMA((len(chosen),))],
            moved=2 * block_bytes,
            aliases={4 + len(chosen): 0} if more else None,
        )(place, lengths, own, gain, *[crossed_got[d] for d in chosen], *more)
    return out


def solution(mesh):
    placed = (
        P(("outer", "inner"), None),
        P(("outer", "inner"), None),
        P(("outer", "inner"), None),
        P(),
        P(),
    )
    return jax.shard_map(
        body, mesh=mesh, in_specs=placed, out_specs=P(("outer", "inner"), None), check_vma=False
    )
```

```python
import functools

import jax
import jax.numpy as jnp
from jax import lax
from jax.experimental import pallas as pl
from jax.experimental.pallas import tpu as pltpu
from jax.sharding import PartitionSpec as P

HEAD_DIM = 128
BLOCK = 16
CORES = 2
SHARE = 4
EPSILON = 1e-05
SMEM = pl.BlockSpec(memory_space=pltpu.SMEM)
VMEM = pl.BlockSpec(memory_space=pltpu.VMEM)
ANY = pl.BlockSpec(memory_space=pl.ANY)
HBM = pl.BlockSpec(memory_space=pltpu.HBM)


def columns_of(member, width):
    return pl.ds(pl.multiple_of(member * width, width), width)


def heads_of(heads):
    return [slice(h * HEAD_DIM, (h + 1) * HEAD_DIM) for h in range(heads)]


def start_of(lengths, docs, token):
    begin = jnp.int32(0)
    found = jnp.int32(0)
    after = jnp.int32(jnp.iinfo(jnp.int32).max)
    for i in range(docs):
        found = jnp.where(begin <= token, begin, found)
        after = jnp.where(begin > token, jnp.minimum(begin, after), after)
        begin = begin + lengths[i] * BLOCK
    return found, after


def spread(members, width, place, queries, keys, values, *refs):
    half = members // CORES
    near, cross = refs[:half], refs[half]
    buffers, sems = refs[half + 1 : half + 4], refs[half + 4]
    me = place[0]

    def copies(d):
        span = columns_of(me ^ d, width)
        sources = (keys, values) if d < half else (keys, values, queries)
        return [
            pltpu.make_async_copy(source.at[:, span], buffers[i].at[d], sems.at[i, d])
            for i, source in enumerate(sources)
        ]

    order = list(reversed(range(half))) + list(range(half, members))
    for d in order:
        for copy in copies(d):
            copy.start()
    for d in order:
        for i, copy in enumerate(copies(d)):
            copy.wait()
            part = buffers[i][d].astype(jnp.float32)
            if d < half:
                near[half - 1 - d][i] = part
            else:
                cross[d - half, i] = part


def forward(half, swapped, *outs):
    for e in range(1, half):
        outs[half - 1 - e][...] = swapped[e, 0:2]


def join_queries(half, width, gates, place, queries, swapped, *refs):
    outs = refs[gates:]
    me = place[0]
    for e in range(half):
        outs[half - 1 - e][0] = queries[:, columns_of(me ^ e, width)].astype(jnp.float32)
        outs[half - 1 - e][1] = swapped[e, 2]


def gather_states(members, heads, docs, rows, place, lengths, *refs):
    half = members // CORES
    parts = refs[:half][::-1] + refs[half:members][::-1]
    carry_out, total_out, key_blocks, value_blocks = refs[members + 1 :]
    me, base = place[0], place[1]
    row = lax.broadcasted_iota(jnp.int32, (rows, heads * HEAD_DIM), 0)
    for d in range(members):
        j = me ^ d
        since, _ = start_of(lengths, docs, base + (j + 1) * rows)
        key, value = (parts[d][0, 0], parts[d][0, 1]) if d == half else (parts[d][0], parts[d][1])
        key_blocks[j] = jnp.where(row >= since - base - j * rows, key, 0.0).astype(jnp.bfloat16)
        value_blocks[j] = value.astype(jnp.bfloat16)
    state = [jnp.zeros((HEAD_DIM, HEAD_DIM), jnp.float32) for _ in range(heads)]
    for j in range(members):
        since, _ = start_of(lengths, docs, base + (j + 1) * rows)
        keep = jnp.where(since <= base + j * rows, 1.0, 0.0).astype(jnp.float32)
        for h, span in enumerate(heads_of(heads)):
            carry_out[j, h] = state[h]
            own = lax.dot_general(
                key_blocks[j, :, span],
                value_blocks[j, :, span],
                (((0,), (0,)), ((), ())),
                preferred_element_type=jnp.float32,
            )
            state[h] = keep * state[h] + own
    for h in range(heads):
        total_out[h] = state[h]


def inside(head_count, docs, rows, place, lengths, queries, keys, values, out):
    begin = place[2]
    row = lax.broadcasted_iota(jnp.int32, (rows, rows), 0)
    lane = lax.broadcasted_iota(jnp.int32, (rows, rows), 1)
    since = jnp.zeros((rows, rows), jnp.int32)
    start = -begin
    for i in range(docs):
        since = jnp.where(start <= row, start, since)
        start = start + lengths[i] * BLOCK
    allowed = (lane <= row) & (lane >= since)
    for span in heads_of(head_count):
        scores = lax.dot_general(
            queries[:, span], keys[:, span], (((1,), (1,)), ((), ())), preferred_element_type=jnp.float32
        )
        weights = jnp.where(allowed, scores, 0.0).astype(jnp.bfloat16)
        out[:, span] = jnp.dot(weights, values[:, span], preferred_element_type=jnp.float32)


def reach_back(members, heads, docs, rows, place, lengths, *refs):
    half = members // CORES
    query_parts = refs[:half][::-1]
    carry, earlier = refs[half : half + 2]
    outs = refs[half + 3 :][::-1]
    me, base = place[0], place[1]
    for e in range(half):
        for side in range(CORES):
            d = e ^ (side * half)
            j = me ^ d
            first, _ = start_of(lengths, docs, base + j * rows)
            before = jnp.where(first < base, 1.0, 0.0).astype(jnp.float32)
            for h, span in enumerate(heads_of(heads)):
                held = (carry[j, h] + before * earlier[h]).astype(jnp.bfloat16)
                query = query_parts[e][side, :, span].astype(jnp.bfloat16)
                outs[d][:, span] = jnp.dot(query, held, preferred_element_type=jnp.float32)


def finish(chosen, heads, docs, rows, place, lengths, own, gain, *refs):
    count = len(chosen)
    parts, out = refs[:count], refs[-3]
    buffer, sems = refs[-2:]
    width = heads * HEAD_DIM
    me, begin = place[0], place[2]
    row = lax.broadcasted_iota(jnp.int32, (rows, HEAD_DIM), 0)
    _, after = start_of(lengths, docs, begin)
    continued = row < after - begin
    copies = []
    for i, d in enumerate(chosen):
        columns = columns_of(me ^ d, width)
        inner = own[:, columns]
        scales = gain[:, columns]
        for span in heads_of(heads):
            mixed = inner[:, span] + jnp.where(continued, parts[i][:, span], 0.0)
            scale = lax.rsqrt(jnp.mean(mixed * mixed, axis=-1, keepdims=True) + EPSILON)
            buffer[i, :, span] = (mixed * scale * scales[:, span]).astype(jnp.bfloat16)
        copy = pltpu.make_async_copy(buffer.at[i], out.at[:, columns], sems.at[i])
        copy.start()
        copies.append(copy)
    for copy in copies:
        copy.wait()


def body(queries, keys, values, lengths, norm_gain):
    rows, columns = queries.shape
    head_count = columns // HEAD_DIM
    docs = lengths.shape[0]
    inner_count = lax.axis_size("inner")
    devices = lax.axis_size("outer") * inner_count
    members = CORES * inner_count
    half = inner_count
    planes = devices // members
    heads = head_count // members
    width = heads * HEAD_DIM
    reach = -(-(devices // SHARE) // members)
    everyone = ("outer", "inner")
    index = lax.axis_index("outer") * inner_count + lax.axis_index("inner")
    me = index % members
    base = (index - me) * rows
    place = jnp.stack([me, base, index * rows]).astype(jnp.int32)
    f32, bf16 = jnp.float32, jnp.bfloat16
    params = pltpu.CompilerParams(vmem_limit_bytes=48 * 1024 * 1024)

    def call(kernel, name, out_shape, in_specs, out_specs, scratch=(), flops=0, moved=0, aliases=None):
        return pl.pallas_call(
            kernel,
            out_shape=out_shape,
            in_specs=in_specs,
            out_specs=out_specs,
            scratch_shapes=scratch,
            compiler_params=params,
            cost_estimate=pl.CostEstimate(flops=flops, bytes_accessed=moved, transcendentals=0),
            input_output_aliases=aliases or {},
            name=name,
        )

    def shape(*sizes, dtype=f32):
        return jax.ShapeDtypeStruct(sizes, dtype)

    def swap(part, d):
        pairs = [(g, g - g % members + (g % members ^ d)) for g in range(devices)]
        return lax.ppermute(part, everyone, pairs)

    downward = list(reversed(range(half)))
    block_bytes = rows * columns * 4
    parts = call(
        functools.partial(spread, members, width),
        "spread",
        [shape(2, rows, width)] * half + [shape(half, 3, rows, width)],
        [SMEM, HBM, HBM, HBM],
        [VMEM] * (half + 1),
        [pltpu.VMEM((members, rows, width), bf16)] * 3 + [pltpu.SemaphoreType.DMA((3, members))],
    )(place, *[pltpu.with_memory_space_constraint(x, pltpu.HBM) for x in (queries, keys, values)])
    near_got = [swap(part, e) if e else part for e, part in zip(downward, parts)]
    swapped = swap(parts[half], half)
    far_parts = call(
        functools.partial(forward, half),
        "forward",
        [shape(2, rows, width)] * (half - 1),
        [VMEM],
        [VMEM] * (half - 1),
        moved=2 * block_bytes,
    )(swapped)
    far_got = [swap(part, e) for e, part in zip(downward, far_parts)] + [swapped]
    gates = near_got[:-1]
    query_parts = call(
        functools.partial(join_queries, half, width, len(gates)),
        "join_queries",
        [shape(CORES, rows, width)] * half,
        [SMEM, VMEM, VMEM] + [ANY] * len(gates),
        [VMEM] * half,
        moved=2 * block_bytes,
    )(place, queries, swapped, *gates)
    query_got = [swap(part, e) if e else part for e, part in zip(downward, query_parts)]

    own = call(
        functools.partial(inside, head_count, docs, rows),
        "inside",
        shape(rows, columns),
        [SMEM, SMEM, VMEM, VMEM, VMEM],
        VMEM,
        flops=4 * rows * rows * columns,
        moved=3 * block_bytes,
    )(place, lengths, queries, keys, values)

    carry, total = call(
        functools.partial(gather_states, members, heads, docs, rows),
        "gather_states",
        [shape(members, heads, HEAD_DIM, HEAD_DIM), shape(heads, HEAD_DIM, HEAD_DIM)],
        [SMEM, SMEM] + [VMEM] * members + [ANY],
        [VMEM] * 2,
        [pltpu.VMEM((members, rows, width), bf16)] * 2,
        flops=2 * rows * HEAD_DIM * columns,
        moved=4 * block_bytes,
    )(place, lengths, *near_got, *far_got, query_parts[-1])
    up = [(g, g + members) for g in range(devices - members)]
    moving = lax.ppermute(total, everyone, up)
    earlier = moving
    if reach > 1:
        starts = BLOCK * (jnp.cumsum(lengths) - lengths)
        opens = jnp.max(jnp.where(starts <= base, starts, 0))
        for k in range(2, min(reach, planes - 1) + 1):
            moving = lax.ppermute(moving, everyone, up)
            earlier = earlier + jnp.where(opens < base - (k - 1) * members * rows, moving, 0.0)
    crossed = call(
        functools.partial(reach_back, members, heads, docs, rows),
        "reach_back",
        [shape(rows, width)] * members,
        [SMEM, SMEM] + [VMEM] * (half + 2) + [ANY],
        [VMEM] * members,
        flops=2 * rows * HEAD_DIM * columns,
        moved=4 * block_bytes,
    )(place, lengths, *query_got, carry, earlier, own)
    crossed_got = [swap(crossed[members - 1 - d], d) if d else crossed[-1] for d in range(members)]

    gain = norm_gain.reshape(1, columns)
    last = [d for d in range(members) if d % half in (1, 2)]
    first = [d for d in reversed(range(members)) if d not in last]
    out = None
    for chosen in (first, last):
        more = [] if out is None else [out]
        out = call(
            functools.partial(finish, chosen, heads, docs, rows),
            "finish",
            shape(rows, columns, dtype=bf16),
            [SMEM, SMEM, VMEM, VMEM] + [VMEM] * len(chosen) + [ANY] * len(more),
            ANY,
            [pltpu.VMEM((len(chosen), rows, width), bf16), pltpu.SemaphoreType.DMA((len(chosen),))],
            moved=2 * block_bytes,
            aliases={4 + len(chosen): 0} if more else None,
        )(place, lengths, own, gain, *[crossed_got[d] for d in chosen], *more)
    return out


def solution(mesh):
    placed = (
        P(("outer", "inner"), None),
        P(("outer", "inner"), None),
        P(("outer", "inner"), None),
        P(),
        P(),
    )
    return jax.shard_map(
        body, mesh=mesh, in_specs=placed, out_specs=P(("outer", "inner"), None), check_vma=False
    )
```

```python
import functools

import jax
import jax.numpy as jnp
from jax import lax
from jax.experimental import pallas as pl
from jax.experimental.pallas import tpu as pltpu
from jax.sharding import PartitionSpec as P

HEAD_DIM = 128
BLOCK = 16
CORES = 2
SHARE = 4
EPSILON = 1e-05
SMEM = pl.BlockSpec(memory_space=pltpu.SMEM)
VMEM = pl.BlockSpec(memory_space=pltpu.VMEM)
ANY = pl.BlockSpec(memory_space=pl.ANY)
HBM = pl.BlockSpec(memory_space=pltpu.HBM)


def columns_of(member, width):
    return pl.ds(pl.multiple_of(member * width, width), width)


def heads_of(heads):
    return [slice(h * HEAD_DIM, (h + 1) * HEAD_DIM) for h in range(heads)]


def start_of(lengths, docs, token):
    begin = jnp.int32(0)
    found = jnp.int32(0)
    after = jnp.int32(jnp.iinfo(jnp.int32).max)
    for i in range(docs):
        found = jnp.where(begin <= token, begin, found)
        after = jnp.where(begin > token, jnp.minimum(begin, after), after)
        begin = begin + lengths[i] * BLOCK
    return found, after


def spread(members, width, place, keys, values, *refs):
    half = members // CORES
    near, cross = refs[:half], refs[half]
    buffers, sems = refs[half + 1 : half + 3], refs[half + 3]
    me = place[0]

    def copies(d):
        span = columns_of(me ^ d, width)
        return [
            pltpu.make_async_copy(source.at[:, span], buffers[i].at[d], sems.at[i, d])
            for i, source in enumerate((keys, values))
        ]

    order = list(reversed(range(half))) + list(range(half, members))
    for d in order:
        for copy in copies(d):
            copy.start()
    for d in order:
        for i, copy in enumerate(copies(d)):
            copy.wait()
            part = buffers[i][d].astype(jnp.float32)
            if d < half:
                near[half - 1 - d][i] = part
            else:
                cross[d - half, i] = part


def forward(half, swapped, *outs):
    for e in range(1, half):
        outs[half - 1 - e][...] = swapped[e]


def pick_queries(half, width, place, queries, out):
    for e in range(half):
        out[e] = queries[:, columns_of(place[0] ^ e ^ half, width)].astype(jnp.float32)


def join_queries(half, width, gates, place, queries, swapped, *refs):
    outs = refs[gates:]
    me = place[0]
    for e in range(half):
        outs[half - 1 - e][0] = queries[:, columns_of(me ^ e, width)].astype(jnp.float32)
        outs[half - 1 - e][1] = swapped[e]


def gather_states(members, heads, docs, rows, place, lengths, *refs):
    half = members // CORES
    parts = refs[:half][::-1] + refs[half:members][::-1]
    carry_out, total_out, key_blocks, value_blocks = refs[members + 1 :]
    me, base = place[0], place[1]
    row = lax.broadcasted_iota(jnp.int32, (rows, heads * HEAD_DIM), 0)
    for d in range(members):
        j = me ^ d
        since, _ = start_of(lengths, docs, base + (j + 1) * rows)
        key, value = (parts[d][0, 0], parts[d][0, 1]) if d == half else (parts[d][0], parts[d][1])
        key_blocks[j] = jnp.where(row >= since - base - j * rows, key, 0.0).astype(jnp.bfloat16)
        value_blocks[j] = value.astype(jnp.bfloat16)
    state = [jnp.zeros((HEAD_DIM, HEAD_DIM), jnp.float32) for _ in range(heads)]
    for j in range(members):
        since, _ = start_of(lengths, docs, base + (j + 1) * rows)
        keep = jnp.where(since <= base + j * rows, 1.0, 0.0).astype(jnp.float32)
        for h, span in enumerate(heads_of(heads)):
            carry_out[j, h] = state[h]
            own = lax.dot_general(
                key_blocks[j, :, span],
                value_blocks[j, :, span],
                (((0,), (0,)), ((), ())),
                preferred_element_type=jnp.float32,
            )
            state[h] = keep * state[h] + own
    for h in range(heads):
        total_out[h] = state[h]


def inside(head_count, docs, rows, place, lengths, queries, keys, values, out):
    begin = place[2]
    row = lax.broadcasted_iota(jnp.int32, (rows, rows), 0)
    lane = lax.broadcasted_iota(jnp.int32, (rows, rows), 1)
    since = jnp.zeros((rows, rows), jnp.int32)
    start = -begin
    for i in range(docs):
        since = jnp.where(start <= row, start, since)
        start = start + lengths[i] * BLOCK
    allowed = (lane <= row) & (lane >= since)
    for span in heads_of(head_count):
        scores = lax.dot_general(
            queries[:, span], keys[:, span], (((1,), (1,)), ((), ())), preferred_element_type=jnp.float32
        )
        weights = jnp.where(allowed, scores, 0.0).astype(jnp.bfloat16)
        out[:, span] = jnp.dot(weights, values[:, span], preferred_element_type=jnp.float32)


def reach_back(members, heads, docs, rows, chosen, gates, place, lengths, carry, earlier, *refs):
    count = len(chosen)
    half = members // CORES
    query_parts, outs = refs[:count], refs[count + gates :]
    me, base = place[0], place[1]
    for n, e in enumerate(chosen):
        for side in range(CORES):
            j = me ^ e ^ (side * half)
            first, _ = start_of(lengths, docs, base + j * rows)
            before = jnp.where(first < base, 1.0, 0.0).astype(jnp.float32)
            for h, span in enumerate(heads_of(heads)):
                held = (carry[j, h] + before * earlier[h]).astype(jnp.bfloat16)
                query = query_parts[n][side, :, span].astype(jnp.bfloat16)
                outs[n * CORES + side][:, span] = jnp.dot(query, held, preferred_element_type=jnp.float32)


def finish(chosen, heads, docs, rows, place, lengths, own, gain, *refs):
    count = len(chosen)
    parts, out = refs[:count], refs[-3]
    buffer, sems = refs[-2:]
    width = heads * HEAD_DIM
    me, begin = place[0], place[2]
    row = lax.broadcasted_iota(jnp.int32, (rows, HEAD_DIM), 0)
    _, after = start_of(lengths, docs, begin)
    continued = row < after - begin
    copies = []
    for i, d in enumerate(chosen):
        columns = columns_of(me ^ d, width)
        inner = own[:, columns]
        scales = gain[:, columns]
        for span in heads_of(heads):
            mixed = inner[:, span] + jnp.where(continued, parts[i][:, span], 0.0)
            scale = lax.rsqrt(jnp.mean(mixed * mixed, axis=-1, keepdims=True) + EPSILON)
            buffer[i, :, span] = (mixed * scale * scales[:, span]).astype(jnp.bfloat16)
        copy = pltpu.make_async_copy(buffer.at[i], out.at[:, columns], sems.at[i])
        copy.start()
        copies.append(copy)
    for copy in copies:
        copy.wait()


def body(queries, keys, values, lengths, norm_gain):
    rows, columns = queries.shape
    head_count = columns // HEAD_DIM
    docs = lengths.shape[0]
    inner_count = lax.axis_size("inner")
    devices = lax.axis_size("outer") * inner_count
    members = CORES * inner_count
    half = inner_count
    planes = devices // members
    heads = head_count // members
    width = heads * HEAD_DIM
    reach = -(-(devices // SHARE) // members)
    everyone = ("outer", "inner")
    index = lax.axis_index("outer") * inner_count + lax.axis_index("inner")
    me = index % members
    base = (index - me) * rows
    place = jnp.stack([me, base, index * rows]).astype(jnp.int32)
    f32, bf16 = jnp.float32, jnp.bfloat16
    params = pltpu.CompilerParams(vmem_limit_bytes=48 * 1024 * 1024)

    def call(kernel, name, out_shape, in_specs, out_specs, scratch=(), flops=0, moved=0, aliases=None):
        return pl.pallas_call(
            kernel,
            out_shape=out_shape,
            in_specs=in_specs,
            out_specs=out_specs,
            scratch_shapes=scratch,
            compiler_params=params,
            cost_estimate=pl.CostEstimate(flops=flops, bytes_accessed=moved, transcendentals=0),
            input_output_aliases=aliases or {},
            name=name,
        )

    def shape(*sizes, dtype=f32):
        return jax.ShapeDtypeStruct(sizes, dtype)

    def swap(part, d):
        pairs = [(g, g - g % members + (g % members ^ d)) for g in range(devices)]
        return lax.ppermute(part, everyone, pairs)

    downward = list(reversed(range(half)))
    block_bytes = rows * columns * 4
    parts = call(
        functools.partial(spread, members, width),
        "spread",
        [shape(2, rows, width)] * half + [shape(half, 2, rows, width)],
        [SMEM, HBM, HBM],
        [VMEM] * (half + 1),
        [pltpu.VMEM((members, rows, width), bf16)] * 2 + [pltpu.SemaphoreType.DMA((2, members))],
    )(place, *[pltpu.with_memory_space_constraint(x, pltpu.HBM) for x in (keys, values)])
    near_got = [swap(part, e) if e else part for e, part in zip(downward, parts)]
    swapped = swap(parts[half], half)
    far_parts = call(
        functools.partial(forward, half),
        "forward",
        [shape(2, rows, width)] * (half - 1),
        [VMEM],
        [VMEM] * (half - 1),
        moved=2 * block_bytes,
    )(swapped)
    far_got = [swap(part, e) for e, part in zip(downward, far_parts)] + [swapped]
    picked = call(
        functools.partial(pick_queries, half, width),
        "pick_queries",
        shape(half, rows, width),
        [SMEM, VMEM],
        VMEM,
        moved=block_bytes,
    )(place, queries)
    swapped_queries = swap(picked, half)
    gates = near_got[:-1]
    query_parts = call(
        functools.partial(join_queries, half, width, len(gates)),
        "join_queries",
        [shape(CORES, rows, width)] * half,
        [SMEM, VMEM, VMEM] + [ANY] * len(gates),
        [VMEM] * half,
        moved=2 * block_bytes,
    )(place, queries, swapped_queries, *gates)
    query_got = [swap(part, e) if e else part for e, part in zip(downward, query_parts)]

    own = call(
        functools.partial(inside, head_count, docs, rows),
        "inside",
        shape(rows, columns),
        [SMEM, SMEM, VMEM, VMEM, VMEM],
        VMEM,
        flops=4 * rows * rows * columns,
        moved=3 * block_bytes,
    )(place, lengths, queries, keys, values)

    carry, total = call(
        functools.partial(gather_states, members, heads, docs, rows),
        "gather_states",
        [shape(members, heads, HEAD_DIM, HEAD_DIM), shape(heads, HEAD_DIM, HEAD_DIM)],
        [SMEM, SMEM] + [VMEM] * members + [ANY],
        [VMEM] * 2,
        [pltpu.VMEM((members, rows, width), bf16)] * 2,
        flops=2 * rows * HEAD_DIM * columns,
        moved=4 * block_bytes,
    )(place, lengths, *near_got, *far_got, query_parts[-1])
    up = [(g, g + members) for g in range(devices - members)]
    moving = lax.ppermute(total, everyone, up)
    earlier = moving
    if reach > 1:
        starts = BLOCK * (jnp.cumsum(lengths) - lengths)
        opens = jnp.max(jnp.where(starts <= base, starts, 0))
        for k in range(2, min(reach, planes - 1) + 1):
            moving = lax.ppermute(moving, everyone, up)
            earlier = earlier + jnp.where(opens < base - (k - 1) * members * rows, moving, 0.0)
    crossed_got = {}
    late = [e for e in downward if e in (1, 2)]
    soon = [e for e in downward if e not in late]
    for chosen, gates in ((soon, [own]), (late, [])):
        crossed = call(
            functools.partial(reach_back, members, heads, docs, rows, chosen, len(gates)),
            "reach_back",
            [shape(rows, width)] * (CORES * len(chosen)),
            [SMEM, SMEM] + [VMEM] * (len(chosen) + 2) + [ANY] * len(gates),
            [VMEM] * (CORES * len(chosen)),
            flops=2 * rows * HEAD_DIM * width * CORES * len(chosen),
            moved=2 * block_bytes,
        )(place, lengths, carry, earlier, *[query_got[half - 1 - e] for e in chosen], *gates)
        for n, e in enumerate(chosen):
            for side in range(CORES):
                d = e ^ (side * half)
                part = crossed[n * CORES + side]
                crossed_got[d] = swap(part, d) if d else part

    gain = norm_gain.reshape(1, columns)
    out = None
    groups = [[e ^ (side * half) for e in soon for side in range(CORES)]]
    groups += [[e ^ (side * half) for e in late] for side in range(CORES)]
    for chosen in groups:
        more = [] if out is None else [out]
        out = call(
            functools.partial(finish, chosen, heads, docs, rows),
            "finish",
            shape(rows, columns, dtype=bf16),
            [SMEM, SMEM, VMEM, VMEM] + [VMEM] * len(chosen) + [ANY] * len(more),
            ANY,
            [pltpu.VMEM((len(chosen), rows, width), bf16), pltpu.SemaphoreType.DMA((len(chosen),))],
            moved=2 * block_bytes,
            aliases={4 + len(chosen): 0} if more else None,
        )(place, lengths, own, gain, *[crossed_got[d] for d in chosen], *more)
    return out


def solution(mesh):
    placed = (
        P(("outer", "inner"), None),
        P(("outer", "inner"), None),
        P(("outer", "inner"), None),
        P(),
        P(),
    )
    return jax.shard_map(
        body, mesh=mesh, in_specs=placed, out_specs=P(("outer", "inner"), None), check_vma=False
    )
```

```python
import functools

import jax
import jax.numpy as jnp
from jax import lax
from jax.experimental import pallas as pl
from jax.experimental.pallas import tpu as pltpu
from jax.sharding import PartitionSpec as P

HEAD_DIM = 128
BLOCK = 16
CORES = 2
SHARE = 4
EPSILON = 1e-05
SMEM = pl.BlockSpec(memory_space=pltpu.SMEM)
VMEM = pl.BlockSpec(memory_space=pltpu.VMEM)
ANY = pl.BlockSpec(memory_space=pl.ANY)
HBM = pl.BlockSpec(memory_space=pltpu.HBM)


def columns_of(member, width):
    return pl.ds(pl.multiple_of(member * width, width), width)


def position():
    inner_count = lax.axis_size("inner")
    index = lax.axis_index("outer") * inner_count + lax.axis_index("inner")
    return index, index % (CORES * inner_count)


def heads_of(heads):
    return [slice(h * HEAD_DIM, (h + 1) * HEAD_DIM) for h in range(heads)]


def start_of(lengths, docs, token):
    begin = jnp.int32(0)
    found = jnp.int32(0)
    after = jnp.int32(jnp.iinfo(jnp.int32).max)
    for i in range(docs):
        found = jnp.where(begin <= token, begin, found)
        after = jnp.where(begin > token, jnp.minimum(begin, after), after)
        begin = begin + lengths[i] * BLOCK
    return found, after


def spread(members, width, queries, keys, values, *refs):
    half = members // CORES
    near, cross = refs[:half], refs[half]
    buffers, sems = refs[half + 1 : half + 4], refs[half + 4]
    _, me = position()

    def copies(d):
        span = columns_of(me ^ d, width)
        sources = (keys, values) if d < half else (keys, values, queries)
        return [
            pltpu.make_async_copy(source.at[:, span], buffers[i].at[d], sems.at[i, d])
            for i, source in enumerate(sources)
        ]

    order = list(reversed(range(half))) + list(range(half, members))
    for d in order:
        for copy in copies(d):
            copy.start()
    for d in order:
        for i, copy in enumerate(copies(d)):
            copy.wait()
            part = buffers[i][d].astype(jnp.float32)
            if d < half:
                near[half - 1 - d][i] = part
            else:
                cross[d - half, i] = part


def forward(half, swapped, *outs):
    for e in range(1, half):
        outs[half - 1 - e][...] = swapped[e, 0:2]


def join_queries(members, width, rows, docs, gates, lengths, queries, swapped, *refs):
    half = members // CORES
    outs, table = refs[gates:-1], refs[-1]
    index, me = position()
    for e in range(half):
        outs[half - 1 - e][0] = queries[:, columns_of(me ^ e, width)].astype(jnp.float32)
        outs[half - 1 - e][1] = swapped[e, 2]
    base = (index - me) * rows
    for j in range(members + 1):
        found, _ = start_of(lengths, docs, base + j * rows)
        table[j : j + 1, :] = jnp.full((1, HEAD_DIM), found - base, jnp.int32)
    _, after = start_of(lengths, docs, index * rows)
    table[members + 1 : members + 2, :] = jnp.full((1, HEAD_DIM), after - index * rows, jnp.int32)


def gather_states(members, heads, rows, table, *refs):
    half = members // CORES
    parts = refs[:half][::-1] + refs[half:members][::-1]
    carry_out, total_out, key_blocks, value_blocks = refs[members:]
    _, me = position()
    row = lax.broadcasted_iota(jnp.int32, (rows, HEAD_DIM), 0)
    for d in range(members):
        j = me ^ d
        kept = row >= table[pl.ds(j + 1, 1), :] - j * rows
        key, value = (parts[d][0, 0], parts[d][0, 1]) if d == half else (parts[d][0], parts[d][1])
        for span in heads_of(heads):
            key_blocks[j, :, span] = jnp.where(kept, key[:, span], 0.0).astype(jnp.bfloat16)
        value_blocks[j] = value.astype(jnp.bfloat16)
    state = [jnp.zeros((HEAD_DIM, HEAD_DIM), jnp.float32) for _ in range(heads)]
    for j in range(members):
        keep = jnp.where(table[j + 1 : j + 2, :] <= j * rows, 1.0, 0.0).astype(jnp.float32)
        for h, span in enumerate(heads_of(heads)):
            carry_out[j, h] = state[h]
            own = lax.dot_general(
                key_blocks[j, :, span],
                value_blocks[j, :, span],
                (((0,), (0,)), ((), ())),
                preferred_element_type=jnp.float32,
            )
            state[h] = keep * state[h] + own
    for h in range(heads):
        total_out[h] = state[h]


def inside(head_count, docs, rows, lengths, queries, keys, values, out):
    begin = position()[0] * rows
    row = lax.broadcasted_iota(jnp.int32, (rows, rows), 0)
    lane = lax.broadcasted_iota(jnp.int32, (rows, rows), 1)
    since = jnp.zeros((rows, rows), jnp.int32)
    start = -begin
    for i in range(docs):
        since = jnp.where(start <= row, start, since)
        start = start + lengths[i] * BLOCK
    allowed = (lane <= row) & (lane >= since)
    for span in heads_of(head_count):
        scores = lax.dot_general(
            queries[:, span], keys[:, span], (((1,), (1,)), ((), ())), preferred_element_type=jnp.float32
        )
        weights = jnp.where(allowed, scores, 0.0).astype(jnp.bfloat16)
        out[:, span] = jnp.dot(weights, values[:, span], preferred_element_type=jnp.float32)


def reach_back(members, heads, table, *refs):
    half = members // CORES
    query_parts = refs[:half][::-1]
    carry, earlier = refs[half : half + 2]
    outs = refs[half + 3 :][::-1]
    _, me = position()
    for e in reversed(range(half)):
        for side in range(CORES):
            d = e ^ (side * half)
            j = me ^ d
            before = jnp.where(table[pl.ds(j, 1), :] < 0, 1.0, 0.0).astype(jnp.float32)
            for h, span in enumerate(heads_of(heads)):
                held = (carry[j, h] + before * earlier[h]).astype(jnp.bfloat16)
                query = query_parts[e][side, :, span].astype(jnp.bfloat16)
                outs[d][:, span] = jnp.dot(query, held, preferred_element_type=jnp.float32)


def finish(chosen, members, heads, rows, table, own, gain, *refs):
    count = len(chosen)
    parts, out = refs[:count], refs[-3]
    buffer, sems = refs[-2:]
    width = heads * HEAD_DIM
    _, me = position()
    continued = lax.broadcasted_iota(jnp.int32, (rows, HEAD_DIM), 0) < table[members + 1 : members + 2, :]
    copies = []
    for i, d in enumerate(chosen):
        columns = columns_of(me ^ d, width)
        inner = own[:, columns]
        scales = gain[:, columns]
        for span in heads_of(heads):
            mixed = inner[:, span] + jnp.where(continued, parts[i][:, span], 0.0)
            scale = lax.rsqrt(jnp.mean(mixed * mixed, axis=-1, keepdims=True) + EPSILON)
            buffer[i, :, span] = (mixed * scale * scales[:, span]).astype(jnp.bfloat16)
        copy = pltpu.make_async_copy(buffer.at[i], out.at[:, columns], sems.at[i])
        copy.start()
        copies.append(copy)
    for copy in copies:
        copy.wait()


def body(queries, keys, values, lengths, norm_gain):
    rows, columns = queries.shape
    head_count = columns // HEAD_DIM
    docs = lengths.shape[0]
    inner_count = lax.axis_size("inner")
    devices = lax.axis_size("outer") * inner_count
    members = CORES * inner_count
    half = inner_count
    planes = devices // members
    heads = head_count // members
    width = heads * HEAD_DIM
    reach = -(-(devices // SHARE) // members)
    everyone = ("outer", "inner")
    index = lax.axis_index("outer") * inner_count + lax.axis_index("inner")
    me = index % members
    base = (index - me) * rows
    f32, bf16 = jnp.float32, jnp.bfloat16

    def call(kernel, name, out_shape, in_specs, out_specs, scratch=(), flops=0, moved=0, aliases=None):
        return pl.pallas_call(
            kernel,
            out_shape=out_shape,
            in_specs=in_specs,
            out_specs=out_specs,
            scratch_shapes=scratch,
            compiler_params=pltpu.CompilerParams(vmem_limit_bytes=48 * 1024 * 1024),
            cost_estimate=pl.CostEstimate(flops=flops, bytes_accessed=moved, transcendentals=0),
            input_output_aliases=aliases or {},
            name=name,
        )

    def shape(*sizes, dtype=f32):
        return jax.ShapeDtypeStruct(sizes, dtype)

    def swap(part, d):
        pairs = [(g, g - g % members + (g % members ^ d)) for g in range(devices)]
        return lax.ppermute(part, everyone, pairs)

    downward = list(reversed(range(half)))
    block_bytes = rows * columns * 4
    parts = call(
        functools.partial(spread, members, width),
        "spread",
        [shape(2, rows, width)] * half + [shape(half, 3, rows, width)],
        [HBM, HBM, HBM],
        [VMEM] * (half + 1),
        [pltpu.VMEM((members, rows, width), bf16)] * 3 + [pltpu.SemaphoreType.DMA((3, members))],
    )(*[pltpu.with_memory_space_constraint(x, pltpu.HBM) for x in (queries, keys, values)])
    near_got = [swap(part, e) if e else part for e, part in zip(downward, parts)]
    swapped = swap(parts[half], half)
    far_parts = call(
        functools.partial(forward, half),
        "forward",
        [shape(2, rows, width)] * (half - 1),
        [VMEM],
        [VMEM] * (half - 1),
        moved=2 * block_bytes,
    )(swapped)
    far_got = [swap(part, e) for e, part in zip(downward, far_parts)] + [swapped]
    gates = near_got[:-1]
    *query_parts, table = call(
        functools.partial(join_queries, members, width, rows, docs, len(gates)),
        "join_queries",
        [shape(CORES, rows, width)] * half + [shape(members + 2, HEAD_DIM, dtype=jnp.int32)],
        [SMEM, VMEM, VMEM] + [ANY] * len(gates),
        [VMEM] * (half + 1),
        moved=2 * block_bytes,
    )(lengths, queries, swapped, *gates)
    query_got = [swap(part, e) if e else part for e, part in zip(downward, query_parts)]

    own = call(
        functools.partial(inside, head_count, docs, rows),
        "inside",
        shape(rows, columns),
        [SMEM, VMEM, VMEM, VMEM],
        VMEM,
        flops=4 * rows * rows * columns,
        moved=3 * block_bytes,
    )(lengths, queries, keys, values)

    carry, total = call(
        functools.partial(gather_states, members, heads, rows),
        "gather_states",
        [shape(members, heads, HEAD_DIM, HEAD_DIM), shape(heads, HEAD_DIM, HEAD_DIM)],
        [VMEM] * (members + 1),
        [VMEM] * 2,
        [pltpu.VMEM((members, rows, width), bf16)] * 2,
        flops=2 * rows * HEAD_DIM * columns,
        moved=4 * block_bytes,
    )(table, *near_got, *far_got)
    up = [(g, g + members) for g in range(devices - members)]
    moving = lax.ppermute(total, everyone, up)
    earlier = moving
    if reach > 1:
        starts = BLOCK * (jnp.cumsum(lengths) - lengths)
        opens = jnp.max(jnp.where(starts <= base, starts, 0))
        for k in range(2, min(reach, planes - 1) + 1):
            moving = lax.ppermute(moving, everyone, up)
            earlier = earlier + jnp.where(opens < base - (k - 1) * members * rows, moving, 0.0)
    crossed = call(
        functools.partial(reach_back, members, heads),
        "reach_back",
        [shape(rows, width)] * members,
        [VMEM] * (half + 3) + [ANY],
        [VMEM] * members,
        flops=2 * rows * HEAD_DIM * columns,
        moved=4 * block_bytes,
    )(table, *query_got, carry, earlier, own)
    crossed_got = [swap(crossed[members - 1 - d], d) if d else crossed[-1] for d in range(members)]

    gain = norm_gain.reshape(1, columns)
    last = [d for d in range(members) if d % half in (1, 2)]
    first = [d for d in range(members) if d not in last]
    first.sort(key=lambda d: (d != half, -d))
    out = None
    for chosen in (first, last):
        more = [] if out is None else [out]
        out = call(
            functools.partial(finish, chosen, members, heads, rows),
            "finish",
            shape(rows, columns, dtype=bf16),
            [VMEM] * (3 + len(chosen)) + [ANY] * len(more),
            ANY,
            [pltpu.VMEM((len(chosen), rows, width), bf16), pltpu.SemaphoreType.DMA((len(chosen),))],
            moved=2 * block_bytes,
            aliases={3 + len(chosen): 0} if more else None,
        )(table, own, gain, *[crossed_got[d] for d in chosen], *more)
    return out


def solution(mesh):
    placed = (
        P(("outer", "inner"), None),
        P(("outer", "inner"), None),
        P(("outer", "inner"), None),
        P(),
        P(),
    )
    return jax.shard_map(
        body, mesh=mesh, in_specs=placed, out_specs=P(("outer", "inner"), None), check_vma=False
    )
```

```python
import functools

import jax
import jax.numpy as jnp
from jax import lax
from jax.experimental import pallas as pl
from jax.experimental.pallas import tpu as pltpu
from jax.sharding import PartitionSpec as P

HEAD_DIM = 128
BLOCK = 16
CORES = 2
SHARE = 4
EPSILON = 1e-05
SMEM = pl.BlockSpec(memory_space=pltpu.SMEM)
VMEM = pl.BlockSpec(memory_space=pltpu.VMEM)
ANY = pl.BlockSpec(memory_space=pl.ANY)
HBM = pl.BlockSpec(memory_space=pltpu.HBM)


def columns_of(member, width):
    return pl.ds(pl.multiple_of(member * width, width), width)


def position():
    inner_count = lax.axis_size("inner")
    index = lax.axis_index("outer") * inner_count + lax.axis_index("inner")
    return index, index % (CORES * inner_count)


def heads_of(heads):
    return [slice(h * HEAD_DIM, (h + 1) * HEAD_DIM) for h in range(heads)]


def start_of(lengths, docs, token):
    begin = jnp.int32(0)
    found = jnp.int32(0)
    after = jnp.int32(jnp.iinfo(jnp.int32).max)
    for i in range(docs):
        found = jnp.where(begin <= token, begin, found)
        after = jnp.where(begin > token, jnp.minimum(begin, after), after)
        begin = begin + lengths[i] * BLOCK
    return found, after


def spread(members, width, queries, keys, values, *refs):
    half = members // CORES
    near, cross = refs[:half], refs[half]
    buffers, sems = refs[half + 1 : half + 4], refs[half + 4]
    _, me = position()

    def copies(d):
        span = columns_of(me ^ d, width)
        sources = (keys, values) if d < half else (keys, values, queries)
        return [
            pltpu.make_async_copy(source.at[:, span], buffers[i].at[d], sems.at[i, d])
            for i, source in enumerate(sources)
        ]

    order = list(reversed(range(half))) + list(range(half, members))
    for d in order:
        for copy in copies(d):
            copy.start()
    for d in order:
        for i, copy in enumerate(copies(d)):
            copy.wait()
            part = buffers[i][d].astype(jnp.float32)
            if d < half:
                near[half - 1 - d][i] = part
            else:
                cross[d - half, i] = part


def forward(half, swapped, *outs):
    for e in range(1, half):
        outs[half - 1 - e][...] = swapped[e, 0:2]


def join_queries(members, width, rows, docs, gates, lengths, queries, swapped, *refs):
    half = members // CORES
    outs, table = refs[gates:-1], refs[-1]
    index, me = position()
    for e in range(half):
        outs[half - 1 - e][0] = queries[:, columns_of(me ^ e, width)].astype(jnp.float32)
        outs[half - 1 - e][1] = swapped[e, 2]
    base = (index - me) * rows
    for j in range(members + 1):
        found, _ = start_of(lengths, docs, base + j * rows)
        table[j : j + 1, :] = jnp.full((1, HEAD_DIM), found - base, jnp.int32)
    _, after = start_of(lengths, docs, index * rows)
    table[members + 1 : members + 2, :] = jnp.full((1, HEAD_DIM), after - index * rows, jnp.int32)


def gather_states(members, heads, rows, table, *refs):
    half = members // CORES
    parts = refs[:half][::-1] + refs[half:members][::-1]
    carry_out, total_out, key_blocks, value_blocks = refs[members + 1 :]
    _, me = position()
    row = lax.broadcasted_iota(jnp.int32, (rows, HEAD_DIM), 0)
    for d in range(members):
        j = me ^ d
        kept = row >= table[pl.ds(j + 1, 1), :] - j * rows
        key, value = (parts[d][0, 0], parts[d][0, 1]) if d == half else (parts[d][0], parts[d][1])
        for span in heads_of(heads):
            key_blocks[j, :, span] = jnp.where(kept, key[:, span], 0.0).astype(jnp.bfloat16)
        value_blocks[j] = value.astype(jnp.bfloat16)
    state = [jnp.zeros((HEAD_DIM, HEAD_DIM), jnp.float32) for _ in range(heads)]
    for j in range(members):
        keep = jnp.where(table[j + 1 : j + 2, :] <= j * rows, 1.0, 0.0).astype(jnp.float32)
        for h, span in enumerate(heads_of(heads)):
            carry_out[j, h] = state[h]
            own = lax.dot_general(
                key_blocks[j, :, span],
                value_blocks[j, :, span],
                (((0,), (0,)), ((), ())),
                preferred_element_type=jnp.float32,
            )
            state[h] = keep * state[h] + own
    for h in range(heads):
        total_out[h] = state[h]


def inside(head_count, docs, rows, lengths, queries, keys, values, out):
    begin = position()[0] * rows
    row = lax.broadcasted_iota(jnp.int32, (rows, rows), 0)
    lane = lax.broadcasted_iota(jnp.int32, (rows, rows), 1)
    since = jnp.zeros((rows, rows), jnp.int32)
    start = -begin
    for i in range(docs):
        since = jnp.where(start <= row, start, since)
        start = start + lengths[i] * BLOCK
    allowed = (lane <= row) & (lane >= since)
    for span in heads_of(head_count):
        scores = lax.dot_general(
            queries[:, span], keys[:, span], (((1,), (1,)), ((), ())), preferred_element_type=jnp.float32
        )
        weights = jnp.where(allowed, scores, 0.0).astype(jnp.bfloat16)
        out[:, span] = jnp.dot(weights, values[:, span], preferred_element_type=jnp.float32)


def reach_back(members, heads, chosen, gates, table, carry, earlier, *refs):
    count = len(chosen)
    half = members // CORES
    query_parts, outs = refs[:count], refs[count + gates :]
    _, me = position()
    for n, e in enumerate(chosen):
        for side in range(CORES):
            j = me ^ e ^ (side * half)
            before = jnp.where(table[pl.ds(j, 1), :] < 0, 1.0, 0.0).astype(jnp.float32)
            for h, span in enumerate(heads_of(heads)):
                held = (carry[j, h] + before * earlier[h]).astype(jnp.bfloat16)
                query = query_parts[n][side, :, span].astype(jnp.bfloat16)
                outs[n * CORES + side][:, span] = jnp.dot(query, held, preferred_element_type=jnp.float32)


def finish(chosen, members, heads, rows, table, own, gain, *refs):
    count = len(chosen)
    parts, out = refs[:count], refs[-3]
    buffer, sems = refs[-2:]
    width = heads * HEAD_DIM
    _, me = position()
    continued = lax.broadcasted_iota(jnp.int32, (rows, HEAD_DIM), 0) < table[members + 1 : members + 2, :]
    copies = []
    for i, d in enumerate(chosen):
        columns = columns_of(me ^ d, width)
        inner = own[:, columns]
        scales = gain[:, columns]
        for span in heads_of(heads):
            mixed = inner[:, span] + jnp.where(continued, parts[i][:, span], 0.0)
            scale = lax.rsqrt(jnp.mean(mixed * mixed, axis=-1, keepdims=True) + EPSILON)
            buffer[i, :, span] = (mixed * scale * scales[:, span]).astype(jnp.bfloat16)
        copy = pltpu.make_async_copy(buffer.at[i], out.at[:, columns], sems.at[i])
        copy.start()
        copies.append(copy)
    for copy in copies:
        copy.wait()


def body(queries, keys, values, lengths, norm_gain):
    rows, columns = queries.shape
    head_count = columns // HEAD_DIM
    docs = lengths.shape[0]
    inner_count = lax.axis_size("inner")
    devices = lax.axis_size("outer") * inner_count
    members = CORES * inner_count
    half = inner_count
    planes = devices // members
    heads = head_count // members
    width = heads * HEAD_DIM
    reach = -(-(devices // SHARE) // members)
    everyone = ("outer", "inner")
    index = lax.axis_index("outer") * inner_count + lax.axis_index("inner")
    me = index % members
    base = (index - me) * rows
    f32, bf16 = jnp.float32, jnp.bfloat16

    def call(kernel, name, out_shape, in_specs, out_specs, scratch=(), flops=0, moved=0, aliases=None):
        return pl.pallas_call(
            kernel,
            out_shape=out_shape,
            in_specs=in_specs,
            out_specs=out_specs,
            scratch_shapes=scratch,
            compiler_params=pltpu.CompilerParams(vmem_limit_bytes=16 * 1024 * 1024),
            cost_estimate=pl.CostEstimate(flops=flops, bytes_accessed=moved, transcendentals=0),
            input_output_aliases=aliases or {},
            name=name,
        )

    def shape(*sizes, dtype=f32):
        return jax.ShapeDtypeStruct(sizes, dtype)

    def swap(part, d):
        pairs = [(g, g - g % members + (g % members ^ d)) for g in range(devices)]
        return lax.ppermute(part, everyone, pairs)

    downward = list(reversed(range(half)))
    block_bytes = rows * columns * 4
    parts = call(
        functools.partial(spread, members, width),
        "spread",
        [shape(2, rows, width)] * half + [shape(half, 3, rows, width)],
        [HBM, HBM, HBM],
        [VMEM] * (half + 1),
        [pltpu.VMEM((members, rows, width), bf16)] * 3 + [pltpu.SemaphoreType.DMA((3, members))],
    )(*[pltpu.with_memory_space_constraint(x, pltpu.HBM) for x in (queries, keys, values)])
    near_got = [swap(part, e) if e else part for e, part in zip(downward, parts)]
    swapped = swap(parts[half], half)
    far_parts = call(
        functools.partial(forward, half),
        "forward",
        [shape(2, rows, width)] * (half - 1),
        [VMEM],
        [VMEM] * (half - 1),
        moved=2 * block_bytes,
    )(swapped)
    far_got = [swap(part, e) for e, part in zip(downward, far_parts)] + [swapped]
    gates = near_got[:-1]
    *query_parts, table = call(
        functools.partial(join_queries, members, width, rows, docs, len(gates)),
        "join_queries",
        [shape(CORES, rows, width)] * half + [shape(members + 2, HEAD_DIM, dtype=jnp.int32)],
        [SMEM, VMEM, VMEM] + [ANY] * len(gates),
        [VMEM] * (half + 1),
        moved=2 * block_bytes,
    )(lengths, queries, swapped, *gates)
    query_got = [swap(part, e) if e else part for e, part in zip(downward, query_parts)]

    own = call(
        functools.partial(inside, head_count, docs, rows),
        "inside",
        shape(rows, columns),
        [SMEM, VMEM, VMEM, VMEM],
        VMEM,
        flops=4 * rows * rows * columns,
        moved=3 * block_bytes,
    )(lengths, queries, keys, values)

    carry, total = call(
        functools.partial(gather_states, members, heads, rows),
        "gather_states",
        [shape(members, heads, HEAD_DIM, HEAD_DIM), shape(heads, HEAD_DIM, HEAD_DIM)],
        [VMEM] * (members + 1) + [ANY],
        [VMEM] * 2,
        [pltpu.VMEM((members, rows, width), bf16)] * 2,
        flops=2 * rows * HEAD_DIM * columns,
        moved=4 * block_bytes,
    )(table, *near_got, *far_got, own)
    up = [(g, g + members) for g in range(devices - members)]
    moving = lax.ppermute(total, everyone, up)
    earlier = moving
    if reach > 1:
        starts = BLOCK * (jnp.cumsum(lengths) - lengths)
        opens = jnp.max(jnp.where(starts <= base, starts, 0))
        for k in range(2, min(reach, planes - 1) + 1):
            moving = lax.ppermute(moving, everyone, up)
            earlier = earlier + jnp.where(opens < base - (k - 1) * members * rows, moving, 0.0)
    crossed_got = {}
    late = [e for e in downward if e in (1, 2)]
    soon = [e for e in downward if e not in late]
    for chosen, gates in ((soon, []), (late, [])):
        crossed = call(
            functools.partial(reach_back, members, heads, chosen, len(gates)),
            "reach_back",
            [shape(rows, width)] * (CORES * len(chosen)),
            [VMEM] * (len(chosen) + 3) + [ANY] * len(gates),
            [VMEM] * (CORES * len(chosen)),
            flops=2 * rows * HEAD_DIM * width * CORES * len(chosen),
            moved=2 * block_bytes,
        )(table, carry, earlier, *[query_got[half - 1 - e] for e in chosen], *gates)
        for n, e in enumerate(chosen):
            for side in range(CORES):
                d = e ^ (side * half)
                part = crossed[n * CORES + side]
                crossed_got[d] = swap(part, d) if d else part

    gain = norm_gain.reshape(1, columns)
    out = None
    groups = [[e ^ (side * half) for e in soon for side in range(CORES)]]
    groups += [[e ^ (side * half) for e in late for side in range(CORES)]]
    for chosen in groups:
        more = [] if out is None else [out]
        out = call(
            functools.partial(finish, chosen, members, heads, rows),
            "finish",
            shape(rows, columns, dtype=bf16),
            [VMEM] * (3 + len(chosen)) + [ANY] * len(more),
            ANY,
            [pltpu.VMEM((len(chosen), rows, width), bf16), pltpu.SemaphoreType.DMA((len(chosen),))],
            moved=2 * block_bytes,
            aliases={3 + len(chosen): 0} if more else None,
        )(table, own, gain, *[crossed_got[d] for d in chosen], *more)
    return out


def solution(mesh):
    placed = (
        P(("outer", "inner"), None),
        P(("outer", "inner"), None),
        P(("outer", "inner"), None),
        P(),
        P(),
    )
    return jax.shard_map(
        body, mesh=mesh, in_specs=placed, out_specs=P(("outer", "inner"), None), check_vma=False
    )
```

```python
import functools

import jax
import jax.numpy as jnp
from jax import lax
from jax.experimental import pallas as pl
from jax.experimental.pallas import tpu as pltpu
from jax.sharding import PartitionSpec as P

HEAD_DIM = 128
BLOCK = 16
CORES = 2
SHARE = 4
EPSILON = 1e-05
SMEM = pl.BlockSpec(memory_space=pltpu.SMEM)
VMEM = pl.BlockSpec(memory_space=pltpu.VMEM)
ANY = pl.BlockSpec(memory_space=pl.ANY)
HBM = pl.BlockSpec(memory_space=pltpu.HBM)


def columns_of(member, width):
    return pl.ds(pl.multiple_of(member * width, width), width)


def position():
    inner_count = lax.axis_size("inner")
    index = lax.axis_index("outer") * inner_count + lax.axis_index("inner")
    return index, index % (CORES * inner_count)


def heads_of(heads):
    return [slice(h * HEAD_DIM, (h + 1) * HEAD_DIM) for h in range(heads)]


def start_of(lengths, docs, token):
    begin = jnp.int32(0)
    found = jnp.int32(0)
    after = jnp.int32(jnp.iinfo(jnp.int32).max)
    for i in range(docs):
        found = jnp.where(begin <= token, begin, found)
        after = jnp.where(begin > token, jnp.minimum(begin, after), after)
        begin = begin + lengths[i] * BLOCK
    return found, after


def spread(members, width, queries, keys, values, *refs):
    half = members // CORES
    near, cross = refs[:half], refs[half]
    buffers, sems = refs[half + 1 : half + 4], refs[half + 4]
    _, me = position()

    def copies(d):
        span = columns_of(me ^ d, width)
        sources = (keys, values) if d < half else (keys, values, queries)
        return [
            pltpu.make_async_copy(source.at[:, span], buffers[i].at[d], sems.at[i, d])
            for i, source in enumerate(sources)
        ]

    order = list(reversed(range(half))) + list(range(half, members))
    for d in order:
        for copy in copies(d):
            copy.start()
    for d in order:
        for i, copy in enumerate(copies(d)):
            copy.wait()
            part = buffers[i][d].astype(jnp.float32)
            if d < half:
                near[half - 1 - d][i] = part
            else:
                cross[d - half, i] = part


def forward(half, swapped, *outs):
    for e in range(1, half):
        outs[half - 1 - e][...] = swapped[e, 0:2]


def join_queries(members, width, rows, docs, gates, lengths, queries, swapped, *refs):
    half = members // CORES
    outs, table = refs[gates:-1], refs[-1]
    index, me = position()
    for e in range(half):
        outs[half - 1 - e][0] = queries[:, columns_of(me ^ e, width)].astype(jnp.float32)
        outs[half - 1 - e][1] = swapped[e, 2]
    base = (index - me) * rows
    for j in range(members + 1):
        found, _ = start_of(lengths, docs, base + j * rows)
        table[j : j + 1, :] = jnp.full((1, HEAD_DIM), found - base, jnp.int32)
    _, after = start_of(lengths, docs, index * rows)
    table[members + 1 : members + 2, :] = jnp.full((1, HEAD_DIM), after - index * rows, jnp.int32)


def gather_states(members, heads, rows, table, *refs):
    half = members // CORES
    parts = refs[:half][::-1] + refs[half:members][::-1]
    carry_out, total_out, key_blocks, value_blocks = refs[members + 1 :]
    _, me = position()
    row = lax.broadcasted_iota(jnp.int32, (rows, HEAD_DIM), 0)
    for d in range(members):
        j = me ^ d
        kept = row >= table[pl.ds(j + 1, 1), :] - j * rows
        key, value = (parts[d][0, 0], parts[d][0, 1]) if d == half else (parts[d][0], parts[d][1])
        for span in heads_of(heads):
            key_blocks[j, :, span] = jnp.where(kept, key[:, span], 0.0).astype(jnp.bfloat16)
        value_blocks[j] = value.astype(jnp.bfloat16)
    state = [jnp.zeros((HEAD_DIM, HEAD_DIM), jnp.float32) for _ in range(heads)]
    for j in range(members):
        keep = jnp.where(table[j + 1 : j + 2, :] <= j * rows, 1.0, 0.0).astype(jnp.float32)
        for h, span in enumerate(heads_of(heads)):
            carry_out[j, h] = state[h]
            own = lax.dot_general(
                key_blocks[j, :, span],
                value_blocks[j, :, span],
                (((0,), (0,)), ((), ())),
                preferred_element_type=jnp.float32,
            )
            state[h] = keep * state[h] + own
    for h in range(heads):
        total_out[h] = state[h]


def inside(head_count, docs, rows, lengths, queries, keys, values, out):
    begin = position()[0] * rows
    row = lax.broadcasted_iota(jnp.int32, (rows, rows), 0)
    lane = lax.broadcasted_iota(jnp.int32, (rows, rows), 1)
    since = jnp.zeros((rows, rows), jnp.int32)
    start = -begin
    for i in range(docs):
        since = jnp.where(start <= row, start, since)
        start = start + lengths[i] * BLOCK
    allowed = (lane <= row) & (lane >= since)
    for span in heads_of(head_count):
        scores = lax.dot_general(
            queries[:, span], keys[:, span], (((1,), (1,)), ((), ())), preferred_element_type=jnp.float32
        )
        weights = jnp.where(allowed, scores, 0.0).astype(jnp.bfloat16)
        out[:, span] = jnp.dot(weights, values[:, span], preferred_element_type=jnp.float32)


def reach_back(members, heads, chosen, gates, table, carry, earlier, *refs):
    count = len(chosen)
    half = members // CORES
    query_parts, outs = refs[:count], refs[count + gates :]
    _, me = position()
    for n, e in enumerate(chosen):
        for side in range(CORES):
            j = me ^ e ^ (side * half)
            before = jnp.where(table[pl.ds(j, 1), :] < 0, 1.0, 0.0).astype(jnp.float32)
            for h, span in enumerate(heads_of(heads)):
                held = (carry[j, h] + before * earlier[h]).astype(jnp.bfloat16)
                query = query_parts[n][side, :, span].astype(jnp.bfloat16)
                outs[n * CORES + side][:, span] = jnp.dot(query, held, preferred_element_type=jnp.float32)


def finish(chosen, members, heads, rows, table, own, gain, *refs):
    count = len(chosen)
    parts, out = refs[:count], refs[-3]
    buffer, sems = refs[-2:]
    width = heads * HEAD_DIM
    _, me = position()
    continued = lax.broadcasted_iota(jnp.int32, (rows, HEAD_DIM), 0) < table[members + 1 : members + 2, :]
    copies = []
    for i, d in enumerate(chosen):
        columns = columns_of(me ^ d, width)
        inner = own[:, columns]
        scales = gain[:, columns]
        for span in heads_of(heads):
            mixed = inner[:, span] + jnp.where(continued, parts[i][:, span], 0.0)
            scale = lax.rsqrt(jnp.mean(mixed * mixed, axis=-1, keepdims=True) + EPSILON)
            buffer[i, :, span] = (mixed * scale * scales[:, span]).astype(jnp.bfloat16)
        copy = pltpu.make_async_copy(buffer.at[i], out.at[:, columns], sems.at[i])
        copy.start()
        copies.append(copy)
    for copy in copies:
        copy.wait()


def body(queries, keys, values, lengths, norm_gain):
    rows, columns = queries.shape
    head_count = columns // HEAD_DIM
    docs = lengths.shape[0]
    inner_count = lax.axis_size("inner")
    devices = lax.axis_size("outer") * inner_count
    members = CORES * inner_count
    half = inner_count
    planes = devices // members
    heads = head_count // members
    width = heads * HEAD_DIM
    reach = -(-(devices // SHARE) // members)
    everyone = ("outer", "inner")
    index = lax.axis_index("outer") * inner_count + lax.axis_index("inner")
    me = index % members
    base = (index - me) * rows
    f32, bf16 = jnp.float32, jnp.bfloat16

    def call(kernel, name, out_shape, in_specs, out_specs, scratch=(), flops=0, moved=0, aliases=None):
        return pl.pallas_call(
            kernel,
            out_shape=out_shape,
            in_specs=in_specs,
            out_specs=out_specs,
            scratch_shapes=scratch,
            compiler_params=pltpu.CompilerParams(vmem_limit_bytes=16 * 1024 * 1024),
            cost_estimate=pl.CostEstimate(flops=flops, bytes_accessed=moved, transcendentals=0),
            input_output_aliases=aliases or {},
            name=name,
        )

    def shape(*sizes, dtype=f32):
        return jax.ShapeDtypeStruct(sizes, dtype)

    def swap(part, d):
        pairs = [(g, g - g % members + (g % members ^ d)) for g in range(devices)]
        return lax.ppermute(part, everyone, pairs)

    downward = list(reversed(range(half)))
    block_bytes = rows * columns * 4
    parts = call(
        functools.partial(spread, members, width),
        "spread",
        [shape(2, rows, width)] * half + [shape(half, 3, rows, width)],
        [HBM, HBM, HBM],
        [VMEM] * (half + 1),
        [pltpu.VMEM((members, rows, width), bf16)] * 3 + [pltpu.SemaphoreType.DMA((3, members))],
    )(*[pltpu.with_memory_space_constraint(x, pltpu.HBM) for x in (queries, keys, values)])
    near_got = [swap(part, e) if e else part for e, part in zip(downward, parts)]
    swapped = swap(parts[half], half)
    far_parts = call(
        functools.partial(forward, half),
        "forward",
        [shape(2, rows, width)] * (half - 1),
        [VMEM],
        [VMEM] * (half - 1),
        moved=2 * block_bytes,
    )(swapped)
    far_got = [swap(part, e) for e, part in zip(downward, far_parts)] + [swapped]
    gates = near_got[:-1]
    *query_parts, table = call(
        functools.partial(join_queries, members, width, rows, docs, len(gates)),
        "join_queries",
        [shape(CORES, rows, width)] * half + [shape(members + 2, HEAD_DIM, dtype=jnp.int32)],
        [SMEM, VMEM, VMEM] + [ANY] * len(gates),
        [VMEM] * (half + 1),
        moved=2 * block_bytes,
    )(lengths, queries, swapped, *gates)
    query_got = [swap(part, e) if e else part for e, part in zip(downward, query_parts)]

    own = call(
        functools.partial(inside, head_count, docs, rows),
        "inside",
        shape(rows, columns),
        [SMEM, VMEM, VMEM, VMEM],
        VMEM,
        flops=4 * rows * rows * columns,
        moved=3 * block_bytes,
    )(lengths, queries, keys, values)

    carry, total = call(
        functools.partial(gather_states, members, heads, rows),
        "gather_states",
        [shape(members, heads, HEAD_DIM, HEAD_DIM), shape(heads, HEAD_DIM, HEAD_DIM)],
        [VMEM] * (members + 1) + [ANY],
        [VMEM] * 2,
        [pltpu.VMEM((members, rows, width), bf16)] * 2,
        flops=2 * rows * HEAD_DIM * columns,
        moved=4 * block_bytes,
    )(table, *near_got, *far_got, own)
    up = [(g, g + members) for g in range(devices - members)]
    moving = lax.ppermute(total, everyone, up)
    earlier = moving
    if reach > 1:
        starts = BLOCK * (jnp.cumsum(lengths) - lengths)
        opens = jnp.max(jnp.where(starts <= base, starts, 0))
        for k in range(2, min(reach, planes - 1) + 1):
            moving = lax.ppermute(moving, everyone, up)
            earlier = earlier + jnp.where(opens < base - (k - 1) * members * rows, moving, 0.0)
    crossed_got = {}
    late = [e for e in downward if e in (0, 1, 2)]
    soon = [e for e in downward if e not in late]
    gates = []
    for chosen in (soon, late):
        crossed = call(
            functools.partial(reach_back, members, heads, chosen, len(gates)),
            "reach_back",
            [shape(rows, width)] * (CORES * len(chosen)),
            [VMEM] * (len(chosen) + 3) + [ANY] * len(gates),
            [VMEM] * (CORES * len(chosen)),
            flops=2 * rows * HEAD_DIM * width * CORES * len(chosen),
            moved=2 * block_bytes,
        )(table, carry, earlier, *[query_got[half - 1 - e] for e in chosen], *gates)
        for n, e in enumerate(chosen):
            for side in range(CORES):
                d = e ^ (side * half)
                part = crossed[n * CORES + side]
                crossed_got[d] = swap(part, d) if d else part
        gates = crossed[:1]

    gain = norm_gain.reshape(1, columns)
    out = None
    groups = [[0] + [e ^ (side * half) for e in soon for side in range(CORES)]]
    groups += [[half] + [e ^ (side * half) for e in late if e for side in range(CORES)]]
    for chosen in groups:
        more = [] if out is None else [out]
        out = call(
            functools.partial(finish, chosen, members, heads, rows),
            "finish",
            shape(rows, columns, dtype=bf16),
            [VMEM] * (3 + len(chosen)) + [ANY] * len(more),
            ANY,
            [pltpu.VMEM((len(chosen), rows, width), bf16), pltpu.SemaphoreType.DMA((len(chosen),))],
            moved=2 * block_bytes,
            aliases={3 + len(chosen): 0} if more else None,
        )(table, own, gain, *[crossed_got[d] for d in chosen], *more)
    return out


def solution(mesh):
    placed = (
        P(("outer", "inner"), None),
        P(("outer", "inner"), None),
        P(("outer", "inner"), None),
        P(),
        P(),
    )
    return jax.shard_map(
        body, mesh=mesh, in_specs=placed, out_specs=P(("outer", "inner"), None), check_vma=False
    )
```

```python
import functools

import jax
import jax.numpy as jnp
from jax import lax
from jax.experimental import pallas as pl
from jax.experimental.pallas import tpu as pltpu
from jax.sharding import PartitionSpec as P

HEAD_DIM = 128
BLOCK = 16
CORES = 2
SHARE = 4
EPSILON = 1e-05
SMEM = pl.BlockSpec(memory_space=pltpu.SMEM)
VMEM = pl.BlockSpec(memory_space=pltpu.VMEM)
ANY = pl.BlockSpec(memory_space=pl.ANY)
HBM = pl.BlockSpec(memory_space=pltpu.HBM)


def columns_of(member, width):
    return pl.ds(pl.multiple_of(member * width, width), width)


def position():
    inner_count = lax.axis_size("inner")
    index = lax.axis_index("outer") * inner_count + lax.axis_index("inner")
    return index, index % (CORES * inner_count)


def heads_of(heads):
    return [slice(h * HEAD_DIM, (h + 1) * HEAD_DIM) for h in range(heads)]


def start_of(lengths, docs, token):
    begin = jnp.int32(0)
    found = jnp.int32(0)
    after = jnp.int32(jnp.iinfo(jnp.int32).max)
    for i in range(docs):
        found = jnp.where(begin <= token, begin, found)
        after = jnp.where(begin > token, jnp.minimum(begin, after), after)
        begin = begin + lengths[i] * BLOCK
    return found, after


def spread(members, width, queries, keys, values, *refs):
    half = members // CORES
    near, cross = refs[:half], refs[half]
    buffers, sems = refs[half + 1 : half + 4], refs[half + 4]
    _, me = position()

    def copies(d):
        span = columns_of(me ^ d, width)
        sources = (keys, values) if d < half else (keys, values, queries)
        return [
            pltpu.make_async_copy(source.at[:, span], buffers[i].at[d], sems.at[i, d])
            for i, source in enumerate(sources)
        ]

    order = list(reversed(range(half))) + list(range(half, members))
    for d in order:
        for copy in copies(d):
            copy.start()
    for d in order:
        for i, copy in enumerate(copies(d)):
            copy.wait()
            part = buffers[i][d].astype(jnp.float32)
            if d < half:
                near[half - 1 - d][i] = part
            else:
                cross[d - half, i] = part


def forward(half, swapped, *outs):
    for e in range(1, half):
        outs[half - 1 - e][...] = swapped[e, 0:2]


def join_queries(members, width, rows, docs, gates, lengths, queries, swapped, *refs):
    half = members // CORES
    outs, table = refs[gates:-1], refs[-1]
    index, me = position()
    for e in range(half):
        outs[half - 1 - e][0] = queries[:, columns_of(me ^ e, width)].astype(jnp.float32)
        outs[half - 1 - e][1] = swapped[e, 2]
    base = (index - me) * rows
    for j in range(members + 1):
        found, _ = start_of(lengths, docs, base + j * rows)
        table[j : j + 1, :] = jnp.full((1, HEAD_DIM), found - base, jnp.int32)
    _, after = start_of(lengths, docs, index * rows)
    table[members + 1 : members + 2, :] = jnp.full((1, HEAD_DIM), after - index * rows, jnp.int32)


def gather_states(members, heads, rows, table, *refs):
    half = members // CORES
    parts = refs[:half][::-1] + refs[half:members][::-1]
    carry_out, total_out, key_blocks, value_blocks = refs[members + 1 :]
    _, me = position()
    row = lax.broadcasted_iota(jnp.int32, (rows, HEAD_DIM), 0)
    for d in range(members):
        j = me ^ d
        kept = row >= table[pl.ds(j + 1, 1), :] - j * rows
        key, value = (parts[d][0, 0], parts[d][0, 1]) if d == half else (parts[d][0], parts[d][1])
        for span in heads_of(heads):
            key_blocks[j, :, span] = jnp.where(kept, key[:, span], 0.0).astype(jnp.bfloat16)
        value_blocks[j] = value.astype(jnp.bfloat16)
    state = [jnp.zeros((HEAD_DIM, HEAD_DIM), jnp.float32) for _ in range(heads)]
    for j in range(members):
        keep = jnp.where(table[j + 1 : j + 2, :] <= j * rows, 1.0, 0.0).astype(jnp.float32)
        for h, span in enumerate(heads_of(heads)):
            carry_out[j, h] = state[h]
            own = lax.dot_general(
                key_blocks[j, :, span],
                value_blocks[j, :, span],
                (((0,), (0,)), ((), ())),
                preferred_element_type=jnp.float32,
            )
            state[h] = keep * state[h] + own
    for h in range(heads):
        total_out[h] = state[h]


def inside(head_count, docs, rows, lengths, queries, keys, values, out):
    begin = position()[0] * rows
    row = lax.broadcasted_iota(jnp.int32, (rows, rows), 0)
    lane = lax.broadcasted_iota(jnp.int32, (rows, rows), 1)
    since = jnp.zeros((rows, rows), jnp.int32)
    start = -begin
    for i in range(docs):
        since = jnp.where(start <= row, start, since)
        start = start + lengths[i] * BLOCK
    allowed = (lane <= row) & (lane >= since)
    for span in heads_of(head_count):
        scores = lax.dot_general(
            queries[:, span], keys[:, span], (((1,), (1,)), ((), ())), preferred_element_type=jnp.float32
        )
        weights = jnp.where(allowed, scores, 0.0).astype(jnp.bfloat16)
        out[:, span] = jnp.dot(weights, values[:, span], preferred_element_type=jnp.float32)


def reach_back(members, heads, chosen, gates, table, carry, earlier, *refs):
    count = len(chosen)
    half = members // CORES
    query_parts, outs = refs[:count], refs[count + gates :]
    _, me = position()
    for n, e in enumerate(chosen):
        for side in range(CORES):
            j = me ^ e ^ (side * half)
            before = jnp.where(table[pl.ds(j, 1), :] < 0, 1.0, 0.0).astype(jnp.float32)
            for h, span in enumerate(heads_of(heads)):
                held = (carry[j, h] + before * earlier[h]).astype(jnp.bfloat16)
                query = query_parts[n][side, :, span].astype(jnp.bfloat16)
                outs[n * CORES + side][:, span] = jnp.dot(query, held, preferred_element_type=jnp.float32)


def finish(chosen, members, heads, rows, table, own, gain, *refs):
    count = len(chosen)
    parts, out = refs[:count], refs[-3]
    buffer, sems = refs[-2:]
    width = heads * HEAD_DIM
    _, me = position()
    continued = lax.broadcasted_iota(jnp.int32, (rows, HEAD_DIM), 0) < table[members + 1 : members + 2, :]
    copies = []
    for i, d in enumerate(chosen):
        columns = columns_of(me ^ d, width)
        inner = own[:, columns]
        scales = gain[:, columns]
        for span in heads_of(heads):
            mixed = inner[:, span] + jnp.where(continued, parts[i][:, span], 0.0)
            scale = lax.rsqrt(jnp.mean(mixed * mixed, axis=-1, keepdims=True) + EPSILON)
            buffer[i, :, span] = (mixed * scale * scales[:, span]).astype(jnp.bfloat16)
        copy = pltpu.make_async_copy(buffer.at[i], out.at[:, columns], sems.at[i])
        copy.start()
        copies.append(copy)
    for copy in copies:
        copy.wait()


def body(queries, keys, values, lengths, norm_gain):
    rows, columns = queries.shape
    head_count = columns // HEAD_DIM
    docs = lengths.shape[0]
    inner_count = lax.axis_size("inner")
    devices = lax.axis_size("outer") * inner_count
    members = CORES * inner_count
    half = inner_count
    planes = devices // members
    heads = head_count // members
    width = heads * HEAD_DIM
    reach = -(-(devices // SHARE) // members)
    everyone = ("outer", "inner")
    index = lax.axis_index("outer") * inner_count + lax.axis_index("inner")
    me = index % members
    base = (index - me) * rows
    f32, bf16 = jnp.float32, jnp.bfloat16

    def call(kernel, name, out_shape, in_specs, out_specs, scratch=(), flops=0, moved=0, aliases=None):
        return pl.pallas_call(
            kernel,
            out_shape=out_shape,
            in_specs=in_specs,
            out_specs=out_specs,
            scratch_shapes=scratch,
            compiler_params=pltpu.CompilerParams(vmem_limit_bytes=16 * 1024 * 1024),
            cost_estimate=pl.CostEstimate(flops=flops, bytes_accessed=moved, transcendentals=0),
            input_output_aliases=aliases or {},
            name=name,
        )

    def shape(*sizes, dtype=f32):
        return jax.ShapeDtypeStruct(sizes, dtype)

    def swap(part, d):
        pairs = [(g, g - g % members + (g % members ^ d)) for g in range(devices)]
        return lax.ppermute(part, everyone, pairs)

    downward = list(reversed(range(half)))
    block_bytes = rows * columns * 4
    parts = call(
        functools.partial(spread, members, width),
        "spread",
        [shape(2, rows, width)] * half + [shape(half, 3, rows, width)],
        [HBM, HBM, HBM],
        [VMEM] * (half + 1),
        [pltpu.VMEM((members, rows, width), bf16)] * 3 + [pltpu.SemaphoreType.DMA((3, members))],
    )(*[pltpu.with_memory_space_constraint(x, pltpu.HBM) for x in (queries, keys, values)])
    near_got = [swap(part, e) if e else part for e, part in zip(downward, parts)]
    swapped = swap(parts[half], half)
    far_parts = call(
        functools.partial(forward, half),
        "forward",
        [shape(2, rows, width)] * (half - 1),
        [VMEM],
        [VMEM] * (half - 1),
        moved=2 * block_bytes,
    )(swapped)
    far_got = [swap(part, e) for e, part in zip(downward, far_parts)] + [swapped]
    gates = [*near_got[:-1], far_got[0]]
    *query_parts, table = call(
        functools.partial(join_queries, members, width, rows, docs, len(gates)),
        "join_queries",
        [shape(CORES, rows, width)] * half + [shape(members + 2, HEAD_DIM, dtype=jnp.int32)],
        [SMEM, VMEM, VMEM] + [ANY] * len(gates),
        [VMEM] * (half + 1),
        moved=2 * block_bytes,
    )(lengths, queries, swapped, *gates)
    query_got = [swap(part, e) if e else part for e, part in zip(downward, query_parts)]

    own = call(
        functools.partial(inside, head_count, docs, rows),
        "inside",
        shape(rows, columns),
        [SMEM, VMEM, VMEM, VMEM],
        VMEM,
        flops=4 * rows * rows * columns,
        moved=3 * block_bytes,
    )(lengths, queries, keys, values)

    carry, total = call(
        functools.partial(gather_states, members, heads, rows),
        "gather_states",
        [shape(members, heads, HEAD_DIM, HEAD_DIM), shape(heads, HEAD_DIM, HEAD_DIM)],
        [VMEM] * (members + 1) + [ANY],
        [VMEM] * 2,
        [pltpu.VMEM((members, rows, width), bf16)] * 2,
        flops=2 * rows * HEAD_DIM * columns,
        moved=4 * block_bytes,
    )(table, *near_got, *far_got, own)
    up = [(g, g + members) for g in range(devices - members)]
    moving = lax.ppermute(total, everyone, up)
    earlier = moving
    if reach > 1:
        starts = BLOCK * (jnp.cumsum(lengths) - lengths)
        opens = jnp.max(jnp.where(starts <= base, starts, 0))
        for k in range(2, min(reach, planes - 1) + 1):
            moving = lax.ppermute(moving, everyone, up)
            earlier = earlier + jnp.where(opens < base - (k - 1) * members * rows, moving, 0.0)
    crossed_got = {}
    late = [e for e in (1, 2, 0) if e < half]
    soon = [e for e in downward if e not in late]
    gates = []
    for chosen in (soon, late):
        crossed = call(
            functools.partial(reach_back, members, heads, chosen, len(gates)),
            "reach_back",
            [shape(rows, width)] * (CORES * len(chosen)),
            [VMEM] * (len(chosen) + 3) + [ANY] * len(gates),
            [VMEM] * (CORES * len(chosen)),
            flops=2 * rows * HEAD_DIM * width * CORES * len(chosen),
            moved=2 * block_bytes,
        )(table, carry, earlier, *[query_got[half - 1 - e] for e in chosen], *gates)
        for n, e in enumerate(chosen):
            for side in range(CORES):
                d = e ^ (side * half)
                part = crossed[n * CORES + side]
                crossed_got[d] = swap(part, d) if d else part
        gates = crossed[:1]

    gain = norm_gain.reshape(1, columns)
    out = None
    groups = [[0] + [e ^ (side * half) for e in soon for side in range(CORES)]]
    groups += [[e ^ (side * half) for side in range(CORES) for e in late if e] + [half]]
    for chosen in groups:
        more = [] if out is None else [out]
        out = call(
            functools.partial(finish, chosen, members, heads, rows),
            "finish",
            shape(rows, columns, dtype=bf16),
            [VMEM] * (3 + len(chosen)) + [ANY] * len(more),
            ANY,
            [pltpu.VMEM((len(chosen), rows, width), bf16), pltpu.SemaphoreType.DMA((len(chosen),))],
            moved=2 * block_bytes,
            aliases={3 + len(chosen): 0} if more else None,
        )(table, own, gain, *[crossed_got[d] for d in chosen], *more)
    return out


def solution(mesh):
    placed = (
        P(("outer", "inner"), None),
        P(("outer", "inner"), None),
        P(("outer", "inner"), None),
        P(),
        P(),
    )
    return jax.shard_map(
        body, mesh=mesh, in_specs=placed, out_specs=P(("outer", "inner"), None), check_vma=False
    )
```

```python
import functools

import jax
import jax.numpy as jnp
from jax import lax
from jax.experimental import pallas as pl
from jax.experimental.pallas import tpu as pltpu
from jax.sharding import PartitionSpec as P

HEAD_DIM = 128
BLOCK = 16
CORES = 2
SHARE = 4
EPSILON = 1e-05
SMEM = pl.BlockSpec(memory_space=pltpu.SMEM)
VMEM = pl.BlockSpec(memory_space=pltpu.VMEM)
ANY = pl.BlockSpec(memory_space=pl.ANY)
HBM = pl.BlockSpec(memory_space=pltpu.HBM)


def columns_of(member, width):
    return pl.ds(pl.multiple_of(member * width, width), width)


def position():
    inner_count = lax.axis_size("inner")
    index = lax.axis_index("outer") * inner_count + lax.axis_index("inner")
    return index, index % (CORES * inner_count)


def ranked(count, *first):
    first = [e for e in first if e < count]
    return [e for e in range(count) if e not in first and e > max(first)] + first


def heads_of(heads):
    return [slice(h * HEAD_DIM, (h + 1) * HEAD_DIM) for h in range(heads)]


def start_of(lengths, docs, token):
    begin = jnp.int32(0)
    found = jnp.int32(0)
    after = jnp.int32(jnp.iinfo(jnp.int32).max)
    for i in range(docs):
        found = jnp.where(begin <= token, begin, found)
        after = jnp.where(begin > token, jnp.minimum(begin, after), after)
        begin = begin + lengths[i] * BLOCK
    return found, after


def spread(members, width, near_order, queries, keys, values, *refs):
    half = members // CORES
    near, cross = refs[:half], refs[half]
    buffers, sems = refs[half + 1 : half + 4], refs[half + 4]
    _, me = position()

    def copies(d):
        span = columns_of(me ^ d, width)
        sources = (keys, values) if d < half else (keys, values, queries)
        return [
            pltpu.make_async_copy(source.at[:, span], buffers[i].at[d], sems.at[i, d])
            for i, source in enumerate(sources)
        ]

    order = near_order + list(range(half, members))
    for d in order:
        for copy in copies(d):
            copy.start()
    for d in order:
        for i, copy in enumerate(copies(d)):
            copy.wait()
            part = buffers[i][d].astype(jnp.float32)
            if d < half:
                near[near_order.index(d)][i] = part
            else:
                cross[d - half, i] = part


def forward(order, swapped, *outs):
    for n, e in enumerate(order):
        outs[n][...] = swapped[e, 0:2]


def join_queries(members, width, order, rows, docs, gates, lengths, queries, swapped, *refs):
    half = members // CORES
    outs, table = refs[gates:-1], refs[-1]
    index, me = position()
    for n, e in enumerate(order):
        outs[n][0] = queries[:, columns_of(me ^ e, width)].astype(jnp.float32)
        outs[n][1] = swapped[e, 2]
    base = (index - me) * rows
    for j in range(members + 1):
        found, _ = start_of(lengths, docs, base + j * rows)
        table[j : j + 1, :] = jnp.full((1, HEAD_DIM), found - base, jnp.int32)
    _, after = start_of(lengths, docs, index * rows)
    table[members + 1 : members + 2, :] = jnp.full((1, HEAD_DIM), after - index * rows, jnp.int32)


def gather_states(members, heads, rows, order, table, *refs):
    half = members // CORES
    parts = dict(zip(order, refs))
    carry_out, total_out, key_blocks, value_blocks = refs[members + 1 :]
    _, me = position()
    row = lax.broadcasted_iota(jnp.int32, (rows, HEAD_DIM), 0)
    for d in range(members):
        j = me ^ d
        kept = row >= table[pl.ds(j + 1, 1), :] - j * rows
        key, value = (parts[d][0, 0], parts[d][0, 1]) if d == half else (parts[d][0], parts[d][1])
        for span in heads_of(heads):
            key_blocks[j, :, span] = jnp.where(kept, key[:, span], 0.0).astype(jnp.bfloat16)
        value_blocks[j] = value.astype(jnp.bfloat16)
    state = [jnp.zeros((HEAD_DIM, HEAD_DIM), jnp.float32) for _ in range(heads)]
    for j in range(members):
        keep = jnp.where(table[j + 1 : j + 2, :] <= j * rows, 1.0, 0.0).astype(jnp.float32)
        for h, span in enumerate(heads_of(heads)):
            carry_out[j, h] = state[h]
            own = lax.dot_general(
                key_blocks[j, :, span],
                value_blocks[j, :, span],
                (((0,), (0,)), ((), ())),
                preferred_element_type=jnp.float32,
            )
            state[h] = keep * state[h] + own
    for h in range(heads):
        total_out[h] = state[h]


def inside(head_count, docs, rows, lengths, queries, keys, values, out):
    begin = position()[0] * rows
    row = lax.broadcasted_iota(jnp.int32, (rows, rows), 0)
    lane = lax.broadcasted_iota(jnp.int32, (rows, rows), 1)
    since = jnp.zeros((rows, rows), jnp.int32)
    start = -begin
    for i in range(docs):
        since = jnp.where(start <= row, start, since)
        start = start + lengths[i] * BLOCK
    allowed = (lane <= row) & (lane >= since)
    for span in heads_of(head_count):
        scores = lax.dot_general(
            queries[:, span], keys[:, span], (((1,), (1,)), ((), ())), preferred_element_type=jnp.float32
        )
        weights = jnp.where(allowed, scores, 0.0).astype(jnp.bfloat16)
        out[:, span] = jnp.dot(weights, values[:, span], preferred_element_type=jnp.float32)


def reach_back(members, heads, chosen, gates, table, carry, earlier, *refs):
    count = len(chosen)
    half = members // CORES
    query_parts, outs = refs[:count], refs[count + gates :]
    _, me = position()
    for n, e in enumerate(chosen):
        for side in range(CORES):
            j = me ^ e ^ (side * half)
            before = jnp.where(table[pl.ds(j, 1), :] < 0, 1.0, 0.0).astype(jnp.float32)
            for h, span in enumerate(heads_of(heads)):
                held = (carry[j, h] + before * earlier[h]).astype(jnp.bfloat16)
                query = query_parts[n][side, :, span].astype(jnp.bfloat16)
                outs[n * CORES + side][:, span] = jnp.dot(query, held, preferred_element_type=jnp.float32)


def finish(chosen, members, heads, rows, table, own, gain, *refs):
    count = len(chosen)
    parts, out = refs[:count], refs[-3]
    buffer, sems = refs[-2:]
    width = heads * HEAD_DIM
    _, me = position()
    continued = lax.broadcasted_iota(jnp.int32, (rows, HEAD_DIM), 0) < table[members + 1 : members + 2, :]
    copies = []
    for i, d in enumerate(chosen):
        columns = columns_of(me ^ d, width)
        inner = own[:, columns]
        scales = gain[:, columns]
        for span in heads_of(heads):
            mixed = inner[:, span] + jnp.where(continued, parts[i][:, span], 0.0)
            scale = lax.rsqrt(jnp.mean(mixed * mixed, axis=-1, keepdims=True) + EPSILON)
            buffer[i, :, span] = (mixed * scale * scales[:, span]).astype(jnp.bfloat16)
        copy = pltpu.make_async_copy(buffer.at[i], out.at[:, columns], sems.at[i])
        copy.start()
        copies.append(copy)
    for copy in copies:
        copy.wait()


def body(queries, keys, values, lengths, norm_gain):
    rows, columns = queries.shape
    head_count = columns // HEAD_DIM
    docs = lengths.shape[0]
    inner_count = lax.axis_size("inner")
    devices = lax.axis_size("outer") * inner_count
    members = CORES * inner_count
    half = inner_count
    planes = devices // members
    heads = head_count // members
    width = heads * HEAD_DIM
    reach = -(-(devices // SHARE) // members)
    everyone = ("outer", "inner")
    index = lax.axis_index("outer") * inner_count + lax.axis_index("inner")
    me = index % members
    base = (index - me) * rows
    f32, bf16 = jnp.float32, jnp.bfloat16

    def call(kernel, name, out_shape, in_specs, out_specs, scratch=(), flops=0, moved=0, aliases=None):
        return pl.pallas_call(
            kernel,
            out_shape=out_shape,
            in_specs=in_specs,
            out_specs=out_specs,
            scratch_shapes=scratch,
            compiler_params=pltpu.CompilerParams(vmem_limit_bytes=16 * 1024 * 1024),
            cost_estimate=pl.CostEstimate(flops=flops, bytes_accessed=moved, transcendentals=0),
            input_output_aliases=aliases or {},
            name=name,
        )

    def shape(*sizes, dtype=f32):
        return jax.ShapeDtypeStruct(sizes, dtype)

    def swap(part, d):
        pairs = [(g, g - g % members + (g % members ^ d)) for g in range(devices)]
        return lax.ppermute(part, everyone, pairs)

    near_order = ranked(half, 2, 1, 3, 0)
    far_order = ranked(half, 3, 2, 1, 0)[:-1]
    query_order = ranked(half, 3, 2, 1, 0)
    block_bytes = rows * columns * 4
    parts = call(
        functools.partial(spread, members, width, near_order),
        "spread",
        [shape(2, rows, width)] * half + [shape(half, 3, rows, width)],
        [HBM, HBM, HBM],
        [VMEM] * (half + 1),
        [pltpu.VMEM((members, rows, width), bf16)] * 3 + [pltpu.SemaphoreType.DMA((3, members))],
    )(*[pltpu.with_memory_space_constraint(x, pltpu.HBM) for x in (queries, keys, values)])
    near_got = [swap(part, e) if e else part for e, part in zip(near_order, parts)]
    swapped = swap(parts[half], half)
    far_parts = call(
        functools.partial(forward, far_order),
        "forward",
        [shape(2, rows, width)] * (half - 1),
        [VMEM],
        [VMEM] * (half - 1),
        moved=2 * block_bytes,
    )(swapped)
    far_got = [swap(part, e) for e, part in zip(far_order, far_parts)] + [swapped]
    gates = near_got[:-1]
    *query_parts, table = call(
        functools.partial(join_queries, members, width, query_order, rows, docs, len(gates)),
        "join_queries",
        [shape(CORES, rows, width)] * half + [shape(members + 2, HEAD_DIM, dtype=jnp.int32)],
        [SMEM, VMEM, VMEM] + [ANY] * len(gates),
        [VMEM] * (half + 1),
        moved=2 * block_bytes,
    )(lengths, queries, swapped, *gates)
    query_got = [swap(part, e) if e else part for e, part in zip(query_order, query_parts)]

    own = call(
        functools.partial(inside, head_count, docs, rows),
        "inside",
        shape(rows, columns),
        [SMEM, VMEM, VMEM, VMEM],
        VMEM,
        flops=4 * rows * rows * columns,
        moved=3 * block_bytes,
    )(lengths, queries, keys, values)

    carry, total = call(
        functools.partial(gather_states, members, heads, rows, near_order + [e + half for e in far_order + [0]]),
        "gather_states",
        [shape(members, heads, HEAD_DIM, HEAD_DIM), shape(heads, HEAD_DIM, HEAD_DIM)],
        [VMEM] * (members + 1) + [ANY],
        [VMEM] * 2,
        [pltpu.VMEM((members, rows, width), bf16)] * 2,
        flops=2 * rows * HEAD_DIM * columns,
        moved=4 * block_bytes,
    )(table, *near_got, *far_got, own)
    up = [(g, g + members) for g in range(devices - members)]
    moving = lax.ppermute(total, everyone, up)
    earlier = moving
    if reach > 1:
        starts = BLOCK * (jnp.cumsum(lengths) - lengths)
        opens = jnp.max(jnp.where(starts <= base, starts, 0))
        for k in range(2, min(reach, planes - 1) + 1):
            moving = lax.ppermute(moving, everyone, up)
            earlier = earlier + jnp.where(opens < base - (k - 1) * members * rows, moving, 0.0)
    crossed_got = {}
    late = [e for e in (2, 1, 0,) if e < half]
    soon = [e for e in ranked(half, 3) if e not in late]
    gates = []
    for chosen in (soon, late):
        crossed = call(
            functools.partial(reach_back, members, heads, chosen, len(gates)),
            "reach_back",
            [shape(rows, width)] * (CORES * len(chosen)),
            [VMEM] * (len(chosen) + 3) + [ANY] * len(gates),
            [VMEM] * (CORES * len(chosen)),
            flops=2 * rows * HEAD_DIM * width * CORES * len(chosen),
            moved=2 * block_bytes,
        )(table, carry, earlier, *[query_got[query_order.index(e)] for e in chosen], *gates)
        for n, e in enumerate(chosen):
            for side in range(CORES):
                d = e ^ (side * half)
                part = crossed[n * CORES + side]
                crossed_got[d] = swap(part, d) if d else part
        gates = crossed[:1]

    gain = norm_gain.reshape(1, columns)
    out = None
    listed = [[(0, 0), (3, 1), (3, 0)], [(0, 1), (1, 0), (2, 0), (1, 1), (2, 1)]]
    named = [pair for group in listed for pair in group]
    listed[0] += [(e, side) for e in soon for side in range(CORES) if (e, side) not in named]
    groups = [[e + side * half for e, side in group] for group in listed]
    for chosen in groups:
        more = [] if out is None else [out]
        out = call(
            functools.partial(finish, chosen, members, heads, rows),
            "finish",
            shape(rows, columns, dtype=bf16),
            [VMEM] * (3 + len(chosen)) + [ANY] * len(more),
            ANY,
            [pltpu.VMEM((len(chosen), rows, width), bf16), pltpu.SemaphoreType.DMA((len(chosen),))],
            moved=2 * block_bytes,
            aliases={3 + len(chosen): 0} if more else None,
        )(table, own, gain, *[crossed_got[d] for d in chosen], *more)
    return out


def solution(mesh):
    placed = (
        P(("outer", "inner"), None),
        P(("outer", "inner"), None),
        P(("outer", "inner"), None),
        P(),
        P(),
    )
    return jax.shard_map(
        body, mesh=mesh, in_specs=placed, out_specs=P(("outer", "inner"), None), check_vma=False
    )
```

```python
import functools

import jax
import jax.numpy as jnp
from jax import lax
from jax.experimental import pallas as pl
from jax.experimental.pallas import tpu as pltpu
from jax.sharding import PartitionSpec as P

HEAD_DIM = 128
BLOCK = 16
CORES = 2
SHARE = 4
EPSILON = 1e-05
SMEM = pl.BlockSpec(memory_space=pltpu.SMEM)
VMEM = pl.BlockSpec(memory_space=pltpu.VMEM)
ANY = pl.BlockSpec(memory_space=pl.ANY)
HBM = pl.BlockSpec(memory_space=pltpu.HBM)


def columns_of(member, width):
    return pl.ds(pl.multiple_of(member * width, width), width)


def position():
    inner_count = lax.axis_size("inner")
    index = lax.axis_index("outer") * inner_count + lax.axis_index("inner")
    return index, index % (CORES * inner_count)


def ranked(count, *first):
    first = [e for e in first if e < count]
    return [e for e in range(count) if e not in first and e > max(first)] + first


def heads_of(heads):
    return [slice(h * HEAD_DIM, (h + 1) * HEAD_DIM) for h in range(heads)]


def start_of(lengths, docs, token):
    begin = jnp.int32(0)
    found = jnp.int32(0)
    after = jnp.int32(jnp.iinfo(jnp.int32).max)
    for i in range(docs):
        found = jnp.where(begin <= token, begin, found)
        after = jnp.where(begin > token, jnp.minimum(begin, after), after)
        begin = begin + lengths[i] * BLOCK
    return found, after


def spread(members, width, near_order, queries, keys, values, *refs):
    half = members // CORES
    near, cross = refs[:half], refs[half]
    near_buffer, cross_buffer, sems = refs[half + 1 :]
    _, me = position()
    side = me // half
    near_copies = [
        pltpu.make_async_copy(source.at[:, columns_of(side, half * width)], near_buffer.at[i], sems.at[0, i])
        for i, source in enumerate((keys, values))
    ]
    cross_copies = [
        pltpu.make_async_copy(source.at[:, columns_of(1 - side, half * width)], cross_buffer.at[i], sems.at[1, i])
        for i, source in enumerate((keys, values, queries))
    ]
    for copy in near_copies + cross_copies:
        copy.start()
    for i, copy in enumerate(near_copies):
        copy.wait()
        for n, d in enumerate(near_order):
            near[n][i] = near_buffer[i, :, columns_of((me ^ d) % half, width)].astype(jnp.float32)
    for i, copy in enumerate(cross_copies):
        copy.wait()
        for e in range(half):
            cross[e, i] = cross_buffer[i, :, columns_of((me ^ e) % half, width)].astype(jnp.float32)


def forward(order, swapped, *outs):
    for n, e in enumerate(order):
        outs[n][...] = swapped[e, 0:2]


def join_queries(members, width, order, rows, docs, gates, lengths, queries, swapped, *refs):
    half = members // CORES
    outs, table = refs[gates:-1], refs[-1]
    index, me = position()
    for n, e in enumerate(order):
        outs[n][0] = queries[:, columns_of(me ^ e, width)].astype(jnp.float32)
        outs[n][1] = swapped[e, 2]
    base = (index - me) * rows
    for j in range(members + 1):
        found, _ = start_of(lengths, docs, base + j * rows)
        table[j : j + 1, :] = jnp.full((1, HEAD_DIM), found - base, jnp.int32)
    _, after = start_of(lengths, docs, index * rows)
    table[members + 1 : members + 2, :] = jnp.full((1, HEAD_DIM), after - index * rows, jnp.int32)


def gather_states(members, heads, rows, order, table, *refs):
    half = members // CORES
    parts = dict(zip(order, refs))
    carry_out, total_out, key_blocks, value_blocks = refs[members + 1 :]
    _, me = position()
    row = lax.broadcasted_iota(jnp.int32, (rows, HEAD_DIM), 0)
    for d in range(members):
        j = me ^ d
        kept = row >= table[pl.ds(j + 1, 1), :] - j * rows
        key, value = (parts[d][0, 0], parts[d][0, 1]) if d == half else (parts[d][0], parts[d][1])
        for span in heads_of(heads):
            key_blocks[j, :, span] = jnp.where(kept, key[:, span], 0.0).astype(jnp.bfloat16)
        value_blocks[j] = value.astype(jnp.bfloat16)
    state = [jnp.zeros((HEAD_DIM, HEAD_DIM), jnp.float32) for _ in range(heads)]
    for j in range(members):
        keep = jnp.where(table[j + 1 : j + 2, :] <= j * rows, 1.0, 0.0).astype(jnp.float32)
        for h, span in enumerate(heads_of(heads)):
            carry_out[j, h] = state[h]
            own = lax.dot_general(
                key_blocks[j, :, span],
                value_blocks[j, :, span],
                (((0,), (0,)), ((), ())),
                preferred_element_type=jnp.float32,
            )
            state[h] = keep * state[h] + own
    for h in range(heads):
        total_out[h] = state[h]


def inside(head_count, docs, rows, lengths, queries, keys, values, out):
    begin = position()[0] * rows
    row = lax.broadcasted_iota(jnp.int32, (rows, rows), 0)
    lane = lax.broadcasted_iota(jnp.int32, (rows, rows), 1)
    since = jnp.zeros((rows, rows), jnp.int32)
    start = -begin
    for i in range(docs):
        since = jnp.where(start <= row, start, since)
        start = start + lengths[i] * BLOCK
    allowed = (lane <= row) & (lane >= since)
    for span in heads_of(head_count):
        scores = lax.dot_general(
            queries[:, span], keys[:, span], (((1,), (1,)), ((), ())), preferred_element_type=jnp.float32
        )
        weights = jnp.where(allowed, scores, 0.0).astype(jnp.bfloat16)
        out[:, span] = jnp.dot(weights, values[:, span], preferred_element_type=jnp.float32)


def reach_back(members, heads, chosen, gates, table, carry, earlier, *refs):
    count = len(chosen)
    half = members // CORES
    query_parts, outs = refs[:count], refs[count + gates :]
    _, me = position()
    for n, e in enumerate(chosen):
        for side in range(CORES):
            j = me ^ e ^ (side * half)
            before = jnp.where(table[pl.ds(j, 1), :] < 0, 1.0, 0.0).astype(jnp.float32)
            for h, span in enumerate(heads_of(heads)):
                held = (carry[j, h] + before * earlier[h]).astype(jnp.bfloat16)
                query = query_parts[n][side, :, span].astype(jnp.bfloat16)
                outs[n * CORES + 1 - side][:, span] = jnp.dot(query, held, preferred_element_type=jnp.float32)


def finish(chosen, members, heads, rows, table, own, gain, *refs):
    count = len(chosen)
    parts, out = refs[:count], refs[-3]
    buffer, sems = refs[-2:]
    width = heads * HEAD_DIM
    _, me = position()
    continued = lax.broadcasted_iota(jnp.int32, (rows, HEAD_DIM), 0) < table[members + 1 : members + 2, :]
    copies = []
    for i, d in enumerate(chosen):
        columns = columns_of(me ^ d, width)
        inner = own[:, columns]
        scales = gain[:, columns]
        for span in heads_of(heads):
            mixed = inner[:, span] + jnp.where(continued, parts[i][:, span], 0.0)
            scale = lax.rsqrt(jnp.mean(mixed * mixed, axis=-1, keepdims=True) + EPSILON)
            buffer[i, :, span] = (mixed * scale * scales[:, span]).astype(jnp.bfloat16)
        copy = pltpu.make_async_copy(buffer.at[i], out.at[:, columns], sems.at[i])
        copy.start()
        copies.append(copy)
    for copy in copies:
        copy.wait()


def body(queries, keys, values, lengths, norm_gain):
    rows, columns = queries.shape
    head_count = columns // HEAD_DIM
    docs = lengths.shape[0]
    inner_count = lax.axis_size("inner")
    devices = lax.axis_size("outer") * inner_count
    members = CORES * inner_count
    half = inner_count
    planes = devices // members
    heads = head_count // members
    width = heads * HEAD_DIM
    reach = -(-(devices // SHARE) // members)
    everyone = ("outer", "inner")
    index = lax.axis_index("outer") * inner_count + lax.axis_index("inner")
    me = index % members
    base = (index - me) * rows
    f32, bf16 = jnp.float32, jnp.bfloat16

    def call(kernel, name, out_shape, in_specs, out_specs, scratch=(), flops=0, moved=0, aliases=None):
        return pl.pallas_call(
            kernel,
            out_shape=out_shape,
            in_specs=in_specs,
            out_specs=out_specs,
            scratch_shapes=scratch,
            compiler_params=pltpu.CompilerParams(vmem_limit_bytes=16 * 1024 * 1024),
            cost_estimate=pl.CostEstimate(flops=flops, bytes_accessed=moved, transcendentals=0),
            input_output_aliases=aliases or {},
            name=name,
        )

    def shape(*sizes, dtype=f32):
        return jax.ShapeDtypeStruct(sizes, dtype)

    def swap(part, d):
        pairs = [(g, g - g % members + (g % members ^ d)) for g in range(devices)]
        return lax.ppermute(part, everyone, pairs)

    near_order = ranked(half, 2, 1, 3, 0)
    far_order = ranked(half, 3, 2, 1, 0)[:-1]
    query_order = ranked(half, 3, 2, 1, 0)
    block_bytes = rows * columns * 4
    parts = call(
        functools.partial(spread, members, width, near_order),
        "spread",
        [shape(2, rows, width)] * half + [shape(half, 3, rows, width)],
        [HBM, HBM, HBM],
        [VMEM] * (half + 1),
        [
            pltpu.VMEM((2, rows, half * width), bf16),
            pltpu.VMEM((3, rows, half * width), bf16),
            pltpu.SemaphoreType.DMA((CORES, 3)),
        ],
    )(*[pltpu.with_memory_space_constraint(x, pltpu.HBM) for x in (queries, keys, values)])
    near_got = [swap(part, e) if e else part for e, part in zip(near_order, parts)]
    swapped = swap(parts[half], half)
    far_parts = call(
        functools.partial(forward, far_order),
        "forward",
        [shape(2, rows, width)] * (half - 1),
        [VMEM],
        [VMEM] * (half - 1),
        moved=2 * block_bytes,
    )(swapped)
    far_got = [swap(part, e) for e, part in zip(far_order, far_parts)] + [swapped]
    gates = near_got[:-1]
    *query_parts, table = call(
        functools.partial(join_queries, members, width, query_order, rows, docs, len(gates)),
        "join_queries",
        [shape(CORES, rows, width)] * half + [shape(members + 2, HEAD_DIM, dtype=jnp.int32)],
        [SMEM, VMEM, VMEM] + [ANY] * len(gates),
        [VMEM] * (half + 1),
        moved=2 * block_bytes,
    )(lengths, queries, swapped, *gates)
    query_got = [swap(part, e) if e else part for e, part in zip(query_order, query_parts)]

    own = call(
        functools.partial(inside, head_count, docs, rows),
        "inside",
        shape(rows, columns),
        [SMEM, VMEM, VMEM, VMEM],
        VMEM,
        flops=4 * rows * rows * columns,
        moved=3 * block_bytes,
    )(lengths, queries, keys, values)

    carry, total = call(
        functools.partial(gather_states, members, heads, rows, near_order + [e + half for e in far_order + [0]]),
        "gather_states",
        [shape(members, heads, HEAD_DIM, HEAD_DIM), shape(heads, HEAD_DIM, HEAD_DIM)],
        [VMEM] * (members + 1) + [ANY],
        [VMEM] * 2,
        [pltpu.VMEM((members, rows, width), bf16)] * 2,
        flops=2 * rows * HEAD_DIM * columns,
        moved=4 * block_bytes,
    )(table, *near_got, *far_got, own)
    up = [(g, g + members) for g in range(devices - members)]
    moving = lax.ppermute(total, everyone, up)
    earlier = moving
    if reach > 1:
        starts = BLOCK * (jnp.cumsum(lengths) - lengths)
        opens = jnp.max(jnp.where(starts <= base, starts, 0))
        for k in range(2, min(reach, planes - 1) + 1):
            moving = lax.ppermute(moving, everyone, up)
            earlier = earlier + jnp.where(opens < base - (k - 1) * members * rows, moving, 0.0)
    crossed_got = {}
    late = [e for e in (2, 0, 1,) if e < half]
    soon = [e for e in ranked(half, 3) if e not in late]
    gates = []
    for chosen in (soon, late):
        crossed = call(
            functools.partial(reach_back, members, heads, chosen, len(gates)),
            "reach_back",
            [shape(rows, width)] * (CORES * len(chosen)),
            [VMEM] * (len(chosen) + 3) + [ANY] * len(gates),
            [VMEM] * (CORES * len(chosen)),
            flops=2 * rows * HEAD_DIM * width * CORES * len(chosen),
            moved=2 * block_bytes,
        )(table, carry, earlier, *[query_got[query_order.index(e)] for e in chosen], *gates)
        for n, e in enumerate(chosen):
            for side in reversed(range(CORES)):
                d = e ^ (side * half)
                part = crossed[n * CORES + 1 - side]
                crossed_got[d] = swap(part, d) if d else part
        gates = crossed[:1]

    gain = norm_gain.reshape(1, columns)
    out = None
    listed = [[(0, 0), (3, 1), (3, 0)], [(0, 1), (1, 0), (2, 0), (1, 1), (2, 1)]]
    named = [pair for group in listed for pair in group]
    listed[0] += [(e, side) for e in soon for side in range(CORES) if (e, side) not in named]
    groups = [[e + side * half for e, side in group] for group in listed]
    for chosen in groups:
        more = [] if out is None else [out]
        out = call(
            functools.partial(finish, chosen, members, heads, rows),
            "finish",
            shape(rows, columns, dtype=bf16),
            [VMEM] * (3 + len(chosen)) + [ANY] * len(more),
            ANY,
            [pltpu.VMEM((len(chosen), rows, width), bf16), pltpu.SemaphoreType.DMA((len(chosen),))],
            moved=2 * block_bytes,
            aliases={3 + len(chosen): 0} if more else None,
        )(table, own, gain, *[crossed_got[d] for d in chosen], *more)
    return out


def solution(mesh):
    placed = (
        P(("outer", "inner"), None),
        P(("outer", "inner"), None),
        P(("outer", "inner"), None),
        P(),
        P(),
    )
    return jax.shard_map(
        body, mesh=mesh, in_specs=placed, out_specs=P(("outer", "inner"), None), check_vma=False
    )
```

```python
import functools

import jax
import jax.numpy as jnp
from jax import lax
from jax.experimental import pallas as pl
from jax.experimental.pallas import tpu as pltpu
from jax.sharding import PartitionSpec as P

HEAD_DIM = 128
BLOCK = 16
CORES = 2
SHARE = 4
EPSILON = 1e-05
SMEM = pl.BlockSpec(memory_space=pltpu.SMEM)
VMEM = pl.BlockSpec(memory_space=pltpu.VMEM)
ANY = pl.BlockSpec(memory_space=pl.ANY)
HBM = pl.BlockSpec(memory_space=pltpu.HBM)


def columns_of(member, width):
    return pl.ds(pl.multiple_of(member * width, width), width)


def position():
    inner_count = lax.axis_size("inner")
    index = lax.axis_index("outer") * inner_count + lax.axis_index("inner")
    return index, index % (CORES * inner_count)


def ranked(count, *first):
    first = [e for e in first if e < count]
    return [e for e in range(count) if e not in first and e > max(first)] + first


def heads_of(heads):
    return [slice(h * HEAD_DIM, (h + 1) * HEAD_DIM) for h in range(heads)]


def start_of(lengths, docs, token):
    begin = jnp.int32(0)
    found = jnp.int32(0)
    after = jnp.int32(jnp.iinfo(jnp.int32).max)
    for i in range(docs):
        found = jnp.where(begin <= token, begin, found)
        after = jnp.where(begin > token, jnp.minimum(begin, after), after)
        begin = begin + lengths[i] * BLOCK
    return found, after


def spread(members, width, near_order, queries, keys, values, *refs):
    half = members // CORES
    near, cross = refs[:half], refs[half]
    near_buffer, cross_buffer, sems = refs[half + 1 :]
    _, me = position()
    side = me // half
    near_copies = [
        pltpu.make_async_copy(source.at[:, columns_of(side, half * width)], near_buffer.at[i], sems.at[0, i])
        for i, source in enumerate((keys, values))
    ]
    cross_copies = [
        pltpu.make_async_copy(source.at[:, columns_of(1 - side, half * width)], cross_buffer.at[i], sems.at[1, i])
        for i, source in enumerate((keys, values, queries))
    ]
    for copy in near_copies + cross_copies:
        copy.start()
    for i, copy in enumerate(near_copies):
        copy.wait()
        for n, d in enumerate(near_order):
            near[n][i] = near_buffer[i, :, columns_of((me ^ d) % half, width)].astype(jnp.float32)
    for i, copy in enumerate(cross_copies):
        copy.wait()
        for e in range(half):
            cross[e, i] = cross_buffer[i, :, columns_of((me ^ e) % half, width)].astype(jnp.float32)


def forward(order, swapped, *outs):
    for n, e in enumerate(order):
        outs[n][...] = swapped[e, 0:2]


def join_queries(members, width, order, rows, docs, gates, lengths, queries, swapped, *refs):
    half = members // CORES
    outs, table = refs[gates:-1], refs[-1]
    index, me = position()
    for n, e in enumerate(order):
        outs[n][0] = queries[:, columns_of(me ^ e, width)].astype(jnp.float32)
        outs[n][1] = swapped[e, 2]
    base = (index - me) * rows
    for j in range(members + 1):
        found, _ = start_of(lengths, docs, base + j * rows)
        table[j : j + 1, :] = jnp.full((1, HEAD_DIM), found - base, jnp.int32)
    _, after = start_of(lengths, docs, index * rows)
    table[members + 1 : members + 2, :] = jnp.full((1, HEAD_DIM), after - index * rows, jnp.int32)


def gather_states(members, heads, rows, order, table, *refs):
    half = members // CORES
    parts = dict(zip(order, refs))
    carry_out, total_out, key_blocks, value_blocks = refs[members + 1 :]
    _, me = position()
    row = lax.broadcasted_iota(jnp.int32, (rows, HEAD_DIM), 0)
    for d in range(members):
        j = me ^ d
        kept = row >= table[pl.ds(j + 1, 1), :] - j * rows
        key, value = (parts[d][0, 0], parts[d][0, 1]) if d == half else (parts[d][0], parts[d][1])
        for span in heads_of(heads):
            key_blocks[j, :, span] = jnp.where(kept, key[:, span], 0.0).astype(jnp.bfloat16)
        value_blocks[j] = value.astype(jnp.bfloat16)
    state = [jnp.zeros((HEAD_DIM, HEAD_DIM), jnp.float32) for _ in range(heads)]
    for j in range(members):
        keep = jnp.where(table[j + 1 : j + 2, :] <= j * rows, 1.0, 0.0).astype(jnp.float32)
        for h, span in enumerate(heads_of(heads)):
            carry_out[j, h] = state[h]
            own = lax.dot_general(
                key_blocks[j, :, span],
                value_blocks[j, :, span],
                (((0,), (0,)), ((), ())),
                preferred_element_type=jnp.float32,
            )
            state[h] = keep * state[h] + own
    for h in range(heads):
        total_out[h] = state[h]


def inside(head_count, docs, rows, lengths, queries, keys, values, out):
    begin = position()[0] * rows
    row = lax.broadcasted_iota(jnp.int32, (rows, rows), 0)
    lane = lax.broadcasted_iota(jnp.int32, (rows, rows), 1)
    since = jnp.zeros((rows, rows), jnp.int32)
    start = -begin
    for i in range(docs):
        since = jnp.where(start <= row, start, since)
        start = start + lengths[i] * BLOCK
    allowed = (lane <= row) & (lane >= since)
    for span in heads_of(head_count):
        scores = lax.dot_general(
            queries[:, span], keys[:, span], (((1,), (1,)), ((), ())), preferred_element_type=jnp.float32
        )
        weights = jnp.where(allowed, scores, 0.0).astype(jnp.bfloat16)
        out[:, span] = jnp.dot(weights, values[:, span], preferred_element_type=jnp.float32)


def reach_back(members, heads, chosen, gates, table, carry, earlier, *refs):
    count = len(chosen)
    half = members // CORES
    query_parts, outs = refs[:count], refs[count + gates :]
    _, me = position()
    for n, e in enumerate(chosen):
        for side in range(CORES):
            j = me ^ e ^ (side * half)
            before = jnp.where(table[pl.ds(j, 1), :] < 0, 1.0, 0.0).astype(jnp.float32)
            for h, span in enumerate(heads_of(heads)):
                held = (carry[j, h] + before * earlier[h]).astype(jnp.bfloat16)
                query = query_parts[n][side, :, span].astype(jnp.bfloat16)
                outs[n * CORES + 1 - side][:, span] = jnp.dot(query, held, preferred_element_type=jnp.float32)


def finish(chosen, members, heads, rows, table, own, gain, *refs):
    count = len(chosen)
    parts, out = refs[:count], refs[-3]
    buffer, sems = refs[-2:]
    width = heads * HEAD_DIM
    _, me = position()
    continued = lax.broadcasted_iota(jnp.int32, (rows, HEAD_DIM), 0) < table[members + 1 : members + 2, :]
    copies = []
    for i, d in enumerate(chosen):
        columns = columns_of(me ^ d, width)
        inner = own[:, columns]
        scales = gain[:, columns]
        for span in heads_of(heads):
            mixed = inner[:, span] + jnp.where(continued, parts[i][:, span], 0.0)
            scale = lax.rsqrt(jnp.mean(mixed * mixed, axis=-1, keepdims=True) + EPSILON)
            buffer[i, :, span] = (mixed * scale * scales[:, span]).astype(jnp.bfloat16)
        copy = pltpu.make_async_copy(buffer.at[i], out.at[:, columns], sems.at[i])
        copy.start()
        copies.append(copy)
    for copy in copies:
        copy.wait()


def body(queries, keys, values, lengths, norm_gain):
    rows, columns = queries.shape
    head_count = columns // HEAD_DIM
    docs = lengths.shape[0]
    inner_count = lax.axis_size("inner")
    devices = lax.axis_size("outer") * inner_count
    members = CORES * inner_count
    half = inner_count
    planes = devices // members
    heads = head_count // members
    width = heads * HEAD_DIM
    reach = -(-(devices // SHARE) // members)
    everyone = ("outer", "inner")
    index = lax.axis_index("outer") * inner_count + lax.axis_index("inner")
    me = index % members
    base = (index - me) * rows
    f32, bf16 = jnp.float32, jnp.bfloat16

    def call(kernel, name, out_shape, in_specs, out_specs, scratch=(), flops=0, moved=0, aliases=None):
        return pl.pallas_call(
            kernel,
            out_shape=out_shape,
            in_specs=in_specs,
            out_specs=out_specs,
            scratch_shapes=scratch,
            compiler_params=pltpu.CompilerParams(vmem_limit_bytes=16 * 1024 * 1024),
            cost_estimate=pl.CostEstimate(flops=flops, bytes_accessed=moved, transcendentals=0),
            input_output_aliases=aliases or {},
            name=name,
        )

    def shape(*sizes, dtype=f32):
        return jax.ShapeDtypeStruct(sizes, dtype)

    def swap(part, d):
        pairs = [(g, g - g % members + (g % members ^ d)) for g in range(devices)]
        return lax.ppermute(part, everyone, pairs)

    near_order = ranked(half, 2, 1, 3, 0)
    far_order = ranked(half, 3, 2, 1, 0)[:-1]
    query_order = ranked(half, 3, 2, 1, 0)
    block_bytes = rows * columns * 4
    parts = call(
        functools.partial(spread, members, width, near_order),
        "spread",
        [shape(2, rows, width)] * half + [shape(half, 3, rows, width)],
        [HBM, HBM, HBM],
        [VMEM] * (half + 1),
        [
            pltpu.VMEM((2, rows, half * width), bf16),
            pltpu.VMEM((3, rows, half * width), bf16),
            pltpu.SemaphoreType.DMA((CORES, 3)),
        ],
    )(*[pltpu.with_memory_space_constraint(x, pltpu.HBM) for x in (queries, keys, values)])
    near_got = [swap(part, e) if e else part for e, part in zip(near_order, parts)]
    swapped = swap(parts[half], half)
    far_parts = call(
        functools.partial(forward, far_order),
        "forward",
        [shape(2, rows, width)] * (half - 1),
        [VMEM],
        [VMEM] * (half - 1),
        moved=2 * block_bytes,
    )(swapped)
    far_got = [swap(part, e) for e, part in zip(far_order, far_parts)] + [swapped]
    gates = near_got[:-1]
    *query_parts, table = call(
        functools.partial(join_queries, members, width, query_order, rows, docs, len(gates)),
        "join_queries",
        [shape(CORES, rows, width)] * half + [shape(members + 2, HEAD_DIM, dtype=jnp.int32)],
        [SMEM, VMEM, VMEM] + [ANY] * len(gates),
        [VMEM] * (half + 1),
        moved=2 * block_bytes,
    )(lengths, queries, swapped, *gates)
    query_got = [swap(part, e) if e else part for e, part in zip(query_order, query_parts)]

    own = call(
        functools.partial(inside, head_count, docs, rows),
        "inside",
        shape(rows, columns),
        [SMEM, VMEM, VMEM, VMEM],
        VMEM,
        flops=4 * rows * rows * columns,
        moved=3 * block_bytes,
    )(lengths, queries, keys, values)

    carry, total = call(
        functools.partial(gather_states, members, heads, rows, near_order + [e + half for e in far_order + [0]]),
        "gather_states",
        [shape(members, heads, HEAD_DIM, HEAD_DIM), shape(heads, HEAD_DIM, HEAD_DIM)],
        [VMEM] * (members + 1) + [ANY],
        [VMEM] * 2,
        [pltpu.VMEM((members, rows, width), bf16)] * 2,
        flops=2 * rows * HEAD_DIM * columns,
        moved=4 * block_bytes,
    )(table, *near_got, *far_got, own)
    up = [(g, g + members) for g in range(devices - members)]
    moving = lax.ppermute(total, everyone, up)
    earlier = moving
    if reach > 1:
        starts = BLOCK * (jnp.cumsum(lengths) - lengths)
        opens = jnp.max(jnp.where(starts <= base, starts, 0))
        for k in range(2, min(reach, planes - 1) + 1):
            moving = lax.ppermute(moving, everyone, up)
            earlier = earlier + jnp.where(opens < base - (k - 1) * members * rows, moving, 0.0)
    crossed_got = {}
    late = [e for e in (2, 0, 1,) if e < half]
    soon = [e for e in ranked(half, 3) if e not in late]
    gates = []
    for chosen in (soon, late):
        crossed = call(
            functools.partial(reach_back, members, heads, chosen, len(gates)),
            "reach_back",
            [shape(rows, width)] * (CORES * len(chosen)),
            [VMEM] * (len(chosen) + 3) + [ANY] * len(gates),
            [VMEM] * (CORES * len(chosen)),
            flops=2 * rows * HEAD_DIM * width * CORES * len(chosen),
            moved=2 * block_bytes,
        )(table, carry, earlier, *[query_got[query_order.index(e)] for e in chosen], *gates)
        for n, e in enumerate(chosen):
            for side in reversed(range(CORES)):
                d = e ^ (side * half)
                part = crossed[n * CORES + 1 - side]
                crossed_got[d] = swap(part, d) if d else part
        gates = crossed[:1]

    gain = norm_gain.reshape(1, columns)
    out = None
    listed = [[(0, 0), (3, 1), (3, 0)], [(1, 0), (2, 0), (0, 1), (1, 1), (2, 1)]]
    named = [pair for group in listed for pair in group]
    listed[0] += [(e, side) for e in soon for side in range(CORES) if (e, side) not in named]
    groups = [[e + side * half for e, side in group] for group in listed]
    for chosen in groups:
        more = [] if out is None else [out]
        out = call(
            functools.partial(finish, chosen, members, heads, rows),
            "finish",
            shape(rows, columns, dtype=bf16),
            [VMEM] * (3 + len(chosen)) + [ANY] * len(more),
            ANY,
            [pltpu.VMEM((len(chosen), rows, width), bf16), pltpu.SemaphoreType.DMA((len(chosen),))],
            moved=2 * block_bytes,
            aliases={3 + len(chosen): 0} if more else None,
        )(table, own, gain, *[crossed_got[d] for d in chosen], *more)
    return out


def solution(mesh):
    placed = (
        P(("outer", "inner"), None),
        P(("outer", "inner"), None),
        P(("outer", "inner"), None),
        P(),
        P(),
    )
    return jax.shard_map(
        body, mesh=mesh, in_specs=placed, out_specs=P(("outer", "inner"), None), check_vma=False
    )
```

```python
import functools

import jax
import jax.numpy as jnp
from jax import lax
from jax.experimental import pallas as pl
from jax.experimental.pallas import tpu as pltpu
from jax.sharding import PartitionSpec as P

HEAD_DIM = 128
BLOCK = 16
CORES = 2
SHARE = 4
EPSILON = 1e-05
SMEM = pl.BlockSpec(memory_space=pltpu.SMEM)
VMEM = pl.BlockSpec(memory_space=pltpu.VMEM)
ANY = pl.BlockSpec(memory_space=pl.ANY)
HBM = pl.BlockSpec(memory_space=pltpu.HBM)


def columns_of(member, width):
    return pl.ds(pl.multiple_of(member * width, width), width)


def position():
    inner_count = lax.axis_size("inner")
    index = lax.axis_index("outer") * inner_count + lax.axis_index("inner")
    return index, index % (CORES * inner_count)


def ranked(count, *first):
    first = [e for e in first if e < count]
    return [e for e in range(count) if e not in first and e > max(first)] + first


def heads_of(heads):
    return [slice(h * HEAD_DIM, (h + 1) * HEAD_DIM) for h in range(heads)]


def start_of(lengths, docs, token):
    begin = jnp.int32(0)
    found = jnp.int32(0)
    after = jnp.int32(jnp.iinfo(jnp.int32).max)
    for i in range(docs):
        found = jnp.where(begin <= token, begin, found)
        after = jnp.where(begin > token, jnp.minimum(begin, after), after)
        begin = begin + lengths[i] * BLOCK
    return found, after


def spread(members, width, near_order, queries, keys, values, *refs):
    half = members // CORES
    near, cross = refs[:half], refs[half]
    near_buffer, cross_buffer, sems = refs[half + 1 :]
    _, me = position()
    side = me // half
    near_copies = [
        pltpu.make_async_copy(source.at[:, columns_of(side, half * width)], near_buffer.at[i], sems.at[0, i])
        for i, source in enumerate((keys, values))
    ]
    cross_copies = [
        pltpu.make_async_copy(source.at[:, columns_of(1 - side, half * width)], cross_buffer.at[i], sems.at[1, i])
        for i, source in enumerate((keys, values, queries))
    ]
    for copy in near_copies + cross_copies:
        copy.start()
    for i, copy in enumerate(near_copies):
        copy.wait()
        for n, d in enumerate(near_order):
            near[n][i] = near_buffer[i, :, columns_of((me ^ d) % half, width)].astype(jnp.float32)
    for i, copy in enumerate(cross_copies):
        copy.wait()
        for e in range(half):
            cross[e, i] = cross_buffer[i, :, columns_of((me ^ e) % half, width)].astype(jnp.float32)


def forward(order, swapped, *outs):
    for n, e in enumerate(order):
        outs[n][...] = swapped[e, 0:2]


def join_queries(members, width, order, rows, docs, gates, lengths, queries, swapped, *refs):
    half = members // CORES
    outs, table = refs[gates:-1], refs[-1]
    index, me = position()
    for n, e in enumerate(order):
        outs[n][0] = queries[:, columns_of(me ^ e, width)].astype(jnp.float32)
        outs[n][1] = swapped[e, 2]
    base = (index - me) * rows
    for j in range(members + 1):
        found, _ = start_of(lengths, docs, base + j * rows)
        table[j : j + 1, :] = jnp.full((1, HEAD_DIM), found - base, jnp.int32)
    _, after = start_of(lengths, docs, index * rows)
    table[members + 1 : members + 2, :] = jnp.full((1, HEAD_DIM), after - index * rows, jnp.int32)


def gather_states(members, heads, rows, order, table, *refs):
    half = members // CORES
    parts = dict(zip(order, refs))
    carry_out, total_out, key_blocks, value_blocks = refs[members + 1 :]
    _, me = position()
    row = lax.broadcasted_iota(jnp.int32, (rows, HEAD_DIM), 0)
    for d in range(members):
        j = me ^ d
        kept = row >= table[pl.ds(j + 1, 1), :] - j * rows
        key, value = (parts[d][0, 0], parts[d][0, 1]) if d == half else (parts[d][0], parts[d][1])
        for span in heads_of(heads):
            key_blocks[j, :, span] = jnp.where(kept, key[:, span], 0.0).astype(jnp.bfloat16)
        value_blocks[j] = value.astype(jnp.bfloat16)
    state = [jnp.zeros((HEAD_DIM, HEAD_DIM), jnp.float32) for _ in range(heads)]
    for j in range(members):
        keep = jnp.where(table[j + 1 : j + 2, :] <= j * rows, 1.0, 0.0).astype(jnp.float32)
        for h, span in enumerate(heads_of(heads)):
            carry_out[j, h] = state[h]
            own = lax.dot_general(
                key_blocks[j, :, span],
                value_blocks[j, :, span],
                (((0,), (0,)), ((), ())),
                preferred_element_type=jnp.float32,
            )
            state[h] = keep * state[h] + own
    for h in range(heads):
        total_out[h] = state[h]


def inside(head_count, docs, rows, lengths, queries, keys, values, out):
    begin = position()[0] * rows
    row = lax.broadcasted_iota(jnp.int32, (rows, rows), 0)
    lane = lax.broadcasted_iota(jnp.int32, (rows, rows), 1)
    since = jnp.zeros((rows, rows), jnp.int32)
    start = -begin
    for i in range(docs):
        since = jnp.where(start <= row, start, since)
        start = start + lengths[i] * BLOCK
    allowed = (lane <= row) & (lane >= since)
    for span in heads_of(head_count):
        scores = lax.dot_general(
            queries[:, span], keys[:, span], (((1,), (1,)), ((), ())), preferred_element_type=jnp.float32
        )
        weights = jnp.where(allowed, scores, 0.0).astype(jnp.bfloat16)
        out[:, span] = jnp.dot(weights, values[:, span], preferred_element_type=jnp.float32)


def reach_back(members, heads, chosen, gates, table, carry, earlier, *refs):
    count = len(chosen)
    half = members // CORES
    query_parts, outs = refs[:count], refs[count + gates :]
    _, me = position()
    for n, e in enumerate(chosen):
        for side in range(CORES):
            j = me ^ e ^ (side * half)
            before = jnp.where(table[pl.ds(j, 1), :] < 0, 1.0, 0.0).astype(jnp.float32)
            for h, span in enumerate(heads_of(heads)):
                held = (carry[j, h] + before * earlier[h]).astype(jnp.bfloat16)
                query = query_parts[n][side, :, span].astype(jnp.bfloat16)
                outs[n * CORES + 1 - side][:, span] = jnp.dot(query, held, preferred_element_type=jnp.float32)


def finish(chosen, members, heads, rows, table, own, gain, *refs):
    count = len(chosen)
    parts, out = refs[:count], refs[-3]
    buffer, sems = refs[-2:]
    width = heads * HEAD_DIM
    _, me = position()
    continued = lax.broadcasted_iota(jnp.int32, (rows, HEAD_DIM), 0) < table[members + 1 : members + 2, :]
    copies = []
    for i, d in enumerate(chosen):
        columns = columns_of(me ^ d, width)
        inner = own[:, columns]
        scales = gain[:, columns]
        for span in heads_of(heads):
            mixed = inner[:, span] + jnp.where(continued, parts[i][:, span], 0.0)
            scale = lax.rsqrt(jnp.mean(mixed * mixed, axis=-1, keepdims=True) + EPSILON)
            buffer[i, :, span] = (mixed * scale * scales[:, span]).astype(jnp.bfloat16)
        copy = pltpu.make_async_copy(buffer.at[i], out.at[:, columns], sems.at[i])
        copy.start()
        copies.append(copy)
    for copy in copies:
        copy.wait()


def body(queries, keys, values, lengths, norm_gain):
    rows, columns = queries.shape
    head_count = columns // HEAD_DIM
    docs = lengths.shape[0]
    inner_count = lax.axis_size("inner")
    devices = lax.axis_size("outer") * inner_count
    members = CORES * inner_count
    half = inner_count
    planes = devices // members
    heads = head_count // members
    width = heads * HEAD_DIM
    reach = -(-(devices // SHARE) // members)
    everyone = ("outer", "inner")
    index = lax.axis_index("outer") * inner_count + lax.axis_index("inner")
    me = index % members
    base = (index - me) * rows
    f32, bf16 = jnp.float32, jnp.bfloat16

    def call(kernel, name, out_shape, in_specs, out_specs, scratch=(), flops=0, moved=0, aliases=None):
        return pl.pallas_call(
            kernel,
            out_shape=out_shape,
            in_specs=in_specs,
            out_specs=out_specs,
            scratch_shapes=scratch,
            compiler_params=pltpu.CompilerParams(vmem_limit_bytes=16 * 1024 * 1024),
            cost_estimate=pl.CostEstimate(flops=flops, bytes_accessed=moved, transcendentals=0),
            input_output_aliases=aliases or {},
            name=name,
        )

    def shape(*sizes, dtype=f32):
        return jax.ShapeDtypeStruct(sizes, dtype)

    def swap(part, d):
        pairs = [(g, g - g % members + (g % members ^ d)) for g in range(devices)]
        return lax.ppermute(part, everyone, pairs)

    near_order = ranked(half, 2, 1, 3, 0)
    far_order = ranked(half, 3, 2, 1, 0)[:-1]
    query_order = ranked(half, 3, 2, 1, 0)
    block_bytes = rows * columns * 4
    parts = call(
        functools.partial(spread, members, width, near_order),
        "spread",
        [shape(2, rows, width)] * half + [shape(half, 3, rows, width)],
        [HBM, HBM, HBM],
        [VMEM] * (half + 1),
        [
            pltpu.VMEM((2, rows, half * width), bf16),
            pltpu.VMEM((3, rows, half * width), bf16),
            pltpu.SemaphoreType.DMA((CORES, 3)),
        ],
    )(*[pltpu.with_memory_space_constraint(x, pltpu.HBM) for x in (queries, keys, values)])
    near_got = [swap(part, e) if e else part for e, part in zip(near_order, parts)]
    swapped = swap(parts[half], half)
    far_parts = call(
        functools.partial(forward, far_order),
        "forward",
        [shape(2, rows, width)] * (half - 1),
        [VMEM],
        [VMEM] * (half - 1),
        moved=2 * block_bytes,
    )(swapped)
    far_got = [swap(part, e) for e, part in zip(far_order, far_parts)] + [swapped]
    gates = near_got[:1]
    *query_parts, table = call(
        functools.partial(join_queries, members, width, query_order, rows, docs, len(gates)),
        "join_queries",
        [shape(CORES, rows, width)] * half + [shape(members + 2, HEAD_DIM, dtype=jnp.int32)],
        [SMEM, VMEM, VMEM] + [ANY] * len(gates),
        [VMEM] * (half + 1),
        moved=2 * block_bytes,
    )(lengths, queries, swapped, *gates)
    query_got = [swap(part, e) if e else part for e, part in zip(query_order, query_parts)]

    own = call(
        functools.partial(inside, head_count, docs, rows),
        "inside",
        shape(rows, columns),
        [SMEM, VMEM, VMEM, VMEM],
        VMEM,
        flops=4 * rows * rows * columns,
        moved=3 * block_bytes,
    )(lengths, queries, keys, values)

    carry, total = call(
        functools.partial(gather_states, members, heads, rows, near_order + [e + half for e in far_order + [0]]),
        "gather_states",
        [shape(members, heads, HEAD_DIM, HEAD_DIM), shape(heads, HEAD_DIM, HEAD_DIM)],
        [VMEM] * (members + 1) + [ANY],
        [VMEM] * 2,
        [pltpu.VMEM((members, rows, width), bf16)] * 2,
        flops=2 * rows * HEAD_DIM * columns,
        moved=4 * block_bytes,
    )(table, *near_got, *far_got, own)
    up = [(g, g + members) for g in range(devices - members)]
    moving = lax.ppermute(total, everyone, up)
    earlier = moving
    if reach > 1:
        starts = BLOCK * (jnp.cumsum(lengths) - lengths)
        opens = jnp.max(jnp.where(starts <= base, starts, 0))
        for k in range(2, min(reach, planes - 1) + 1):
            moving = lax.ppermute(moving, everyone, up)
            earlier = earlier + jnp.where(opens < base - (k - 1) * members * rows, moving, 0.0)
    crossed_got = {}
    late = [e for e in (2, 0, 1,) if e < half]
    soon = [e for e in ranked(half, 3) if e not in late]
    gates = []
    for chosen in (soon, late):
        crossed = call(
            functools.partial(reach_back, members, heads, chosen, len(gates)),
            "reach_back",
            [shape(rows, width)] * (CORES * len(chosen)),
            [VMEM] * (len(chosen) + 3) + [ANY] * len(gates),
            [VMEM] * (CORES * len(chosen)),
            flops=2 * rows * HEAD_DIM * width * CORES * len(chosen),
            moved=2 * block_bytes,
        )(table, carry, earlier, *[query_got[query_order.index(e)] for e in chosen], *gates)
        for n, e in enumerate(chosen):
            for side in reversed(range(CORES)):
                d = e ^ (side * half)
                part = crossed[n * CORES + 1 - side]
                crossed_got[d] = swap(part, d) if d else part
        gates = crossed[:1]

    gain = norm_gain.reshape(1, columns)
    out = None
    listed = [[(0, 0), (3, 1), (3, 0)], [(0, 1), (1, 0), (2, 0), (1, 1), (2, 1)]]
    named = [pair for group in listed for pair in group]
    listed[0] += [(e, side) for e in soon for side in range(CORES) if (e, side) not in named]
    groups = [[e + side * half for e, side in group] for group in listed]
    for chosen in groups:
        more = [] if out is None else [out]
        out = call(
            functools.partial(finish, chosen, members, heads, rows),
            "finish",
            shape(rows, columns, dtype=bf16),
            [VMEM] * (3 + len(chosen)) + [ANY] * len(more),
            ANY,
            [pltpu.VMEM((len(chosen), rows, width), bf16), pltpu.SemaphoreType.DMA((len(chosen),))],
            moved=2 * block_bytes,
            aliases={3 + len(chosen): 0} if more else None,
        )(table, own, gain, *[crossed_got[d] for d in chosen], *more)
    return out


def solution(mesh):
    placed = (
        P(("outer", "inner"), None),
        P(("outer", "inner"), None),
        P(("outer", "inner"), None),
        P(),
        P(),
    )
    return jax.shard_map(
        body, mesh=mesh, in_specs=placed, out_specs=P(("outer", "inner"), None), check_vma=False
    )
```

```python
import functools

import jax
import jax.numpy as jnp
from jax import lax
from jax.experimental import pallas as pl
from jax.experimental.pallas import tpu as pltpu
from jax.sharding import PartitionSpec as P

HEAD_DIM = 128
BLOCK = 16
CORES = 2
SHARE = 4
EPSILON = 1e-05
SMEM = pl.BlockSpec(memory_space=pltpu.SMEM)
VMEM = pl.BlockSpec(memory_space=pltpu.VMEM)
ANY = pl.BlockSpec(memory_space=pl.ANY)
HBM = pl.BlockSpec(memory_space=pltpu.HBM)


def columns_of(member, width):
    return pl.ds(pl.multiple_of(member * width, width), width)


def position():
    inner_count = lax.axis_size("inner")
    index = lax.axis_index("outer") * inner_count + lax.axis_index("inner")
    return index, index % (CORES * inner_count)


def ranked(count, *first):
    first = [e for e in first if e < count]
    return [e for e in range(count) if e not in first and e > max(first)] + first


def heads_of(heads):
    return [slice(h * HEAD_DIM, (h + 1) * HEAD_DIM) for h in range(heads)]


def start_of(lengths, docs, token):
    begin = jnp.int32(0)
    found = jnp.int32(0)
    after = jnp.int32(jnp.iinfo(jnp.int32).max)
    for i in range(docs):
        found = jnp.where(begin <= token, begin, found)
        after = jnp.where(begin > token, jnp.minimum(begin, after), after)
        begin = begin + lengths[i] * BLOCK
    return found, after


def spread(members, width, near_order, queries, keys, values, *refs):
    half = members // CORES
    near, cross = refs[:half], refs[half]
    near_buffer, cross_buffer, sems = refs[half + 1 :]
    _, me = position()
    side = me // half
    near_copies = [
        pltpu.make_async_copy(source.at[:, columns_of(side, half * width)], near_buffer.at[i], sems.at[0, i])
        for i, source in enumerate((keys, values))
    ]
    cross_copies = [
        pltpu.make_async_copy(source.at[:, columns_of(1 - side, half * width)], cross_buffer.at[i], sems.at[1, i])
        for i, source in enumerate((keys, values, queries))
    ]
    for copy in near_copies + cross_copies:
        copy.start()
    for i, copy in enumerate(near_copies):
        copy.wait()
        for n, d in enumerate(near_order):
            near[n][i] = near_buffer[i, :, columns_of((me ^ d) % half, width)].astype(jnp.float32)
    for i, copy in enumerate(cross_copies):
        copy.wait()
        for e in range(half):
            cross[e, i] = cross_buffer[i, :, columns_of((me ^ e) % half, width)].astype(jnp.float32)


def forward(order, swapped, *outs):
    for n, e in enumerate(order):
        outs[n][...] = swapped[e, 0:2]


def join_queries(members, width, order, rows, docs, gates, lengths, queries, swapped, *refs):
    half = members // CORES
    outs, table = refs[gates:-1], refs[-1]
    index, me = position()
    for n, e in enumerate(order):
        outs[n][0] = queries[:, columns_of(me ^ e, width)].astype(jnp.float32)
        outs[n][1] = swapped[e, 2]
    base = (index - me) * rows
    for j in range(members + 1):
        found, _ = start_of(lengths, docs, base + j * rows)
        table[j : j + 1, :] = jnp.full((1, HEAD_DIM), found - base, jnp.int32)
    _, after = start_of(lengths, docs, index * rows)
    table[members + 1 : members + 2, :] = jnp.full((1, HEAD_DIM), after - index * rows, jnp.int32)


def gather_states(members, heads, rows, order, table, *refs):
    half = members // CORES
    parts = dict(zip(order, refs))
    carry_out, total_out, key_blocks, value_blocks = refs[members + 1 :]
    _, me = position()
    row = lax.broadcasted_iota(jnp.int32, (rows, HEAD_DIM), 0)
    for d in range(members):
        j = me ^ d
        kept = row >= table[pl.ds(j + 1, 1), :] - j * rows
        key, value = (parts[d][0, 0], parts[d][0, 1]) if d == half else (parts[d][0], parts[d][1])
        for span in heads_of(heads):
            key_blocks[j, :, span] = jnp.where(kept, key[:, span], 0.0).astype(jnp.bfloat16)
        value_blocks[j] = value.astype(jnp.bfloat16)
    state = [jnp.zeros((HEAD_DIM, HEAD_DIM), jnp.float32) for _ in range(heads)]
    for j in range(members):
        keep = jnp.where(table[j + 1 : j + 2, :] <= j * rows, 1.0, 0.0).astype(jnp.float32)
        for h, span in enumerate(heads_of(heads)):
            carry_out[j, h] = state[h]
            own = lax.dot_general(
                key_blocks[j, :, span],
                value_blocks[j, :, span],
                (((0,), (0,)), ((), ())),
                preferred_element_type=jnp.float32,
            )
            state[h] = keep * state[h] + own
    for h in range(heads):
        total_out[h] = state[h]


def inside(head_count, docs, rows, lengths, queries, keys, values, out):
    begin = position()[0] * rows
    row = lax.broadcasted_iota(jnp.int32, (rows, rows), 0)
    lane = lax.broadcasted_iota(jnp.int32, (rows, rows), 1)
    since = jnp.zeros((rows, rows), jnp.int32)
    start = -begin
    for i in range(docs):
        since = jnp.where(start <= row, start, since)
        start = start + lengths[i] * BLOCK
    allowed = (lane <= row) & (lane >= since)
    for span in heads_of(head_count):
        scores = lax.dot_general(
            queries[:, span], keys[:, span], (((1,), (1,)), ((), ())), preferred_element_type=jnp.float32
        )
        weights = jnp.where(allowed, scores, 0.0).astype(jnp.bfloat16)
        out[:, span] = jnp.dot(weights, values[:, span], preferred_element_type=jnp.float32)


def reach_back(members, heads, chosen, gates, table, carry, earlier, *refs):
    count = len(chosen)
    half = members // CORES
    query_parts, outs = refs[:count], refs[count + gates :]
    _, me = position()
    for n, e in enumerate(chosen):
        for side in range(CORES):
            j = me ^ e ^ (side * half)
            before = jnp.where(table[pl.ds(j, 1), :] < 0, 1.0, 0.0).astype(jnp.float32)
            for h, span in enumerate(heads_of(heads)):
                held = (carry[j, h] + before * earlier[h]).astype(jnp.bfloat16)
                query = query_parts[n][side, :, span].astype(jnp.bfloat16)
                outs[n * CORES + 1 - side][:, span] = jnp.dot(query, held, preferred_element_type=jnp.float32)


def finish(chosen, members, heads, rows, table, own, gain, *refs):
    count = len(chosen)
    parts, out = refs[:count], refs[-3]
    buffer, sems = refs[-2:]
    width = heads * HEAD_DIM
    _, me = position()
    continued = lax.broadcasted_iota(jnp.int32, (rows, HEAD_DIM), 0) < table[members + 1 : members + 2, :]
    copies = []
    for i, d in enumerate(chosen):
        columns = columns_of(me ^ d, width)
        inner = own[:, columns]
        scales = gain[:, columns]
        for span in heads_of(heads):
            mixed = inner[:, span] + jnp.where(continued, parts[i][:, span], 0.0)
            scale = lax.rsqrt(jnp.mean(mixed * mixed, axis=-1, keepdims=True) + EPSILON)
            buffer[i, :, span] = (mixed * scale * scales[:, span]).astype(jnp.bfloat16)
        copy = pltpu.make_async_copy(buffer.at[i], out.at[:, columns], sems.at[i])
        copy.start()
        copies.append(copy)
    for copy in copies:
        copy.wait()


def body(queries, keys, values, lengths, norm_gain):
    rows, columns = queries.shape
    head_count = columns // HEAD_DIM
    docs = lengths.shape[0]
    inner_count = lax.axis_size("inner")
    devices = lax.axis_size("outer") * inner_count
    members = CORES * inner_count
    half = inner_count
    planes = devices // members
    heads = head_count // members
    width = heads * HEAD_DIM
    reach = -(-(devices // SHARE) // members)
    everyone = ("outer", "inner")
    index = lax.axis_index("outer") * inner_count + lax.axis_index("inner")
    me = index % members
    base = (index - me) * rows
    f32, bf16 = jnp.float32, jnp.bfloat16

    def call(kernel, name, out_shape, in_specs, out_specs, scratch=(), flops=0, moved=0, aliases=None):
        return pl.pallas_call(
            kernel,
            out_shape=out_shape,
            in_specs=in_specs,
            out_specs=out_specs,
            scratch_shapes=scratch,
            compiler_params=pltpu.CompilerParams(vmem_limit_bytes=16 * 1024 * 1024),
            cost_estimate=pl.CostEstimate(flops=flops, bytes_accessed=moved, transcendentals=0),
            input_output_aliases=aliases or {},
            name=name,
        )

    def shape(*sizes, dtype=f32):
        return jax.ShapeDtypeStruct(sizes, dtype)

    def swap(part, d):
        pairs = [(g, g - g % members + (g % members ^ d)) for g in range(devices)]
        return lax.ppermute(part, everyone, pairs)

    near_order = ranked(half, 2, 1, 3, 0)
    far_order = ranked(half, 2, 3, 1, 0)[:-1]
    query_order = ranked(half, 3, 2, 1, 0)
    block_bytes = rows * columns * 4
    parts = call(
        functools.partial(spread, members, width, near_order),
        "spread",
        [shape(2, rows, width)] * half + [shape(half, 3, rows, width)],
        [HBM, HBM, HBM],
        [VMEM] * (half + 1),
        [
            pltpu.VMEM((2, rows, half * width), bf16),
            pltpu.VMEM((3, rows, half * width), bf16),
            pltpu.SemaphoreType.DMA((CORES, 3)),
        ],
    )(*[pltpu.with_memory_space_constraint(x, pltpu.HBM) for x in (queries, keys, values)])
    near_got = [swap(part, e) if e else part for e, part in zip(near_order, parts)]
    swapped = swap(parts[half], half)
    far_parts = call(
        functools.partial(forward, far_order),
        "forward",
        [shape(2, rows, width)] * (half - 1),
        [VMEM],
        [VMEM] * (half - 1),
        moved=2 * block_bytes,
    )(swapped)
    far_got = [swap(part, e) for e, part in zip(far_order, far_parts)] + [swapped]
    gates = near_got[:-1]
    *query_parts, table = call(
        functools.partial(join_queries, members, width, query_order, rows, docs, len(gates)),
        "join_queries",
        [shape(CORES, rows, width)] * half + [shape(members + 2, HEAD_DIM, dtype=jnp.int32)],
        [SMEM, VMEM, VMEM] + [ANY] * len(gates),
        [VMEM] * (half + 1),
        moved=2 * block_bytes,
    )(lengths, queries, swapped, *gates)
    query_got = [swap(part, e) if e else part for e, part in zip(query_order, query_parts)]

    own = call(
        functools.partial(inside, head_count, docs, rows),
        "inside",
        shape(rows, columns),
        [SMEM, VMEM, VMEM, VMEM],
        VMEM,
        flops=4 * rows * rows * columns,
        moved=3 * block_bytes,
    )(lengths, queries, keys, values)

    carry, total = call(
        functools.partial(gather_states, members, heads, rows, near_order + [e + half for e in far_order + [0]]),
        "gather_states",
        [shape(members, heads, HEAD_DIM, HEAD_DIM), shape(heads, HEAD_DIM, HEAD_DIM)],
        [VMEM] * (members + 1) + [ANY],
        [VMEM] * 2,
        [pltpu.VMEM((members, rows, width), bf16)] * 2,
        flops=2 * rows * HEAD_DIM * columns,
        moved=4 * block_bytes,
    )(table, *near_got, *far_got, own)
    up = [(g, g + members) for g in range(devices - members)]
    moving = lax.ppermute(total, everyone, up)
    earlier = moving
    if reach > 1:
        starts = BLOCK * (jnp.cumsum(lengths) - lengths)
        opens = jnp.max(jnp.where(starts <= base, starts, 0))
        for k in range(2, min(reach, planes - 1) + 1):
            moving = lax.ppermute(moving, everyone, up)
            earlier = earlier + jnp.where(opens < base - (k - 1) * members * rows, moving, 0.0)
    crossed_got = {}
    late = [e for e in (2, 0, 1,) if e < half]
    soon = [e for e in ranked(half, 3) if e not in late]
    gates = []
    for chosen in (soon, late):
        crossed = call(
            functools.partial(reach_back, members, heads, chosen, len(gates)),
            "reach_back",
            [shape(rows, width)] * (CORES * len(chosen)),
            [VMEM] * (len(chosen) + 3) + [ANY] * len(gates),
            [VMEM] * (CORES * len(chosen)),
            flops=2 * rows * HEAD_DIM * width * CORES * len(chosen),
            moved=2 * block_bytes,
        )(table, carry, earlier, *[query_got[query_order.index(e)] for e in chosen], *gates)
        for n, e in enumerate(chosen):
            for side in reversed(range(CORES)):
                d = e ^ (side * half)
                part = crossed[n * CORES + 1 - side]
                crossed_got[d] = swap(part, d) if d else part
        gates = crossed[:1]

    gain = norm_gain.reshape(1, columns)
    out = None
    listed = [[(0, 0), (3, 1), (3, 0)], [(0, 1), (1, 0), (2, 0), (1, 1), (2, 1)]]
    named = [pair for group in listed for pair in group]
    listed[0] += [(e, side) for e in soon for side in range(CORES) if (e, side) not in named]
    groups = [[e + side * half for e, side in group] for group in listed]
    for chosen in groups:
        more = [] if out is None else [out]
        out = call(
            functools.partial(finish, chosen, members, heads, rows),
            "finish",
            shape(rows, columns, dtype=bf16),
            [VMEM] * (3 + len(chosen)) + [ANY] * len(more),
            ANY,
            [pltpu.VMEM((len(chosen), rows, width), bf16), pltpu.SemaphoreType.DMA((len(chosen),))],
            moved=2 * block_bytes,
            aliases={3 + len(chosen): 0} if more else None,
        )(table, own, gain, *[crossed_got[d] for d in chosen], *more)
    return out


def solution(mesh):
    placed = (
        P(("outer", "inner"), None),
        P(("outer", "inner"), None),
        P(("outer", "inner"), None),
        P(),
        P(),
    )
    return jax.shard_map(
        body, mesh=mesh, in_specs=placed, out_specs=P(("outer", "inner"), None), check_vma=False
    )
```

```python
import functools

import jax
import jax.numpy as jnp
from jax import lax
from jax.experimental import pallas as pl
from jax.experimental.pallas import tpu as pltpu
from jax.sharding import PartitionSpec as P

HEAD_DIM = 128
BLOCK = 16
CORES = 2
SHARE = 4
EPSILON = 1e-05
SMEM = pl.BlockSpec(memory_space=pltpu.SMEM)
VMEM = pl.BlockSpec(memory_space=pltpu.VMEM)
ANY = pl.BlockSpec(memory_space=pl.ANY)
HBM = pl.BlockSpec(memory_space=pltpu.HBM)


def columns_of(member, width):
    return pl.ds(pl.multiple_of(member * width, width), width)


def position():
    inner_count = lax.axis_size("inner")
    index = lax.axis_index("outer") * inner_count + lax.axis_index("inner")
    return index, index % (CORES * inner_count)


def ranked(count, *first):
    first = [e for e in first if e < count]
    return [e for e in range(count) if e not in first and e > max(first)] + first


def heads_of(heads):
    return [slice(h * HEAD_DIM, (h + 1) * HEAD_DIM) for h in range(heads)]


def start_of(lengths, docs, token):
    begin = jnp.int32(0)
    found = jnp.int32(0)
    after = jnp.int32(jnp.iinfo(jnp.int32).max)
    for i in range(docs):
        found = jnp.where(begin <= token, begin, found)
        after = jnp.where(begin > token, jnp.minimum(begin, after), after)
        begin = begin + lengths[i] * BLOCK
    return found, after


def spread(members, width, near_order, queries, keys, values, *refs):
    half = members // CORES
    near, cross = refs[:half], refs[half]
    near_buffer, cross_buffer, sems = refs[half + 1 :]
    _, me = position()
    side = me // half
    near_copies = [
        pltpu.make_async_copy(source.at[:, columns_of(side, half * width)], near_buffer.at[i], sems.at[0, i])
        for i, source in enumerate((keys, values))
    ]
    cross_copies = [
        pltpu.make_async_copy(source.at[:, columns_of(1 - side, half * width)], cross_buffer.at[i], sems.at[1, i])
        for i, source in enumerate((keys, values, queries))
    ]
    for copy in near_copies + cross_copies:
        copy.start()
    for i, copy in enumerate(near_copies):
        copy.wait()
        for n, d in enumerate(near_order):
            near[n][i] = near_buffer[i, :, columns_of((me ^ d) % half, width)].astype(jnp.float32)
    for i, copy in enumerate(cross_copies):
        copy.wait()
        for e in range(half):
            cross[e, i] = cross_buffer[i, :, columns_of((me ^ e) % half, width)].astype(jnp.float32)


def forward(order, swapped, *outs):
    for n, e in enumerate(order):
        outs[n][...] = swapped[e, 0:2]


def join_queries(members, width, order, rows, docs, gates, lengths, queries, swapped, *refs):
    half = members // CORES
    outs, table = refs[gates:-1], refs[-1]
    index, me = position()
    for n, e in enumerate(order):
        outs[n][0] = queries[:, columns_of(me ^ e, width)].astype(jnp.float32)
        outs[n][1] = swapped[e, 2]
    base = (index - me) * rows
    for j in range(members + 1):
        found, _ = start_of(lengths, docs, base + j * rows)
        table[j : j + 1, :] = jnp.full((1, HEAD_DIM), found - base, jnp.int32)
    _, after = start_of(lengths, docs, index * rows)
    table[members + 1 : members + 2, :] = jnp.full((1, HEAD_DIM), after - index * rows, jnp.int32)


def gather_states(members, heads, rows, order, table, *refs):
    half = members // CORES
    parts = dict(zip(order, refs))
    carry_out, total_out, key_blocks, value_blocks = refs[members + 1 :]
    _, me = position()
    row = lax.broadcasted_iota(jnp.int32, (rows, HEAD_DIM), 0)
    for d in range(members):
        j = me ^ d
        kept = row >= table[pl.ds(j + 1, 1), :] - j * rows
        key, value = (parts[d][0, 0], parts[d][0, 1]) if d == half else (parts[d][0], parts[d][1])
        for span in heads_of(heads):
            key_blocks[j, :, span] = jnp.where(kept, key[:, span], 0.0).astype(jnp.bfloat16)
        value_blocks[j] = value.astype(jnp.bfloat16)
    state = [jnp.zeros((HEAD_DIM, HEAD_DIM), jnp.float32) for _ in range(heads)]
    for j in range(members):
        keep = jnp.where(table[j + 1 : j + 2, :] <= j * rows, 1.0, 0.0).astype(jnp.float32)
        for h, span in enumerate(heads_of(heads)):
            carry_out[j, h] = state[h]
            own = lax.dot_general(
                key_blocks[j, :, span],
                value_blocks[j, :, span],
                (((0,), (0,)), ((), ())),
                preferred_element_type=jnp.float32,
            )
            state[h] = keep * state[h] + own
    for h in range(heads):
        total_out[h] = state[h]


def inside(head_count, docs, rows, lengths, queries, keys, values, out):
    begin = position()[0] * rows
    row = lax.broadcasted_iota(jnp.int32, (rows, rows), 0)
    lane = lax.broadcasted_iota(jnp.int32, (rows, rows), 1)
    since = jnp.zeros((rows, rows), jnp.int32)
    start = -begin
    for i in range(docs):
        since = jnp.where(start <= row, start, since)
        start = start + lengths[i] * BLOCK
    allowed = (lane <= row) & (lane >= since)
    for span in heads_of(head_count):
        scores = lax.dot_general(
            queries[:, span], keys[:, span], (((1,), (1,)), ((), ())), preferred_element_type=jnp.float32
        )
        weights = jnp.where(allowed, scores, 0.0).astype(jnp.bfloat16)
        out[:, span] = jnp.dot(weights, values[:, span], preferred_element_type=jnp.float32)


def reach_back(members, heads, chosen, gates, table, carry, earlier, *refs):
    count = len(chosen)
    half = members // CORES
    query_parts, outs = refs[:count], refs[count + gates :]
    _, me = position()
    for n, e in enumerate(chosen):
        for side in range(CORES):
            j = me ^ e ^ (side * half)
            before = jnp.where(table[pl.ds(j, 1), :] < 0, 1.0, 0.0).astype(jnp.float32)
            for h, span in enumerate(heads_of(heads)):
                held = (carry[j, h] + before * earlier[h]).astype(jnp.bfloat16)
                query = query_parts[n][side, :, span].astype(jnp.bfloat16)
                outs[n * CORES + 1 - side][:, span] = jnp.dot(query, held, preferred_element_type=jnp.float32)


def finish(chosen, members, heads, rows, table, own, gain, *refs):
    count = len(chosen)
    parts, out = refs[:count], refs[-3]
    buffer, sems = refs[-2:]
    width = heads * HEAD_DIM
    _, me = position()
    continued = lax.broadcasted_iota(jnp.int32, (rows, HEAD_DIM), 0) < table[members + 1 : members + 2, :]
    copies = []
    for i, d in enumerate(chosen):
        columns = columns_of(me ^ d, width)
        inner = own[:, columns]
        scales = gain[:, columns]
        for span in heads_of(heads):
            mixed = inner[:, span] + jnp.where(continued, parts[i][:, span], 0.0)
            scale = lax.rsqrt(jnp.mean(mixed * mixed, axis=-1, keepdims=True) + EPSILON)
            buffer[i, :, span] = (mixed * scale * scales[:, span]).astype(jnp.bfloat16)
        copy = pltpu.make_async_copy(buffer.at[i], out.at[:, columns], sems.at[i])
        copy.start()
        copies.append(copy)
    for copy in copies:
        copy.wait()


def body(queries, keys, values, lengths, norm_gain):
    rows, columns = queries.shape
    head_count = columns // HEAD_DIM
    docs = lengths.shape[0]
    inner_count = lax.axis_size("inner")
    devices = lax.axis_size("outer") * inner_count
    members = CORES * inner_count
    half = inner_count
    planes = devices // members
    heads = head_count // members
    width = heads * HEAD_DIM
    reach = -(-(devices // SHARE) // members)
    everyone = ("outer", "inner")
    index = lax.axis_index("outer") * inner_count + lax.axis_index("inner")
    me = index % members
    base = (index - me) * rows
    f32, bf16 = jnp.float32, jnp.bfloat16

    def call(kernel, name, out_shape, in_specs, out_specs, scratch=(), flops=0, moved=0, aliases=None):
        return pl.pallas_call(
            kernel,
            out_shape=out_shape,
            in_specs=in_specs,
            out_specs=out_specs,
            scratch_shapes=scratch,
            compiler_params=pltpu.CompilerParams(vmem_limit_bytes=16 * 1024 * 1024),
            cost_estimate=pl.CostEstimate(flops=flops, bytes_accessed=moved, transcendentals=0),
            input_output_aliases=aliases or {},
            name=name,
        )

    def shape(*sizes, dtype=f32):
        return jax.ShapeDtypeStruct(sizes, dtype)

    def swap(part, d):
        pairs = [(g, g - g % members + (g % members ^ d)) for g in range(devices)]
        return lax.ppermute(part, everyone, pairs)

    near_order = ranked(half, 2, 1, 3, 0)
    far_order = ranked(half, 2, 3, 1, 0)[:-1]
    query_order = ranked(half, 3, 2, 1, 0)
    block_bytes = rows * columns * 4
    parts = call(
        functools.partial(spread, members, width, near_order),
        "spread",
        [shape(2, rows, width)] * half + [shape(half, 3, rows, width)],
        [HBM, HBM, HBM],
        [VMEM] * (half + 1),
        [
            pltpu.VMEM((2, rows, half * width), bf16),
            pltpu.VMEM((3, rows, half * width), bf16),
            pltpu.SemaphoreType.DMA((CORES, 3)),
        ],
    )(*[pltpu.with_memory_space_constraint(x, pltpu.HBM) for x in (queries, keys, values)])
    near_got = [swap(part, e) if e else part for e, part in zip(near_order, parts)]
    swapped = swap(parts[half], half)
    far_parts = call(
        functools.partial(forward, far_order),
        "forward",
        [shape(2, rows, width)] * (half - 1),
        [VMEM],
        [VMEM] * (half - 1),
        moved=2 * block_bytes,
    )(swapped)
    far_got = [swap(part, e) for e, part in zip(far_order, far_parts)] + [swapped]
    gates = near_got[:1]
    *query_parts, table = call(
        functools.partial(join_queries, members, width, query_order, rows, docs, len(gates)),
        "join_queries",
        [shape(CORES, rows, width)] * half + [shape(members + 2, HEAD_DIM, dtype=jnp.int32)],
        [SMEM, VMEM, VMEM] + [ANY] * len(gates),
        [VMEM] * (half + 1),
        moved=2 * block_bytes,
    )(lengths, queries, swapped, *gates)
    query_got = [swap(part, e) if e else part for e, part in zip(query_order, query_parts)]

    own = call(
        functools.partial(inside, head_count, docs, rows),
        "inside",
        shape(rows, columns),
        [SMEM, VMEM, VMEM, VMEM],
        VMEM,
        flops=4 * rows * rows * columns,
        moved=3 * block_bytes,
    )(lengths, queries, keys, values)

    carry, total = call(
        functools.partial(gather_states, members, heads, rows, near_order + [e + half for e in far_order + [0]]),
        "gather_states",
        [shape(members, heads, HEAD_DIM, HEAD_DIM), shape(heads, HEAD_DIM, HEAD_DIM)],
        [VMEM] * (members + 1) + [ANY],
        [VMEM] * 2,
        [pltpu.VMEM((members, rows, width), bf16)] * 2,
        flops=2 * rows * HEAD_DIM * columns,
        moved=4 * block_bytes,
    )(table, *near_got, *far_got, own)
    up = [(g, g + members) for g in range(devices - members)]
    moving = lax.ppermute(total, everyone, up)
    earlier = moving
    if reach > 1:
        starts = BLOCK * (jnp.cumsum(lengths) - lengths)
        opens = jnp.max(jnp.where(starts <= base, starts, 0))
        for k in range(2, min(reach, planes - 1) + 1):
            moving = lax.ppermute(moving, everyone, up)
            earlier = earlier + jnp.where(opens < base - (k - 1) * members * rows, moving, 0.0)
    crossed_got = {}
    late = [e for e in (2, 0, 1,) if e < half]
    soon = [e for e in ranked(half, 3) if e not in late]
    gates = []
    for chosen in (soon, late):
        crossed = call(
            functools.partial(reach_back, members, heads, chosen, len(gates)),
            "reach_back",
            [shape(rows, width)] * (CORES * len(chosen)),
            [VMEM] * (len(chosen) + 3) + [ANY] * len(gates),
            [VMEM] * (CORES * len(chosen)),
            flops=2 * rows * HEAD_DIM * width * CORES * len(chosen),
            moved=2 * block_bytes,
        )(table, carry, earlier, *[query_got[query_order.index(e)] for e in chosen], *gates)
        for n, e in enumerate(chosen):
            for side in reversed(range(CORES)):
                d = e ^ (side * half)
                part = crossed[n * CORES + 1 - side]
                crossed_got[d] = swap(part, d) if d else part
        gates = crossed[:1]

    gain = norm_gain.reshape(1, columns)
    out = None
    listed = [[(0, 0), (3, 1), (3, 0)], [(0, 1), (1, 0), (2, 0), (1, 1), (2, 1)]]
    named = [pair for group in listed for pair in group]
    listed[0] += [(e, side) for e in soon for side in range(CORES) if (e, side) not in named]
    groups = [[e + side * half for e, side in group] for group in listed]
    for chosen in groups:
        more = [] if out is None else [out]
        out = call(
            functools.partial(finish, chosen, members, heads, rows),
            "finish",
            shape(rows, columns, dtype=bf16),
            [VMEM] * (3 + len(chosen)) + [ANY] * len(more),
            ANY,
            [pltpu.VMEM((len(chosen), rows, width), bf16), pltpu.SemaphoreType.DMA((len(chosen),))],
            moved=2 * block_bytes,
            aliases={3 + len(chosen): 0} if more else None,
        )(table, own, gain, *[crossed_got[d] for d in chosen], *more)
    return out


def solution(mesh):
    placed = (
        P(("outer", "inner"), None),
        P(("outer", "inner"), None),
        P(("outer", "inner"), None),
        P(),
        P(),
    )
    return jax.shard_map(
        body, mesh=mesh, in_specs=placed, out_specs=P(("outer", "inner"), None), check_vma=False
    )
```
